512 devices in a mesh: wide: 64 (over y, x, z_hi), narrow: 8 (over z_lo, core).
Axes of the slice: x: 4, y: 8, z: 8 (z_hi: 2, z_lo: 4; z = z_hi * 4 + z_lo), core: 2. Of those that a mesh axis runs over, the one named last changes fastest.
Arguments:
- front: float32 [32768, 4096], P('wide', 'narrow'), as said below
- child_update: float32 [65536, 4096], P('wide', 'narrow'), may hold values from -0.8 to 0.8
- child_map: int32 [512], replicated, may hold values from -1 to 255, as said below
Outputs:
- factor: float32 [32768, 4096], P('wide', 'narrow')
The draws below stay inside these ranges and needn't reach their ends.
Inputs may be any that keep to these rules, and one draw needn't show every extreme that they name: `child_map`: entry m names the global row block of the front into which child block m is added, or -1 for an empty block. With F = 4, blocks m from p * 2F to p * 2F + 2F - 1 lie on wide index p; those with p < 32 belong to the first child, the others to the second. The first F of them name blocks whose index mod 64 is p mod (32), the last F blocks whose index mod 64 is p mod (32) + 32; within each group of F the named blocks increase and the empty entries come last. Each child names 192 distinct blocks, and one front owner receives a full group from each child. `front`: entries lie within -0.8 and 0.8, except on the global diagonal of the first 512 global columns, where a value between 5 and 40 times the square root of 512 is added.
All inputs are finite; a program needn't handle non-finite values.
Results may differ from the reference program's by a relative error of at most 0.0001.
Values sent between devices are 32-bit elements; how exact they have to be, the bound alone decides.
A program may use at most 64 MiB of HBM per device.

```python
import math
import jax
import jax.numpy as jnp
from jax import lax

BS = 128
PW = 512
FRONT = 32768
WIN = 4096
CHILD = 24576
PANELS = 1
N_WIDE = 64
N_NARROW = 8


def draw_front(key, part):
    rows = jnp.arange(FRONT, dtype=jnp.int32)
    cols = jnp.arange(WIN, dtype=jnp.int32)
    per_owner = FRONT // BS // N_WIDE
    col_slots = WIN // PW // N_NARROW
    wide_of = rows // (per_owner * BS)
    global_row = (rows // BS % per_owner * N_WIDE + wide_of) * BS + rows % BS
    narrow_of = cols // (col_slots * PW)
    global_col = (cols // PW % col_slots * N_NARROW + narrow_of) * PW + cols % PW
    base = jax.random.uniform(jax.random.fold_in(key, 3), (FRONT, WIN), jnp.float32, -0.8, 0.8)
    leading = PANELS * PW
    widths = math.sqrt(leading)
    shifts = jnp.exp(jax.random.uniform(jax.random.fold_in(key, 5), (WIN,), jnp.float32, math.log(5.0), math.log(40.0))) * widths
    on_diagonal = (global_row[:, None] == global_col[None, :]) & (global_col[None, :] < leading)
    return base + jnp.where(on_diagonal, shifts[global_col][None, :], 0.0)


def draw_child_map(key, part):
    blocks = FRONT // BS
    per_owner = blocks // N_WIDE
    half_count = N_WIDE // 2
    slots_device = 2 * per_owner
    used = CHILD // BS
    ids = jnp.arange(blocks, dtype=jnp.int32)
    owners = ids % N_WIDE
    full_owner = jax.random.randint(jax.random.fold_in(key, 2), (), 0, N_WIDE)
    result = jnp.full((2 * blocks,), -1, jnp.int32)
    for child_index in range(2):
        subkey = jax.random.fold_in(key, 17 + child_index)
        shuffled = jax.random.permutation(jax.random.fold_in(subkey, 1), blocks).astype(jnp.int32)
        ranking = jnp.zeros((blocks,), jnp.int32).at[shuffled].set(ids)
        priority = jnp.where(owners == full_owner, ranking - blocks, ranking)
        picked_order = jnp.argsort(priority, stable=True)
        chosen = jnp.zeros((blocks,), jnp.int32).at[picked_order[:used]].set(1)
        grid = chosen.reshape(per_owner, N_WIDE)
        position = (jnp.cumsum(grid, axis=0) - grid).reshape(blocks)
        device = child_index * half_count + owners % half_count
        groups = owners // half_count
        destination = device * slots_device + groups * per_owner + position
        destination = jnp.where(chosen == 1, destination, 2 * blocks)
        result = result.at[destination].set(ids, mode='drop')
    return result


def shard_levels(own_key, shape, split, smallest, top_value):
    def one(dim, shards_of):
        heights = jax.random.uniform(jax.random.fold_in(jax.random.fold_in(own_key, 6), dim), (shards_of,), jnp.float32, smallest / len(split), top_value / len(split))
        return jnp.repeat(jnp.exp(heights), shape[dim] // shards_of).reshape((-1,) + (1,) * (len(shape) - dim - 1))

    gain = one(*split[0])
    for cut in split[1:]:
        gain = gain * one(*cut)
    return gain


def setup_inputs(seed: int = 0) -> dict:
    key_list = jax.random.split(jax.random.key(seed), 4)
    front = draw_front(jax.random.fold_in(key_list[3], 71), 0)
    child_update = jnp.clip(jax.random.uniform(key_list[1], (2 * FRONT, WIN), jnp.float32, -0.8, 0.8) * shard_levels(key_list[1], (2 * FRONT, WIN), ((0, 64), (1, 8)), -0.4, 0.0), -0.8, 0.8)
    child_map = draw_child_map(jax.random.fold_in(key_list[3], 71), 0)
    return {"front": front, "child_update": child_update, "child_map": child_map}


def global_order(stored):
    row_slots = FRONT // BS // N_WIDE
    col_slots = WIN // PW // N_NARROW
    shaped = stored.reshape(N_WIDE, row_slots, BS, N_NARROW, col_slots, PW)
    return shaped.transpose(1, 0, 2, 4, 3, 5).reshape(FRONT, WIN)

def stored_order(matrix):
    row_slots = FRONT // BS // N_WIDE
    col_slots = WIN // PW // N_NARROW
    shaped = matrix.reshape(row_slots, N_WIDE, BS, col_slots, N_NARROW, PW)
    return shaped.transpose(1, 0, 2, 4, 3, 5).reshape(FRONT, WIN)

def reference(front, child_update, child_map):
    block_count = FRONT // BS
    col_slots = WIN // PW // N_NARROW
    matrix = global_order(front)
    children = child_update.reshape(2 * block_count, BS, N_NARROW, col_slots, PW)
    children = children.transpose(0, 1, 3, 2, 4).reshape(2 * block_count, BS, WIN)
    col_blocks = jnp.arange(WIN // BS, dtype=jnp.int32)
    masks = []
    for child_index in range(2):
        names = child_map[child_index * block_count:(child_index + 1) * block_count]
        named = jnp.any(names[:, None] == col_blocks[None, :], axis=0)
        masks.append(jnp.repeat(named, BS))
    column_mask = jnp.stack(masks, 0)
    children = children.reshape(2, block_count, BS, WIN)
    children = jnp.where(column_mask[:, None, None, :], children, jnp.zeros_like(children))
    children = children.reshape(2 * block_count, BS, WIN)
    targets = jnp.where(child_map < 0, block_count, child_map).astype(jnp.int32)
    matrix = matrix.reshape(block_count, BS, WIN).at[targets].add(children, mode='drop').reshape(FRONT, WIN)
    for panel_index in range(PANELS):
        first_col = panel_index * PW
        next_col = first_col + PW
        diag_block = matrix[first_col:next_col, first_col:next_col]
        symmetric = jnp.tril(diag_block) + jnp.tril(diag_block, -1).T
        factor_diag = jnp.tril(jnp.linalg.cholesky(symmetric))
        below = lax.linalg.triangular_solve(factor_diag, matrix[next_col:, first_col:next_col], left_side=False, lower=True, transpose_a=True)
        panel = jnp.concatenate([jnp.zeros((first_col, PW), jnp.float32), factor_diag, below], 0)
        matrix = matrix.at[:, first_col:next_col].set(panel)
        update = jnp.dot(panel[next_col:].astype(jnp.float32), panel[next_col:WIN].T.astype(jnp.float32), precision=lax.Precision.HIGHEST, preferred_element_type=jnp.float32)
        matrix = matrix.at[next_col:, next_col:].add(-update)
    on_or_below = jnp.arange(FRONT)[:, None] >= jnp.arange(WIN)[None, :]
    matrix = jnp.where(on_or_below, matrix, jnp.zeros_like(matrix))
    return stored_order(matrix)
```

```python
import functools

import jax
import jax.numpy as jnp
from jax import lax
from jax.experimental import pallas as pl
from jax.experimental.pallas import tpu as pltpu
from jax.sharding import Mesh
from jax.sharding import PartitionSpec as P

BS = 128
PW = 512
WIDE = ("wide_0", "wide_1", "wide_2")
AXES = ("wide_0", "wide_1", "wide_2", "narrow")
MESH_ID = pl.DeviceIdType.MESH

HIGHEST_PRECISION = lax.Precision.HIGHEST


def from_partner(value, axis, distance):
    return lax.ppermute(value, axis, [(i, i ^ 1 << distance) for i in range(lax.axis_size(axis))])


def positions():
    return tuple(lax.axis_index(a) for a in AXES)


NARROW_CHUNKS = 4


def narrow_bcast_kernel(src_ref, out_ref, send_sem, recv_sem):
    y, x, h, q = positions()
    n = lax.axis_size("narrow")
    rows = out_ref.shape[0] // NARROW_CHUNKS
    even = q % 2 == 0
    has_parent = q > 0
    parent = jnp.where(even, q - 2, q - 1)
    kids = [(even, q + 1), (jnp.logical_and(even, q + 2 < n), q + 2)]

    barrier = pltpu.get_barrier_semaphore()

    @pl.when(has_parent)
    def _():
        pl.semaphore_signal(barrier, 1, device_id=(y, x, h, parent), device_id_type=MESH_ID)

    for cond, kid in kids:
        @pl.when(cond)
        def _():
            pl.semaphore_signal(barrier, 1, device_id=(y, x, h, kid), device_id_type=MESH_ID)

    peers = has_parent.astype(jnp.int32)
    for cond, kid in kids:
        peers = peers + cond.astype(jnp.int32)
    pl.semaphore_wait(barrier, peers)

    @pl.when(q == 0)
    def _():
        out_ref[...] = src_ref[...]

    def copy(src, c, k, kid):
        part = pl.ds(c * rows, rows)
        return pltpu.make_async_remote_copy(
            src_ref=src.at[part],
            dst_ref=out_ref.at[part],
            send_sem=send_sem.at[c, k],
            recv_sem=recv_sem.at[c],
            device_id=(y, x, h, kid),
            device_id_type=MESH_ID,
        )

    for c in range(NARROW_CHUNKS):
        @pl.when(has_parent)
        def _():
            copy(out_ref, c, 0, q).wait_recv()

        for k, (cond, kid) in enumerate(kids):
            @pl.when(jnp.logical_and(cond, q == 0))
            def _():
                copy(src_ref, c, k, kid).start()

            @pl.when(jnp.logical_and(cond, q != 0))
            def _():
                copy(out_ref, c, k, kid).start()

    for c in range(NARROW_CHUNKS):
        for k, (cond, kid) in enumerate(kids):
            @pl.when(cond)
            def _():
                copy(out_ref, c, k, kid).wait_send()


def narrow_bcast(panel):
    return pl.pallas_call(
        narrow_bcast_kernel,
        out_shape=jax.ShapeDtypeStruct(panel.shape, panel.dtype),
        in_specs=[pl.BlockSpec(memory_space=pltpu.VMEM)],
        out_specs=pl.BlockSpec(memory_space=pltpu.VMEM),
        scratch_shapes=[
            pltpu.SemaphoreType.DMA((NARROW_CHUNKS, 2)),
            pltpu.SemaphoreType.DMA((NARROW_CHUNKS,)),
        ],
        compiler_params=pltpu.CompilerParams(collective_id=0, has_side_effects=True),
    )(panel)


WIDE_CHUNKS = 4
N_BLOCKS = 8
N_SLOTS = 6


def wide_tree(y, x, h, root, ny, nx):
    y0 = root // (2 * nx)
    x0 = (root // 2) % nx
    h0 = root % 2
    dy = (y - y0 + ny) % ny
    dx = (x - x0 + nx) % nx
    dh = (h - h0 + 2) % 2
    half = ny // 2
    at_y0 = dy == 0
    at_x0 = jnp.logical_and(at_y0, dx == 0)
    is_root = jnp.logical_and(at_x0, dh == 0)
    up = jnp.logical_and(dy >= 1, dy <= half)
    py = jnp.where(up, (y + ny - 1) % ny, (y + 1) % ny)
    px = jnp.where(dx == 2, (x + nx - 1) % nx, x0)
    parent_y = jnp.where(at_y0, y, py)
    parent_x = jnp.where(jnp.logical_and(at_y0, dx != 0), px, x)
    parent_h = jnp.where(at_x0, h0, h)
    parent = (parent_y, parent_x, parent_h)
    kids = [
        (is_root, (y, x, 1 - h)),
        (at_x0, (y, (x + 1) % nx, h)),
        (at_x0, (y, (x + nx - 1) % nx, h)),
        (jnp.logical_and(at_y0, dx == 1), (y, (x + 1) % nx, h)),
        (dy < half, ((y + 1) % ny, x, h)),
        (jnp.logical_or(at_y0, dy > half + 1), ((y + ny - 1) % ny, x, h)),
    ]
    return is_root, parent, kids


def wide_bcast_kernel(src_ref, out_ref, send_sem, recv_sem):
    y, x, h, q = positions()
    ny = lax.axis_size("wide_0")
    nx = lax.axis_size("wide_1")
    rows = src_ref.shape[0] // WIDE_CHUNKS
    me = (y * nx + x) * 2 + h
    trees = []
    for j in range(N_BLOCKS):
        if j < N_BLOCKS // 2:
            root = j
            active = q >= 0
        else:
            root = 4 * q + (j - N_BLOCKS // 2)
            active = q > 0
        is_root, parent, kids = wide_tree(y, x, h, root, ny, nx)
        trees.append((active, is_root, parent, kids))

    barrier = pltpu.get_barrier_semaphore()
    for active, is_root, parent, kids in trees:
        @pl.when(jnp.logical_and(active, jnp.logical_not(is_root)))
        def _():
            pl.semaphore_signal(barrier, 1, device_id=(*parent, q), device_id_type=MESH_ID)

        for cond, kid in kids:
            @pl.when(jnp.logical_and(active, cond))
            def _():
                pl.semaphore_signal(barrier, 1, device_id=(*kid, q), device_id_type=MESH_ID)

    peers = jnp.int32(0)
    for active, is_root, parent, kids in trees:
        peers = peers + jnp.logical_and(active, jnp.logical_not(is_root)).astype(jnp.int32)
        for cond, kid in kids:
            peers = peers + jnp.logical_and(active, cond).astype(jnp.int32)
    pl.semaphore_wait(barrier, peers)

    for j, (active, is_root, parent, kids) in enumerate(trees):
        @pl.when(jnp.logical_and(active, is_root))
        def _():
            out_ref[j] = src_ref[...]

    def copy(src, j, c, k, kid):
        part = pl.ds(c * rows, rows)
        return pltpu.make_async_remote_copy(
            src_ref=src.at[part],
            dst_ref=out_ref.at[j, part],
            send_sem=send_sem.at[j, c, k],
            recv_sem=recv_sem.at[j, c],
            device_id=(*kid, q),
            device_id_type=MESH_ID,
        )

    for c in range(WIDE_CHUNKS):
        for j, (active, is_root, parent, kids) in enumerate(trees):
            @pl.when(jnp.logical_and(active, jnp.logical_not(is_root)))
            def _():
                copy(out_ref.at[j], j, c, 0, (y, x, h)).wait_recv()

            for k, (cond, kid) in enumerate(kids):
                go = jnp.logical_and(active, cond)

                @pl.when(jnp.logical_and(go, is_root))
                def _():
                    copy(src_ref, j, c, k, kid).start()

                @pl.when(jnp.logical_and(go, jnp.logical_not(is_root)))
                def _():
                    copy(out_ref.at[j], j, c, k, kid).start()

    for c in range(WIDE_CHUNKS):
        for j, (active, is_root, parent, kids) in enumerate(trees):
            for k, (cond, kid) in enumerate(kids):
                @pl.when(jnp.logical_and(active, cond))
                def _():
                    copy(out_ref.at[j], j, c, k, kid).wait_send()


def wide_bcast(block):
    return pl.pallas_call(
        wide_bcast_kernel,
        out_shape=jax.ShapeDtypeStruct((N_BLOCKS, *block.shape), block.dtype),
        in_specs=[pl.BlockSpec(memory_space=pltpu.VMEM)],
        out_specs=pl.BlockSpec(memory_space=pltpu.VMEM),
        scratch_shapes=[
            pltpu.SemaphoreType.DMA((N_BLOCKS, WIDE_CHUNKS, N_SLOTS)),
            pltpu.SemaphoreType.DMA((N_BLOCKS, WIDE_CHUNKS)),
        ],
        compiler_params=pltpu.CompilerParams(collective_id=1, has_side_effects=True),
    )(block)


def mm_t(a, b):
    return lax.dot_general(
        a, b, (((1,), (1,)), ((), ())),
        precision=HIGHEST_PRECISION, preferred_element_type=jnp.float32,
    )


def shards(front, child_update, child_map):
    wide_count = lax.axis_size(WIDE)
    narrow_count = lax.axis_size("narrow")
    wide_index = lax.axis_index(WIDE)
    narrow_index = lax.axis_index("narrow")
    half_count = wide_count // 2
    local_rows, local_cols = front.shape
    front_slots = local_rows // BS
    block_total = front_slots * wide_count
    child_side = wide_index // half_count
    row_local = jnp.arange(local_rows, dtype=jnp.int32)
    global_row = (row_local // BS * wide_count + wide_index) * BS + row_local % BS
    col_local = jnp.arange(local_cols, dtype=jnp.int32)
    global_col = (col_local // PW * narrow_count + narrow_index) * PW + col_local % PW
    child_names = lax.dynamic_slice_in_dim(child_map, child_side * block_total, block_total)
    named_cols = jnp.any(child_names[:, None] == (global_col // BS)[None, :], axis=0)
    groups = child_update.reshape(2, front_slots, BS, local_cols)
    groups = jnp.where(named_cols[None, None, None, :], groups, jnp.zeros_like(groups))
    kept_rows = lax.dynamic_index_in_dim(groups, child_side, 0, keepdims=False)
    leaving = lax.dynamic_index_in_dim(groups, 1 - child_side, 0, keepdims=False)
    arrived = from_partner(leaving, WIDE, half_count.bit_length() - 1)
    partner = (wide_index + half_count) % wide_count
    own_map = lax.dynamic_slice_in_dim(
        child_map, (wide_index * 2 + child_side) * front_slots, front_slots
    )
    got_map = lax.dynamic_slice_in_dim(
        child_map, (partner * 2 + child_side) * front_slots, front_slots
    )
    target = wide_index + wide_count * jnp.arange(front_slots, dtype=jnp.int32)
    own_select = (own_map[None, :] == target[:, None]).astype(jnp.float32)
    got_select = (got_map[None, :] == target[:, None]).astype(jnp.float32)
    own_part = jnp.dot(
        own_select,
        kept_rows.reshape(front_slots, BS * local_cols),
        precision=HIGHEST_PRECISION,
        preferred_element_type=jnp.float32,
    )
    got_part = jnp.dot(
        got_select,
        arrived.reshape(front_slots, BS * local_cols),
        precision=HIGHEST_PRECISION,
        preferred_element_type=jnp.float32,
    )
    matrix = front + (own_part + got_part).reshape(local_rows, local_cols)

    panel = narrow_bcast(matrix)
    blocks = wide_bcast(panel[:BS])
    diag_block = blocks[: N_BLOCKS // 2].reshape(PW, PW)
    col_rows = blocks[N_BLOCKS // 2 :].reshape(PW, PW)

    symmetric = jnp.tril(diag_block) + jnp.tril(diag_block, -1).T
    factor_diag = jnp.tril(jnp.linalg.cholesky(symmetric))
    inverse = lax.linalg.triangular_solve(
        factor_diag, jnp.eye(PW, dtype=jnp.float32), left_side=True, lower=True
    )
    own_factor = mm_t(panel, inverse)
    diag_rows = lax.dynamic_slice_in_dim(factor_diag, jnp.minimum(wide_index, 3) * BS, BS)
    top = jnp.where(wide_index * BS < PW, diag_rows, own_factor[:BS])
    own_factor = jnp.concatenate([top, own_factor[BS:]], 0)
    col_factor = mm_t(col_rows, inverse)
    update = mm_t(own_factor, col_factor)
    renewed = jnp.where(narrow_index == 0, own_factor, matrix - update)
    on_or_below = global_row[:, None] >= global_col[None, :]
    return jnp.where(on_or_below, renewed, jnp.zeros_like(renewed))


def solution(mesh):
    torus = Mesh(
        mesh.devices.reshape(8, 4, 2, mesh.shape["narrow"]),
        AXES,
    )
    placed = (P(WIDE, "narrow"), P(WIDE, "narrow"), P())
    return jax.shard_map(
        shards, mesh=torus, in_specs=placed, out_specs=P(WIDE, "narrow"), check_vma=False
    )
```

```python
import functools

import jax
import jax.numpy as jnp
from jax import lax
from jax.experimental import pallas as pl
from jax.experimental.pallas import tpu as pltpu
from jax.sharding import Mesh
from jax.sharding import PartitionSpec as P

BS = 128
PW = 512
WIDE = ("wide_0", "wide_1", "wide_2")
AXES = ("wide_0", "wide_1", "wide_2", "narrow")
MESH_ID = pl.DeviceIdType.MESH

HIGHEST_PRECISION = lax.Precision.HIGHEST


def from_partner(value, axis, distance):
    return lax.ppermute(value, axis, [(i, i ^ 1 << distance) for i in range(lax.axis_size(axis))])


def positions():
    return tuple(lax.axis_index(a) for a in AXES)


NARROW_CHUNKS = 4


def narrow_bcast_kernel(src_ref, out_ref, send_sem, recv_sem):
    y, x, h, q = positions()
    n = lax.axis_size("narrow")
    rows = out_ref.shape[0] // NARROW_CHUNKS
    even = q % 2 == 0
    has_parent = q > 0
    parent = jnp.where(even, q - 2, q - 1)
    kids = [(even, q + 1), (jnp.logical_and(even, q + 2 < n), q + 2)]

    barrier = pltpu.get_barrier_semaphore()

    @pl.when(has_parent)
    def _():
        pl.semaphore_signal(barrier, 1, device_id=(y, x, h, parent), device_id_type=MESH_ID)

    for cond, kid in kids:
        @pl.when(cond)
        def _():
            pl.semaphore_signal(barrier, 1, device_id=(y, x, h, kid), device_id_type=MESH_ID)

    peers = has_parent.astype(jnp.int32)
    for cond, kid in kids:
        peers = peers + cond.astype(jnp.int32)
    pl.semaphore_wait(barrier, peers)

    @pl.when(q == 0)
    def _():
        out_ref[...] = src_ref[...]

    def copy(src, c, k, kid):
        part = pl.ds(c * rows, rows)
        return pltpu.make_async_remote_copy(
            src_ref=src.at[part],
            dst_ref=out_ref.at[part],
            send_sem=send_sem.at[c, k],
            recv_sem=recv_sem.at[c],
            device_id=(y, x, h, kid),
            device_id_type=MESH_ID,
        )

    for c in range(NARROW_CHUNKS):
        @pl.when(has_parent)
        def _():
            copy(out_ref, c, 0, q).wait_recv()

        for k, (cond, kid) in enumerate(kids):
            @pl.when(jnp.logical_and(cond, q == 0))
            def _():
                copy(src_ref, c, k, kid).start()

            @pl.when(jnp.logical_and(cond, q != 0))
            def _():
                copy(out_ref, c, k, kid).start()

    for c in range(NARROW_CHUNKS):
        for k, (cond, kid) in enumerate(kids):
            @pl.when(cond)
            def _():
                copy(out_ref, c, k, kid).wait_send()


def narrow_bcast(panel):
    return pl.pallas_call(
        narrow_bcast_kernel,
        out_shape=jax.ShapeDtypeStruct(panel.shape, panel.dtype),
        in_specs=[pl.BlockSpec(memory_space=pltpu.VMEM)],
        out_specs=pl.BlockSpec(memory_space=pltpu.VMEM),
        scratch_shapes=[
            pltpu.SemaphoreType.DMA((NARROW_CHUNKS, 2)),
            pltpu.SemaphoreType.DMA((NARROW_CHUNKS,)),
        ],
        compiler_params=pltpu.CompilerParams(collective_id=0, has_side_effects=True),
    )(panel)


N_BLOCKS = 8
N_SLOTS = 6
MAX_DEPTH = 8


def wide_tree(y, x, h, root, ny, nx):
    y0 = root // (2 * nx)
    x0 = (root // 2) % nx
    h0 = root % 2
    dy = (y - y0 + ny) % ny
    dx = (x - x0 + nx) % nx
    dh = (h - h0 + 2) % 2
    half = ny // 2
    at_y0 = dy == 0
    at_x0 = jnp.logical_and(at_y0, dx == 0)
    is_root = jnp.logical_and(at_x0, dh == 0)
    up = jnp.logical_and(dy >= 1, dy <= half)
    py = jnp.where(up, (y + ny - 1) % ny, (y + 1) % ny)
    px = jnp.where(dx == 2, (x + nx - 1) % nx, x0)
    parent_y = jnp.where(at_y0, y, py)
    parent_x = jnp.where(jnp.logical_and(at_y0, dx != 0), px, x)
    parent_h = jnp.where(at_x0, h0, h)
    parent = (parent_y, parent_x, parent_h)
    kids = [
        (is_root, (y, x, 1 - h)),
        (at_x0, (y, (x + 1) % nx, h)),
        (at_x0, (y, (x + nx - 1) % nx, h)),
        (jnp.logical_and(at_y0, dx == 1), (y, (x + 1) % nx, h)),
        (dy < half, ((y + 1) % ny, x, h)),
        (jnp.logical_or(at_y0, dy > half + 1), ((y + ny - 1) % ny, x, h)),
    ]
    x_depth = jnp.where(dx == 0, 0, jnp.where(dx == 2, 2, 1))
    y_depth = jnp.where(dy <= half, dy, ny - dy)
    depth = dh + x_depth + y_depth
    return is_root, parent, kids, depth


def wide_bcast_kernel(src_ref, out_ref, send_sem, recv_sem):
    y, x, h, q = positions()
    ny = lax.axis_size("wide_0")
    nx = lax.axis_size("wide_1")
    trees = []
    for j in range(N_BLOCKS):
        if j < N_BLOCKS // 2:
            root = j
            active = q >= 0
        else:
            root = 4 * q + (j - N_BLOCKS // 2)
            active = q > 0
        is_root, parent, kids, depth = wide_tree(y, x, h, root, ny, nx)
        trees.append((active, is_root, parent, kids, depth))

    barrier = pltpu.get_barrier_semaphore()
    for active, is_root, parent, kids, depth in trees:
        @pl.when(jnp.logical_and(active, jnp.logical_not(is_root)))
        def _():
            pl.semaphore_signal(barrier, 1, device_id=(*parent, q), device_id_type=MESH_ID)

        for cond, kid in kids:
            @pl.when(jnp.logical_and(active, cond))
            def _():
                pl.semaphore_signal(barrier, 1, device_id=(*kid, q), device_id_type=MESH_ID)

    peers = jnp.int32(0)
    for active, is_root, parent, kids, depth in trees:
        peers = peers + jnp.logical_and(active, jnp.logical_not(is_root)).astype(jnp.int32)
        for cond, kid in kids:
            peers = peers + jnp.logical_and(active, cond).astype(jnp.int32)
    pl.semaphore_wait(barrier, peers)

    def copy(src, j, k, kid):
        return pltpu.make_async_remote_copy(
            src_ref=src,
            dst_ref=out_ref.at[j],
            send_sem=send_sem.at[j, k],
            recv_sem=recv_sem.at[j],
            device_id=(*kid, q),
            device_id_type=MESH_ID,
        )

    for j, (active, is_root, parent, kids, depth) in enumerate(trees):
        root_here = jnp.logical_and(active, is_root)

        for k, (cond, kid) in enumerate(kids):
            @pl.when(jnp.logical_and(root_here, cond))
            def _():
                copy(src_ref, j, k, kid).start()

        @pl.when(root_here)
        def _():
            out_ref[j] = src_ref[...]

    for level in range(1, MAX_DEPTH):
        for j, (active, is_root, parent, kids, depth) in enumerate(trees):
            here = jnp.logical_and(active, depth == level)

            @pl.when(here)
            def _():
                copy(out_ref.at[j], j, 0, (y, x, h)).wait_recv()

            for k, (cond, kid) in enumerate(kids):
                @pl.when(jnp.logical_and(here, cond))
                def _():
                    copy(out_ref.at[j], j, k, kid).start()

    for j, (active, is_root, parent, kids, depth) in enumerate(trees):
        for k, (cond, kid) in enumerate(kids):
            @pl.when(jnp.logical_and(active, cond))
            def _():
                copy(out_ref.at[j], j, k, kid).wait_send()


def wide_bcast(block):
    return pl.pallas_call(
        wide_bcast_kernel,
        out_shape=jax.ShapeDtypeStruct((N_BLOCKS, *block.shape), block.dtype),
        in_specs=[pl.BlockSpec(memory_space=pltpu.VMEM)],
        out_specs=pl.BlockSpec(memory_space=pltpu.VMEM),
        scratch_shapes=[
            pltpu.SemaphoreType.DMA((N_BLOCKS, N_SLOTS)),
            pltpu.SemaphoreType.DMA((N_BLOCKS,)),
        ],
        compiler_params=pltpu.CompilerParams(collective_id=1, has_side_effects=True),
    )(block)


def mm_t(a, b):
    return lax.dot_general(
        a, b, (((1,), (1,)), ((), ())),
        precision=HIGHEST_PRECISION, preferred_element_type=jnp.float32,
    )


def mm(a, b):
    return jnp.dot(a, b, precision=HIGHEST_PRECISION, preferred_element_type=jnp.float32)


def triangular_inverse(lower):
    n = lower.shape[0]
    eye = jnp.eye(n, dtype=lower.dtype)
    inverse = eye / jnp.diagonal(lower)[:, None]
    for _ in range(max(1, (n - 1).bit_length())):
        inverse = 2 * inverse - mm(inverse, mm(lower, inverse))
    return inverse


def shards(front, child_update, child_map):
    wide_count = lax.axis_size(WIDE)
    narrow_count = lax.axis_size("narrow")
    wide_index = lax.axis_index(WIDE)
    narrow_index = lax.axis_index("narrow")
    half_count = wide_count // 2
    local_rows, local_cols = front.shape
    front_slots = local_rows // BS
    block_total = front_slots * wide_count
    child_side = wide_index // half_count
    row_local = jnp.arange(local_rows, dtype=jnp.int32)
    global_row = (row_local // BS * wide_count + wide_index) * BS + row_local % BS
    col_local = jnp.arange(local_cols, dtype=jnp.int32)
    global_col = (col_local // PW * narrow_count + narrow_index) * PW + col_local % PW
    child_names = lax.dynamic_slice_in_dim(child_map, child_side * block_total, block_total)
    named_cols = jnp.any(child_names[:, None] == (global_col // BS)[None, :], axis=0)
    groups = child_update.reshape(2, front_slots, BS, local_cols)
    groups = jnp.where(named_cols[None, None, None, :], groups, jnp.zeros_like(groups))
    kept_rows = lax.dynamic_index_in_dim(groups, child_side, 0, keepdims=False)
    leaving = lax.dynamic_index_in_dim(groups, 1 - child_side, 0, keepdims=False)
    arrived = from_partner(leaving, WIDE, half_count.bit_length() - 1)
    partner = (wide_index + half_count) % wide_count
    own_map = lax.dynamic_slice_in_dim(
        child_map, (wide_index * 2 + child_side) * front_slots, front_slots
    )
    got_map = lax.dynamic_slice_in_dim(
        child_map, (partner * 2 + child_side) * front_slots, front_slots
    )
    target = wide_index + wide_count * jnp.arange(front_slots, dtype=jnp.int32)
    own_select = (own_map[None, :] == target[:, None]).astype(jnp.float32)
    got_select = (got_map[None, :] == target[:, None]).astype(jnp.float32)
    own_part = jnp.dot(
        own_select,
        kept_rows.reshape(front_slots, BS * local_cols),
        precision=HIGHEST_PRECISION,
        preferred_element_type=jnp.float32,
    )
    got_part = jnp.dot(
        got_select,
        arrived.reshape(front_slots, BS * local_cols),
        precision=HIGHEST_PRECISION,
        preferred_element_type=jnp.float32,
    )
    matrix = front + (own_part + got_part).reshape(local_rows, local_cols)

    panel = narrow_bcast(matrix)
    blocks = wide_bcast(panel[:BS])
    diag_block = blocks[: N_BLOCKS // 2].reshape(PW, PW)
    col_rows = blocks[N_BLOCKS // 2 :].reshape(PW, PW)

    symmetric = jnp.tril(diag_block) + jnp.tril(diag_block, -1).T
    factor_diag = jnp.tril(jnp.linalg.cholesky(symmetric))
    inverse = triangular_inverse(factor_diag)
    own_factor = mm_t(panel, inverse)
    diag_rows = lax.dynamic_slice_in_dim(factor_diag, jnp.minimum(wide_index, 3) * BS, BS)
    top = jnp.where(wide_index * BS < PW, diag_rows, own_factor[:BS])
    own_factor = jnp.concatenate([top, own_factor[BS:]], 0)
    col_factor = mm_t(col_rows, inverse)
    update = mm_t(own_factor, col_factor)
    renewed = jnp.where(narrow_index == 0, own_factor, matrix - update)
    on_or_below = global_row[:, None] >= global_col[None, :]
    return jnp.where(on_or_below, renewed, jnp.zeros_like(renewed))


def solution(mesh):
    torus = Mesh(
        mesh.devices.reshape(8, 4, 2, mesh.shape["narrow"]),
        AXES,
    )
    placed = (P(WIDE, "narrow"), P(WIDE, "narrow"), P())
    return jax.shard_map(
        shards, mesh=torus, in_specs=placed, out_specs=P(WIDE, "narrow"), check_vma=False
    )
```

```python
import functools

import jax
import jax.numpy as jnp
from jax import lax
from jax.experimental import pallas as pl
from jax.experimental.pallas import tpu as pltpu
from jax.sharding import Mesh
from jax.sharding import PartitionSpec as P

BS = 128
PW = 512
WIDE = ("wide_0", "wide_1", "wide_2")
AXES = ("wide_0", "wide_1", "wide_2", "narrow")
MESH_ID = pl.DeviceIdType.MESH

HIGHEST_PRECISION = lax.Precision.HIGHEST


def from_partner(value, axis, distance):
    return lax.ppermute(value, axis, [(i, i ^ 1 << distance) for i in range(lax.axis_size(axis))])


def positions():
    return tuple(lax.axis_index(a) for a in AXES)


NARROW_CHUNKS = 4


def narrow_bcast_kernel(src_ref, out_ref, send_sem, recv_sem):
    y, x, h, q = positions()
    n = lax.axis_size("narrow")
    rows = out_ref.shape[0] // NARROW_CHUNKS
    even = q % 2 == 0
    has_parent = q > 0
    parent = jnp.where(even, q - 2, q - 1)
    kids = [(even, q + 1), (jnp.logical_and(even, q + 2 < n), q + 2)]

    barrier = pltpu.get_barrier_semaphore()

    @pl.when(has_parent)
    def _():
        pl.semaphore_signal(barrier, 1, device_id=(y, x, h, parent), device_id_type=MESH_ID)

    for cond, kid in kids:
        @pl.when(cond)
        def _():
            pl.semaphore_signal(barrier, 1, device_id=(y, x, h, kid), device_id_type=MESH_ID)

    peers = has_parent.astype(jnp.int32)
    for cond, kid in kids:
        peers = peers + cond.astype(jnp.int32)
    pl.semaphore_wait(barrier, peers)

    @pl.when(q == 0)
    def _():
        out_ref[...] = src_ref[...]

    def copy(src, c, k, kid):
        part = pl.ds(c * rows, rows)
        return pltpu.make_async_remote_copy(
            src_ref=src.at[part],
            dst_ref=out_ref.at[part],
            send_sem=send_sem.at[c, k],
            recv_sem=recv_sem.at[c],
            device_id=(y, x, h, kid),
            device_id_type=MESH_ID,
        )

    for c in range(NARROW_CHUNKS):
        @pl.when(has_parent)
        def _():
            copy(out_ref, c, 0, q).wait_recv()

        for k, (cond, kid) in enumerate(kids):
            @pl.when(jnp.logical_and(cond, q == 0))
            def _():
                copy(src_ref, c, k, kid).start()

            @pl.when(jnp.logical_and(cond, q != 0))
            def _():
                copy(out_ref, c, k, kid).start()

    for c in range(NARROW_CHUNKS):
        for k, (cond, kid) in enumerate(kids):
            @pl.when(cond)
            def _():
                copy(out_ref, c, k, kid).wait_send()


def narrow_bcast(panel):
    return pl.pallas_call(
        narrow_bcast_kernel,
        out_shape=jax.ShapeDtypeStruct(panel.shape, panel.dtype),
        in_specs=[pl.BlockSpec(memory_space=pltpu.VMEM)],
        out_specs=pl.BlockSpec(memory_space=pltpu.VMEM),
        scratch_shapes=[
            pltpu.SemaphoreType.DMA((NARROW_CHUNKS, 2)),
            pltpu.SemaphoreType.DMA((NARROW_CHUNKS,)),
        ],
        compiler_params=pltpu.CompilerParams(collective_id=0, has_side_effects=True),
    )(panel)


N_BLOCKS = 8
N_SLOTS = 6
MAX_DEPTH = 8


def wide_tree(y, x, h, root, ny, nx):
    y0 = root // (2 * nx)
    x0 = (root // 2) % nx
    h0 = root % 2
    dy = (y - y0 + ny) % ny
    dx = (x - x0 + nx) % nx
    dh = (h - h0 + 2) % 2
    half = ny // 2
    at_y0 = dy == 0
    at_x0 = jnp.logical_and(at_y0, dx == 0)
    is_root = jnp.logical_and(at_x0, dh == 0)
    up = jnp.logical_and(dy >= 1, dy <= half)
    py = jnp.where(up, (y + ny - 1) % ny, (y + 1) % ny)
    px = jnp.where(dx == 2, (x + nx - 1) % nx, x0)
    parent_y = jnp.where(at_y0, y, py)
    parent_x = jnp.where(jnp.logical_and(at_y0, dx != 0), px, x)
    parent_h = jnp.where(at_x0, h0, h)
    parent = (parent_y, parent_x, parent_h)
    kids = [
        (is_root, (y, x, 1 - h)),
        (at_x0, (y, (x + 1) % nx, h)),
        (at_x0, (y, (x + nx - 1) % nx, h)),
        (jnp.logical_and(at_y0, dx == 1), (y, (x + 1) % nx, h)),
        (dy < half, ((y + 1) % ny, x, h)),
        (jnp.logical_or(at_y0, dy > half + 1), ((y + ny - 1) % ny, x, h)),
    ]
    x_depth = jnp.where(dx == 0, 0, jnp.where(dx == 2, 2, 1))
    y_depth = jnp.where(dy <= half, dy, ny - dy)
    depth = dh + x_depth + y_depth
    return is_root, parent, kids, depth


def wide_bcast_kernel(src_ref, out_ref, send_sem, recv_sem):
    y, x, h, q = positions()
    ny = lax.axis_size("wide_0")
    nx = lax.axis_size("wide_1")
    trees = []
    for j in range(N_BLOCKS):
        if j < N_BLOCKS // 2:
            root = j
            active = q >= 0
        else:
            root = 4 * q + (j - N_BLOCKS // 2)
            active = q > 0
        is_root, parent, kids, depth = wide_tree(y, x, h, root, ny, nx)
        trees.append((active, is_root, parent, kids, depth))

    barrier = pltpu.get_barrier_semaphore()
    for active, is_root, parent, kids, depth in trees:
        @pl.when(jnp.logical_and(active, jnp.logical_not(is_root)))
        def _():
            pl.semaphore_signal(barrier, 1, device_id=(*parent, q), device_id_type=MESH_ID)

        for cond, kid in kids:
            @pl.when(jnp.logical_and(active, cond))
            def _():
                pl.semaphore_signal(barrier, 1, device_id=(*kid, q), device_id_type=MESH_ID)

    peers = jnp.int32(0)
    for active, is_root, parent, kids, depth in trees:
        peers = peers + jnp.logical_and(active, jnp.logical_not(is_root)).astype(jnp.int32)
        for cond, kid in kids:
            peers = peers + jnp.logical_and(active, cond).astype(jnp.int32)
    pl.semaphore_wait(barrier, peers)

    def copy(src, j, k, kid):
        return pltpu.make_async_remote_copy(
            src_ref=src,
            dst_ref=out_ref.at[j],
            send_sem=send_sem.at[j, k],
            recv_sem=recv_sem.at[j],
            device_id=(*kid, q),
            device_id_type=MESH_ID,
        )

    for j, (active, is_root, parent, kids, depth) in enumerate(trees):
        root_here = jnp.logical_and(active, is_root)

        for k, (cond, kid) in enumerate(kids):
            @pl.when(jnp.logical_and(root_here, cond))
            def _():
                copy(src_ref, j, k, kid).start()

        @pl.when(root_here)
        def _():
            out_ref[j] = src_ref[...]

    for level in range(1, MAX_DEPTH):
        for j, (active, is_root, parent, kids, depth) in enumerate(trees):
            here = jnp.logical_and(active, depth == level)

            @pl.when(here)
            def _():
                copy(out_ref.at[j], j, 0, (y, x, h)).wait_recv()

            for k, (cond, kid) in enumerate(kids):
                @pl.when(jnp.logical_and(here, cond))
                def _():
                    copy(out_ref.at[j], j, k, kid).start()

    for j, (active, is_root, parent, kids, depth) in enumerate(trees):
        for k, (cond, kid) in enumerate(kids):
            @pl.when(jnp.logical_and(active, cond))
            def _():
                copy(out_ref.at[j], j, k, kid).wait_send()


def wide_bcast(block):
    return pl.pallas_call(
        wide_bcast_kernel,
        out_shape=jax.ShapeDtypeStruct((N_BLOCKS, *block.shape), block.dtype),
        in_specs=[pl.BlockSpec(memory_space=pltpu.VMEM)],
        out_specs=pl.BlockSpec(memory_space=pltpu.VMEM),
        scratch_shapes=[
            pltpu.SemaphoreType.DMA((N_BLOCKS, N_SLOTS)),
            pltpu.SemaphoreType.DMA((N_BLOCKS,)),
        ],
        compiler_params=pltpu.CompilerParams(collective_id=1, has_side_effects=True),
    )(block)


def mm_t(a, b):
    return lax.dot_general(
        a, b, (((1,), (1,)), ((), ())),
        precision=HIGHEST_PRECISION, preferred_element_type=jnp.float32,
    )


def mm(a, b):
    return jnp.dot(a, b, precision=HIGHEST_PRECISION, preferred_element_type=jnp.float32)


def newton_inverse(lower, start, steps):
    inverse = start
    for _ in range(steps):
        inverse = 2 * inverse - mm(inverse, mm(lower, inverse))
    return inverse


def diagonal_inverse(lower):
    n = lower.shape[0]
    on_diag = lax.broadcasted_iota(jnp.int32, (n, n), 0) == lax.broadcasted_iota(jnp.int32, (n, n), 1)
    diag = jnp.sum(jnp.where(on_diag, lower, 0.0), axis=1, keepdims=True)
    return jnp.where(on_diag, 1.0 / diag, 0.0)


def cholesky_and_inverse(symmetric):
    n = symmetric.shape[0]
    nb = n // BS
    work = symmetric
    cols = []
    block_inverses = []
    for b in range(nb):
        head = work[:BS, :BS]
        diag = jnp.tril(jnp.linalg.cholesky(head))
        inv = newton_inverse(diag, diagonal_inverse(diag), (BS - 1).bit_length())
        block_inverses.append(inv)
        if b + 1 < nb:
            below = mm_t(work[BS:, :BS], inv)
            work = work[BS:, BS:] - mm_t(below, below)
            cols.append(jnp.concatenate([jnp.zeros((b * BS, BS), jnp.float32), diag, below], 0))
        else:
            cols.append(jnp.concatenate([jnp.zeros((b * BS, BS), jnp.float32), diag], 0))
    factor = jnp.concatenate(cols, 1)
    start = jnp.zeros((n, n), jnp.float32)
    for b in range(nb):
        start = lax.dynamic_update_slice(start, block_inverses[b], (b * BS, b * BS))
    inverse = newton_inverse(factor, start, max(1, (nb - 1).bit_length()))
    return factor, inverse


def shards(front, child_update, child_map):
    wide_count = lax.axis_size(WIDE)
    narrow_count = lax.axis_size("narrow")
    wide_index = lax.axis_index(WIDE)
    narrow_index = lax.axis_index("narrow")
    half_count = wide_count // 2
    local_rows, local_cols = front.shape
    front_slots = local_rows // BS
    block_total = front_slots * wide_count
    child_side = wide_index // half_count
    row_local = jnp.arange(local_rows, dtype=jnp.int32)
    global_row = (row_local // BS * wide_count + wide_index) * BS + row_local % BS
    col_local = jnp.arange(local_cols, dtype=jnp.int32)
    global_col = (col_local // PW * narrow_count + narrow_index) * PW + col_local % PW
    child_names = lax.dynamic_slice_in_dim(child_map, child_side * block_total, block_total)
    named_cols = jnp.any(child_names[:, None] == (global_col // BS)[None, :], axis=0)
    groups = child_update.reshape(2, front_slots, BS, local_cols)
    groups = jnp.where(named_cols[None, None, None, :], groups, jnp.zeros_like(groups))
    kept_rows = lax.dynamic_index_in_dim(groups, child_side, 0, keepdims=False)
    leaving = lax.dynamic_index_in_dim(groups, 1 - child_side, 0, keepdims=False)
    arrived = from_partner(leaving, WIDE, half_count.bit_length() - 1)
    partner = (wide_index + half_count) % wide_count
    own_map = lax.dynamic_slice_in_dim(
        child_map, (wide_index * 2 + child_side) * front_slots, front_slots
    )
    got_map = lax.dynamic_slice_in_dim(
        child_map, (partner * 2 + child_side) * front_slots, front_slots
    )
    target = wide_index + wide_count * jnp.arange(front_slots, dtype=jnp.int32)
    own_select = (own_map[None, :] == target[:, None]).astype(jnp.float32)
    got_select = (got_map[None, :] == target[:, None]).astype(jnp.float32)
    own_part = jnp.dot(
        own_select,
        kept_rows.reshape(front_slots, BS * local_cols),
        precision=HIGHEST_PRECISION,
        preferred_element_type=jnp.float32,
    )
    got_part = jnp.dot(
        got_select,
        arrived.reshape(front_slots, BS * local_cols),
        precision=HIGHEST_PRECISION,
        preferred_element_type=jnp.float32,
    )
    matrix = front + (own_part + got_part).reshape(local_rows, local_cols)

    panel = narrow_bcast(matrix)
    blocks = wide_bcast(panel[:BS])
    diag_block = blocks[: N_BLOCKS // 2].reshape(PW, PW)
    col_rows = blocks[N_BLOCKS // 2 :].reshape(PW, PW)

    symmetric = jnp.tril(diag_block) + jnp.tril(diag_block, -1).T
    factor_diag, inverse = cholesky_and_inverse(symmetric)
    own_factor = mm_t(panel, inverse)
    diag_rows = lax.dynamic_slice_in_dim(factor_diag, jnp.minimum(wide_index, 3) * BS, BS)
    top = jnp.where(wide_index * BS < PW, diag_rows, own_factor[:BS])
    own_factor = jnp.concatenate([top, own_factor[BS:]], 0)
    col_factor = mm_t(col_rows, inverse)
    update = mm_t(own_factor, col_factor)
    renewed = jnp.where(narrow_index == 0, own_factor, matrix - update)
    on_or_below = global_row[:, None] >= global_col[None, :]
    return jnp.where(on_or_below, renewed, jnp.zeros_like(renewed))


def solution(mesh):
    torus = Mesh(
        mesh.devices.reshape(8, 4, 2, mesh.shape["narrow"]),
        AXES,
    )
    placed = (P(WIDE, "narrow"), P(WIDE, "narrow"), P())
    return jax.shard_map(
        shards, mesh=torus, in_specs=placed, out_specs=P(WIDE, "narrow"), check_vma=False
    )
```

```python
import functools

import jax
import jax.numpy as jnp
from jax import lax
from jax.experimental import pallas as pl
from jax.experimental.pallas import tpu as pltpu
from jax.sharding import Mesh
from jax.sharding import PartitionSpec as P

BS = 128
PW = 512
WIDE = ("wide_0", "wide_1", "wide_2")
AXES = ("wide_0", "wide_1", "wide_2", "narrow")
MESH_ID = pl.DeviceIdType.MESH

HIGHEST_PRECISION = lax.Precision.HIGHEST


def from_partner(value, axis, distance):
    return lax.ppermute(value, axis, [(i, i ^ 1 << distance) for i in range(lax.axis_size(axis))])


def positions():
    return tuple(lax.axis_index(a) for a in AXES)


def narrow_bcast_kernel(chunks, src_ref, out_ref, send_sem, recv_sem):
    y, x, h, q = positions()
    n = lax.axis_size("narrow")
    rows = out_ref.shape[0] // chunks
    even = q % 2 == 0
    has_parent = q > 0
    parent = jnp.where(even, q - 2, q - 1)
    kids = [(even, q + 1), (jnp.logical_and(even, q + 2 < n), q + 2)]

    barrier = pltpu.get_barrier_semaphore()

    @pl.when(has_parent)
    def _():
        pl.semaphore_signal(barrier, 1, device_id=(y, x, h, parent), device_id_type=MESH_ID)

    for cond, kid in kids:
        @pl.when(cond)
        def _():
            pl.semaphore_signal(barrier, 1, device_id=(y, x, h, kid), device_id_type=MESH_ID)

    peers = has_parent.astype(jnp.int32)
    for cond, kid in kids:
        peers = peers + cond.astype(jnp.int32)
    pl.semaphore_wait(barrier, peers)

    @pl.when(q == 0)
    def _():
        out_ref[...] = src_ref[...]

    def copy(src, c, k, kid):
        part = pl.ds(c * rows, rows)
        return pltpu.make_async_remote_copy(
            src_ref=src.at[part],
            dst_ref=out_ref.at[part],
            send_sem=send_sem.at[c, k],
            recv_sem=recv_sem.at[c],
            device_id=(y, x, h, kid),
            device_id_type=MESH_ID,
        )

    for c in range(chunks):
        @pl.when(has_parent)
        def _():
            copy(out_ref, c, 0, q).wait_recv()

        for k, (cond, kid) in enumerate(kids):
            @pl.when(jnp.logical_and(cond, q == 0))
            def _():
                copy(src_ref, c, k, kid).start()

            @pl.when(jnp.logical_and(cond, q != 0))
            def _():
                copy(out_ref, c, k, kid).start()

    for c in range(chunks):
        for k, (cond, kid) in enumerate(kids):
            @pl.when(cond)
            def _():
                copy(out_ref, c, k, kid).wait_send()


def narrow_bcast(panel, chunks, collective_id):
    return pl.pallas_call(
        functools.partial(narrow_bcast_kernel, chunks),
        out_shape=jax.ShapeDtypeStruct(panel.shape, panel.dtype),
        in_specs=[pl.BlockSpec(memory_space=pltpu.VMEM)],
        out_specs=pl.BlockSpec(memory_space=pltpu.VMEM),
        scratch_shapes=[
            pltpu.SemaphoreType.DMA((chunks, 2)),
            pltpu.SemaphoreType.DMA((chunks,)),
        ],
        compiler_params=pltpu.CompilerParams(collective_id=collective_id, has_side_effects=True),
    )(panel)


N_BLOCKS = 8
N_SLOTS = 6
MAX_DEPTH = 8


def wide_tree(y, x, h, root, ny, nx):
    y0 = root // (2 * nx)
    x0 = (root // 2) % nx
    h0 = root % 2
    dy = (y - y0 + ny) % ny
    dx = (x - x0 + nx) % nx
    dh = (h - h0 + 2) % 2
    half = ny // 2
    at_y0 = dy == 0
    at_x0 = jnp.logical_and(at_y0, dx == 0)
    is_root = jnp.logical_and(at_x0, dh == 0)
    up = jnp.logical_and(dy >= 1, dy <= half)
    py = jnp.where(up, (y + ny - 1) % ny, (y + 1) % ny)
    px = jnp.where(dx == 2, (x + nx - 1) % nx, x0)
    parent_y = jnp.where(at_y0, y, py)
    parent_x = jnp.where(jnp.logical_and(at_y0, dx != 0), px, x)
    parent_h = jnp.where(at_x0, h0, h)
    parent = (parent_y, parent_x, parent_h)
    kids = [
        (is_root, (y, x, 1 - h)),
        (at_x0, (y, (x + 1) % nx, h)),
        (at_x0, (y, (x + nx - 1) % nx, h)),
        (jnp.logical_and(at_y0, dx == 1), (y, (x + 1) % nx, h)),
        (dy < half, ((y + 1) % ny, x, h)),
        (jnp.logical_or(at_y0, dy > half + 1), ((y + ny - 1) % ny, x, h)),
    ]
    x_depth = jnp.where(dx == 0, 0, jnp.where(dx == 2, 2, 1))
    y_depth = jnp.where(dy <= half, dy, ny - dy)
    depth = dh + x_depth + y_depth
    return is_root, parent, kids, depth


def wide_bcast_kernel(src_ref, out_ref, send_sem, recv_sem):
    y, x, h, q = positions()
    ny = lax.axis_size("wide_0")
    nx = lax.axis_size("wide_1")
    trees = []
    for j in range(N_BLOCKS):
        if j < N_BLOCKS // 2:
            root = j
            active = q >= 0
        else:
            root = 4 * q + (j - N_BLOCKS // 2)
            active = q > 0
        is_root, parent, kids, depth = wide_tree(y, x, h, root, ny, nx)
        trees.append((active, is_root, parent, kids, depth))

    barrier = pltpu.get_barrier_semaphore()
    for active, is_root, parent, kids, depth in trees:
        @pl.when(jnp.logical_and(active, jnp.logical_not(is_root)))
        def _():
            pl.semaphore_signal(barrier, 1, device_id=(*parent, q), device_id_type=MESH_ID)

        for cond, kid in kids:
            @pl.when(jnp.logical_and(active, cond))
            def _():
                pl.semaphore_signal(barrier, 1, device_id=(*kid, q), device_id_type=MESH_ID)

    peers = jnp.int32(0)
    for active, is_root, parent, kids, depth in trees:
        peers = peers + jnp.logical_and(active, jnp.logical_not(is_root)).astype(jnp.int32)
        for cond, kid in kids:
            peers = peers + jnp.logical_and(active, cond).astype(jnp.int32)
    pl.semaphore_wait(barrier, peers)

    def copy(src, j, k, kid):
        return pltpu.make_async_remote_copy(
            src_ref=src,
            dst_ref=out_ref.at[j],
            send_sem=send_sem.at[j, k],
            recv_sem=recv_sem.at[j],
            device_id=(*kid, q),
            device_id_type=MESH_ID,
        )

    for j, (active, is_root, parent, kids, depth) in enumerate(trees):
        root_here = jnp.logical_and(active, is_root)

        for k, (cond, kid) in enumerate(kids):
            @pl.when(jnp.logical_and(root_here, cond))
            def _():
                copy(src_ref, j, k, kid).start()

        @pl.when(root_here)
        def _():
            out_ref[j] = src_ref[...]

    for level in range(1, MAX_DEPTH):
        for j, (active, is_root, parent, kids, depth) in enumerate(trees):
            here = jnp.logical_and(active, depth == level)

            @pl.when(here)
            def _():
                copy(out_ref.at[j], j, 0, (y, x, h)).wait_recv()

            for k, (cond, kid) in enumerate(kids):
                @pl.when(jnp.logical_and(here, cond))
                def _():
                    copy(out_ref.at[j], j, k, kid).start()

    for j, (active, is_root, parent, kids, depth) in enumerate(trees):
        for k, (cond, kid) in enumerate(kids):
            @pl.when(jnp.logical_and(active, cond))
            def _():
                copy(out_ref.at[j], j, k, kid).wait_send()


def wide_bcast(block):
    return pl.pallas_call(
        wide_bcast_kernel,
        out_shape=jax.ShapeDtypeStruct((N_BLOCKS, *block.shape), block.dtype),
        in_specs=[pl.BlockSpec(memory_space=pltpu.VMEM)],
        out_specs=pl.BlockSpec(memory_space=pltpu.VMEM),
        scratch_shapes=[
            pltpu.SemaphoreType.DMA((N_BLOCKS, N_SLOTS)),
            pltpu.SemaphoreType.DMA((N_BLOCKS,)),
        ],
        compiler_params=pltpu.CompilerParams(collective_id=2, has_side_effects=True),
    )(block)


def mm_t(a, b):
    return lax.dot_general(
        a, b, (((1,), (1,)), ((), ())),
        precision=HIGHEST_PRECISION, preferred_element_type=jnp.float32,
    )


def mm(a, b):
    return jnp.dot(a, b, precision=HIGHEST_PRECISION, preferred_element_type=jnp.float32)


def newton_inverse(lower, start, steps):
    inverse = start
    for _ in range(steps):
        inverse = 2 * inverse - mm(inverse, mm(lower, inverse))
    return inverse


def diagonal_inverse(lower):
    n = lower.shape[0]
    on_diag = lax.broadcasted_iota(jnp.int32, (n, n), 0) == lax.broadcasted_iota(jnp.int32, (n, n), 1)
    diag = jnp.sum(jnp.where(on_diag, lower, 0.0), axis=1, keepdims=True)
    return jnp.where(on_diag, 1.0 / diag, 0.0)


def cholesky_and_inverse(symmetric):
    n = symmetric.shape[0]
    nb = n // BS
    work = symmetric
    cols = []
    block_inverses = []
    for b in range(nb):
        head = work[:BS, :BS]
        diag = jnp.tril(jnp.linalg.cholesky(head))
        inv = newton_inverse(diag, diagonal_inverse(diag), (BS - 1).bit_length())
        block_inverses.append(inv)
        if b + 1 < nb:
            below = mm_t(work[BS:, :BS], inv)
            work = work[BS:, BS:] - mm_t(below, below)
            cols.append(jnp.concatenate([jnp.zeros((b * BS, BS), jnp.float32), diag, below], 0))
        else:
            cols.append(jnp.concatenate([jnp.zeros((b * BS, BS), jnp.float32), diag], 0))
    factor = jnp.concatenate(cols, 1)
    start = jnp.zeros((n, n), jnp.float32)
    for b in range(nb):
        start = lax.dynamic_update_slice(start, block_inverses[b], (b * BS, b * BS))
    inverse = newton_inverse(factor, start, max(1, (nb - 1).bit_length()))
    return factor, inverse


def shards(front, child_update, child_map):
    wide_count = lax.axis_size(WIDE)
    narrow_count = lax.axis_size("narrow")
    wide_index = lax.axis_index(WIDE)
    narrow_index = lax.axis_index("narrow")
    half_count = wide_count // 2
    local_rows, local_cols = front.shape
    front_slots = local_rows // BS
    block_total = front_slots * wide_count
    child_side = wide_index // half_count
    row_local = jnp.arange(local_rows, dtype=jnp.int32)
    global_row = (row_local // BS * wide_count + wide_index) * BS + row_local % BS
    col_local = jnp.arange(local_cols, dtype=jnp.int32)
    global_col = (col_local // PW * narrow_count + narrow_index) * PW + col_local % PW
    child_names = lax.dynamic_slice_in_dim(child_map, child_side * block_total, block_total)
    named_cols = jnp.any(child_names[:, None] == (global_col // BS)[None, :], axis=0)
    groups = child_update.reshape(2, front_slots, BS, local_cols)
    groups = jnp.where(named_cols[None, None, None, :], groups, jnp.zeros_like(groups))
    kept_rows = lax.dynamic_index_in_dim(groups, child_side, 0, keepdims=False)
    leaving = lax.dynamic_index_in_dim(groups, 1 - child_side, 0, keepdims=False)
    partner = (wide_index + half_count) % wide_count
    own_map = lax.dynamic_slice_in_dim(
        child_map, (wide_index * 2 + child_side) * front_slots, front_slots
    )
    got_map = lax.dynamic_slice_in_dim(
        child_map, (partner * 2 + child_side) * front_slots, front_slots
    )
    distance = half_count.bit_length() - 1
    arrived_first = from_partner(leaving[:1], WIDE, distance)
    rest, _ = lax.optimization_barrier((leaving[1:], arrived_first))
    arrived_rest = from_partner(rest, WIDE, distance)
    slot0 = (
        front[:BS]
        + jnp.where(own_map[0] == wide_index, kept_rows[0], 0.0)
        + jnp.where(got_map[0] == wide_index, arrived_first[0], 0.0)
    )
    panel0 = narrow_bcast(slot0, 4, 0)
    blocks = wide_bcast(panel0)
    diag_block = blocks[: N_BLOCKS // 2].reshape(PW, PW)
    col_rows = blocks[N_BLOCKS // 2 :].reshape(PW, PW)

    symmetric = jnp.tril(diag_block) + jnp.tril(diag_block, -1).T
    factor_diag, inverse = cholesky_and_inverse(symmetric)

    arrived = jnp.concatenate([arrived_first, arrived_rest], 0)
    target = wide_index + wide_count * jnp.arange(front_slots, dtype=jnp.int32)
    own_select = (own_map[None, :] == target[:, None]).astype(jnp.float32)
    got_select = (got_map[None, :] == target[:, None]).astype(jnp.float32)
    own_part = jnp.dot(
        own_select,
        kept_rows.reshape(front_slots, BS * local_cols),
        precision=HIGHEST_PRECISION,
        preferred_element_type=jnp.float32,
    )
    got_part = jnp.dot(
        got_select,
        arrived.reshape(front_slots, BS * local_cols),
        precision=HIGHEST_PRECISION,
        preferred_element_type=jnp.float32,
    )
    matrix = front + (own_part + got_part).reshape(local_rows, local_cols)
    panel = jnp.concatenate([panel0, narrow_bcast(matrix[BS:], front_slots - 1, 1)], 0)
    own_factor = mm_t(panel, inverse)
    diag_rows = lax.dynamic_slice_in_dim(factor_diag, jnp.minimum(wide_index, 3) * BS, BS)
    top = jnp.where(wide_index * BS < PW, diag_rows, own_factor[:BS])
    own_factor = jnp.concatenate([top, own_factor[BS:]], 0)
    col_factor = mm_t(col_rows, inverse)
    update = mm_t(own_factor, col_factor)
    renewed = jnp.where(narrow_index == 0, own_factor, matrix - update)
    on_or_below = global_row[:, None] >= global_col[None, :]
    return jnp.where(on_or_below, renewed, jnp.zeros_like(renewed))


def solution(mesh):
    torus = Mesh(
        mesh.devices.reshape(8, 4, 2, mesh.shape["narrow"]),
        AXES,
    )
    placed = (P(WIDE, "narrow"), P(WIDE, "narrow"), P())
    return jax.shard_map(
        shards, mesh=torus, in_specs=placed, out_specs=P(WIDE, "narrow"), check_vma=False
    )
```

```python
import functools

import jax
import jax.numpy as jnp
from jax import lax
from jax.experimental import pallas as pl
from jax.experimental.pallas import tpu as pltpu
from jax.sharding import Mesh
from jax.sharding import PartitionSpec as P

BS = 128
PW = 512
WIDE = ("wide_0", "wide_1", "wide_2")
AXES = ("wide_0", "wide_1", "wide_2", "narrow")
MESH_ID = pl.DeviceIdType.MESH

HIGHEST_PRECISION = lax.Precision.HIGHEST


def from_partner(value, axis, distance):
    return lax.ppermute(value, axis, [(i, i ^ 1 << distance) for i in range(lax.axis_size(axis))])


def positions():
    return tuple(lax.axis_index(a) for a in AXES)


def narrow_tree(q, n):
    even = q % 2 == 0
    parent = jnp.where(even, q - 2, q - 1)
    kids = [(even, q + 1), (jnp.logical_and(even, q + 2 < n), q + 2)]
    return q > 0, parent, kids


def wide_tree(y, x, h, root, ny, nx):
    y0 = root // (2 * nx)
    x0 = (root // 2) % nx
    h0 = root % 2
    dy = (y - y0 + ny) % ny
    dx = (x - x0 + nx) % nx
    dh = (h - h0 + 2) % 2
    half = ny // 2
    at_y0 = dy == 0
    at_x0 = jnp.logical_and(at_y0, dx == 0)
    is_root = jnp.logical_and(at_x0, dh == 0)
    up = jnp.logical_and(dy >= 1, dy <= half)
    py = jnp.where(up, (y + ny - 1) % ny, (y + 1) % ny)
    px = jnp.where(dx == 2, (x + nx - 1) % nx, x0)
    parent_y = jnp.where(at_y0, y, py)
    parent_x = jnp.where(jnp.logical_and(at_y0, dx != 0), px, x)
    parent_h = jnp.where(at_x0, h0, h)
    parent = (parent_y, parent_x, parent_h)
    kids = [
        (is_root, (y, x, 1 - h)),
        (at_x0, (y, (x + 1) % nx, h)),
        (at_x0, (y, (x + nx - 1) % nx, h)),
        (jnp.logical_and(at_y0, dx == 1), (y, (x + 1) % nx, h)),
        (dy < half, ((y + 1) % ny, x, h)),
        (jnp.logical_or(at_y0, dy > half + 1), ((y + ny - 1) % ny, x, h)),
    ]
    x_depth = jnp.where(dx == 0, 0, jnp.where(dx == 2, 2, 1))
    y_depth = jnp.where(dy <= half, dy, ny - dy)
    return is_root, parent, kids, dh + x_depth + y_depth


N_CHUNKS = 4
N_BLOCKS = 8
N_SLOTS = 7
MAX_DEPTH = 9


def bcast_kernel(src_ref, panel_ref, blocks_ref, nsend, nrecv, wsend, wrecv):
    y, x, h, q = positions()
    n = lax.axis_size("narrow")
    ny = lax.axis_size("wide_0")
    nx = lax.axis_size("wide_1")
    rows = panel_ref.shape[0] // N_CHUNKS
    even = q % 2 == 0
    n_has_parent, n_parent, n_kids = narrow_tree(q, n)

    trees = []
    for j in range(N_BLOCKS):
        if j < N_BLOCKS // 2:
            is_root, parent, kids, depth = wide_tree(y, x, h, j, ny, nx)
            active = q >= 0
            parent = tuple(jnp.where(even, p, o) for p, o in zip((*parent, q), (y, x, h, q - 1)))
            kids = [(jnp.logical_and(even, c), (*k, q)) for c, k in kids]
            kids.append((even, (y, x, h, q + 1)))
            is_root = jnp.logical_and(even, is_root)
            depth = depth + 1 - even.astype(jnp.int32)
        else:
            root = 4 * q + (j - N_BLOCKS // 2)
            is_root, parent, kids, depth = wide_tree(y, x, h, root, ny, nx)
            active = q > 0
            parent = (*parent, q)
            kids = [(c, (*k, q)) for c, k in kids]
            kids.append((q < 0, (y, x, h, q)))
        trees.append((active, is_root, parent, kids, depth))

    barrier = pltpu.get_barrier_semaphore()

    @pl.when(n_has_parent)
    def _():
        pl.semaphore_signal(barrier, 1, device_id=(y, x, h, n_parent), device_id_type=MESH_ID)

    peers = n_has_parent.astype(jnp.int32)
    for cond, kid in n_kids:
        peers = peers + cond.astype(jnp.int32)

        @pl.when(cond)
        def _():
            pl.semaphore_signal(barrier, 1, device_id=(y, x, h, kid), device_id_type=MESH_ID)

    for active, is_root, parent, kids, depth in trees:
        has_parent = jnp.logical_and(active, jnp.logical_not(is_root))
        peers = peers + has_parent.astype(jnp.int32)

        @pl.when(has_parent)
        def _():
            pl.semaphore_signal(barrier, 1, device_id=parent, device_id_type=MESH_ID)

        for cond, kid in kids:
            go = jnp.logical_and(active, cond)
            peers = peers + go.astype(jnp.int32)

            @pl.when(go)
            def _():
                pl.semaphore_signal(barrier, 1, device_id=kid, device_id_type=MESH_ID)

    pl.semaphore_wait(barrier, peers)

    def narrow_copy(src, c, k, kid):
        part = pl.ds(c * rows, rows)
        return pltpu.make_async_remote_copy(
            src_ref=src.at[part],
            dst_ref=panel_ref.at[part],
            send_sem=nsend.at[c, k],
            recv_sem=nrecv.at[c],
            device_id=(y, x, h, kid),
            device_id_type=MESH_ID,
        )

    def narrow_step(c):
        @pl.when(n_has_parent)
        def _():
            narrow_copy(panel_ref, c, 0, q).wait_recv()

        for k, (cond, kid) in enumerate(n_kids):
            @pl.when(jnp.logical_and(cond, q == 0))
            def _():
                narrow_copy(src_ref, c, k, kid).start()

            @pl.when(jnp.logical_and(cond, q != 0))
            def _():
                narrow_copy(panel_ref, c, k, kid).start()

    def wide_copy(src, j, k, kid):
        return pltpu.make_async_remote_copy(
            src_ref=src,
            dst_ref=blocks_ref.at[j],
            send_sem=wsend.at[j, k],
            recv_sem=wrecv.at[j],
            device_id=kid,
            device_id_type=MESH_ID,
        )

    @pl.when(q == 0)
    def _():
        for c in range(N_CHUNKS):
            narrow_step(c)
        panel_ref[...] = src_ref[...]

    @pl.when(q != 0)
    def _():
        narrow_step(0)

    for j, (active, is_root, parent, kids, depth) in enumerate(trees):
        root_here = jnp.logical_and(active, is_root)
        for k, (cond, kid) in enumerate(kids):
            @pl.when(jnp.logical_and(jnp.logical_and(root_here, cond), q == 0))
            def _():
                wide_copy(src_ref.at[pl.ds(0, rows)], j, k, kid).start()

            @pl.when(jnp.logical_and(jnp.logical_and(root_here, cond), q != 0))
            def _():
                wide_copy(panel_ref.at[pl.ds(0, rows)], j, k, kid).start()

        @pl.when(jnp.logical_and(root_here, q == 0))
        def _():
            blocks_ref[j] = src_ref[pl.ds(0, rows)]

        @pl.when(jnp.logical_and(root_here, q != 0))
        def _():
            blocks_ref[j] = panel_ref[pl.ds(0, rows)]

    for level in range(1, MAX_DEPTH):
        for j, (active, is_root, parent, kids, depth) in enumerate(trees):
            here = jnp.logical_and(active, depth == level)

            @pl.when(here)
            def _():
                wide_copy(blocks_ref.at[j], j, 0, (y, x, h, q)).wait_recv()

            for k, (cond, kid) in enumerate(kids):
                @pl.when(jnp.logical_and(here, cond))
                def _():
                    wide_copy(blocks_ref.at[j], j, k, kid).start()

    @pl.when(q != 0)
    def _():
        for c in range(1, N_CHUNKS):
            narrow_step(c)

    for c in range(N_CHUNKS):
        for k, (cond, kid) in enumerate(n_kids):
            @pl.when(cond)
            def _():
                narrow_copy(panel_ref, c, k, kid).wait_send()

    for j, (active, is_root, parent, kids, depth) in enumerate(trees):
        for k, (cond, kid) in enumerate(kids):
            @pl.when(jnp.logical_and(active, cond))
            def _():
                wide_copy(blocks_ref.at[j], j, k, kid).wait_send()


def broadcast(panel):
    rows = panel.shape[0] // N_CHUNKS
    vmem = pl.BlockSpec(memory_space=pltpu.VMEM)
    return pl.pallas_call(
        bcast_kernel,
        out_shape=(
            jax.ShapeDtypeStruct(panel.shape, panel.dtype),
            jax.ShapeDtypeStruct((N_BLOCKS, rows, panel.shape[1]), panel.dtype),
        ),
        in_specs=[vmem],
        out_specs=(vmem, vmem),
        scratch_shapes=[
            pltpu.SemaphoreType.DMA((N_CHUNKS, 2)),
            pltpu.SemaphoreType.DMA((N_CHUNKS,)),
            pltpu.SemaphoreType.DMA((N_BLOCKS, N_SLOTS)),
            pltpu.SemaphoreType.DMA((N_BLOCKS,)),
        ],
        compiler_params=pltpu.CompilerParams(collective_id=0, has_side_effects=True),
    )(panel)


def mm_t(a, b):
    return lax.dot_general(
        a, b, (((1,), (1,)), ((), ())),
        precision=HIGHEST_PRECISION, preferred_element_type=jnp.float32,
    )


def mm(a, b):
    return jnp.dot(a, b, precision=HIGHEST_PRECISION, preferred_element_type=jnp.float32)


def newton_inverse(lower, start, steps):
    inverse = start
    for _ in range(steps):
        inverse = 2 * inverse - mm(inverse, mm(lower, inverse))
    return inverse


def diagonal_inverse(lower):
    n = lower.shape[0]
    on_diag = lax.broadcasted_iota(jnp.int32, (n, n), 0) == lax.broadcasted_iota(jnp.int32, (n, n), 1)
    diag = jnp.sum(jnp.where(on_diag, lower, 0.0), axis=1, keepdims=True)
    return jnp.where(on_diag, 1.0 / diag, 0.0)


def cholesky_and_inverse(symmetric):
    n = symmetric.shape[0]
    nb = n // BS
    work = symmetric
    cols = []
    block_inverses = []
    for b in range(nb):
        head = work[:BS, :BS]
        diag = jnp.tril(jnp.linalg.cholesky(head, symmetrize_input=False))
        inv = newton_inverse(diag, diagonal_inverse(diag), (BS - 1).bit_length())
        block_inverses.append(inv)
        if b + 1 < nb:
            below = mm_t(work[BS:, :BS], inv)
            work = work[BS:, BS:] - mm_t(below, below)
            cols.append(jnp.concatenate([jnp.zeros((b * BS, BS), jnp.float32), diag, below], 0))
        else:
            cols.append(jnp.concatenate([jnp.zeros((b * BS, BS), jnp.float32), diag], 0))
    factor = jnp.concatenate(cols, 1)
    start = jnp.zeros((n, n), jnp.float32)
    for b in range(nb):
        start = lax.dynamic_update_slice(start, block_inverses[b], (b * BS, b * BS))
    inverse = newton_inverse(factor, start, max(1, (nb - 1).bit_length()))
    return factor, inverse


def shards(front, child_update, child_map):
    wide_count = lax.axis_size(WIDE)
    narrow_count = lax.axis_size("narrow")
    wide_index = lax.axis_index(WIDE)
    narrow_index = lax.axis_index("narrow")
    half_count = wide_count // 2
    local_rows, local_cols = front.shape
    front_slots = local_rows // BS
    block_total = front_slots * wide_count
    child_side = wide_index // half_count
    row_local = jnp.arange(local_rows, dtype=jnp.int32)
    global_row = (row_local // BS * wide_count + wide_index) * BS + row_local % BS
    col_local = jnp.arange(local_cols, dtype=jnp.int32)
    global_col = (col_local // PW * narrow_count + narrow_index) * PW + col_local % PW
    child_names = lax.dynamic_slice_in_dim(child_map, child_side * block_total, block_total)
    named_cols = jnp.any(child_names[:, None] == (global_col // BS)[None, :], axis=0)
    groups = child_update.reshape(2, front_slots, BS, local_cols)
    groups = jnp.where(named_cols[None, None, None, :], groups, jnp.zeros_like(groups))
    kept_rows = lax.dynamic_index_in_dim(groups, child_side, 0, keepdims=False)
    leaving = lax.dynamic_index_in_dim(groups, 1 - child_side, 0, keepdims=False)
    arrived = from_partner(leaving, WIDE, half_count.bit_length() - 1)
    partner = (wide_index + half_count) % wide_count
    own_map = lax.dynamic_slice_in_dim(
        child_map, (wide_index * 2 + child_side) * front_slots, front_slots
    )
    got_map = lax.dynamic_slice_in_dim(
        child_map, (partner * 2 + child_side) * front_slots, front_slots
    )
    target = wide_index + wide_count * jnp.arange(front_slots, dtype=jnp.int32)
    own_select = (own_map[None, :] == target[:, None]).astype(jnp.float32)
    got_select = (got_map[None, :] == target[:, None]).astype(jnp.float32)
    own_part = jnp.dot(
        own_select,
        kept_rows.reshape(front_slots, BS * local_cols),
        precision=HIGHEST_PRECISION,
        preferred_element_type=jnp.float32,
    )
    got_part = jnp.dot(
        got_select,
        arrived.reshape(front_slots, BS * local_cols),
        precision=HIGHEST_PRECISION,
        preferred_element_type=jnp.float32,
    )
    matrix = front + (own_part + got_part).reshape(local_rows, local_cols)

    panel, blocks = broadcast(matrix)
    diag_block = blocks[: N_BLOCKS // 2].reshape(PW, PW)
    col_rows = blocks[N_BLOCKS // 2 :].reshape(PW, PW)

    factor_diag, inverse = cholesky_and_inverse(diag_block)
    own_factor = mm_t(panel, inverse)
    diag_rows = lax.dynamic_slice_in_dim(factor_diag, jnp.minimum(wide_index, 3) * BS, BS)
    top = jnp.where(wide_index * BS < PW, diag_rows, own_factor[:BS])
    own_factor = jnp.concatenate([top, own_factor[BS:]], 0)
    col_factor = mm_t(col_rows, inverse)
    update = mm_t(own_factor, col_factor)
    renewed = jnp.where(narrow_index == 0, own_factor, matrix - update)
    on_or_below = global_row[:, None] >= global_col[None, :]
    return jnp.where(on_or_below, renewed, jnp.zeros_like(renewed))


def solution(mesh):
    torus = Mesh(
        mesh.devices.reshape(8, 4, 2, mesh.shape["narrow"]),
        AXES,
    )
    placed = (P(WIDE, "narrow"), P(WIDE, "narrow"), P())
    return jax.shard_map(
        shards, mesh=torus, in_specs=placed, out_specs=P(WIDE, "narrow"), check_vma=False
    )
```

```python
import functools

import jax
import jax.numpy as jnp
from jax import lax
from jax.experimental import pallas as pl
from jax.experimental.pallas import tpu as pltpu
from jax.sharding import Mesh
from jax.sharding import PartitionSpec as P

BS = 128
PW = 512
WIDE = ("wide_0", "wide_1", "wide_2")
AXES = ("wide_0", "wide_1", "wide_2", "narrow")
MESH_ID = pl.DeviceIdType.MESH

HIGHEST_PRECISION = lax.Precision.HIGHEST


def from_partner(value, axis, distance):
    return lax.ppermute(value, axis, [(i, i ^ 1 << distance) for i in range(lax.axis_size(axis))])


def positions():
    return tuple(lax.axis_index(a) for a in AXES)


def narrow_tree(q, n):
    even = q % 2 == 0
    parent = jnp.where(even, q - 2, q - 1)
    kids = [(even, q + 1), (jnp.logical_and(even, q + 2 < n), q + 2)]
    return q > 0, parent, kids


def wide_tree(y, x, h, root, ny, nx):
    y0 = root // (2 * nx)
    x0 = (root // 2) % nx
    h0 = root % 2
    dy = (y - y0 + ny) % ny
    dx = (x - x0 + nx) % nx
    dh = (h - h0 + 2) % 2
    half = ny // 2
    at_y0 = dy == 0
    at_x0 = jnp.logical_and(at_y0, dx == 0)
    is_root = jnp.logical_and(at_x0, dh == 0)
    up = jnp.logical_and(dy >= 1, dy <= half)
    py = jnp.where(up, (y + ny - 1) % ny, (y + 1) % ny)
    px = jnp.where(dx == 2, (x + nx - 1) % nx, x0)
    parent_y = jnp.where(at_y0, y, py)
    parent_x = jnp.where(jnp.logical_and(at_y0, dx != 0), px, x)
    parent_h = jnp.where(at_x0, h0, h)
    parent = (parent_y, parent_x, parent_h)
    kids = [
        (is_root, (y, x, 1 - h)),
        (at_x0, (y, (x + 1) % nx, h)),
        (at_x0, (y, (x + nx - 1) % nx, h)),
        (jnp.logical_and(at_y0, dx == 1), (y, (x + 1) % nx, h)),
        (dy < half, ((y + 1) % ny, x, h)),
        (jnp.logical_or(at_y0, dy > half + 1), ((y + ny - 1) % ny, x, h)),
    ]
    x_depth = jnp.where(dx == 0, 0, jnp.where(dx == 2, 2, 1))
    y_depth = jnp.where(dy <= half, dy, ny - dy)
    return is_root, parent, kids, dh + x_depth + y_depth


N_CHUNKS = 4
N_BLOCKS = 8
N_SLOTS = 7
MAX_DEPTH = 9
NARROW_LAG = 2


def bcast_kernel(src_ref, panel_ref, blocks_ref, nsend, nrecv, wsend, wrecv):
    y, x, h, q = positions()
    n = lax.axis_size("narrow")
    ny = lax.axis_size("wide_0")
    nx = lax.axis_size("wide_1")
    rows = panel_ref.shape[0] // N_CHUNKS
    even = q % 2 == 0
    n_has_parent, n_parent, n_kids = narrow_tree(q, n)

    trees = []
    for j in range(N_BLOCKS):
        if j < N_BLOCKS // 2:
            is_root, parent, kids, depth = wide_tree(y, x, h, j, ny, nx)
            active = q >= 0
            parent = tuple(jnp.where(even, p, o) for p, o in zip((*parent, q), (y, x, h, q - 1)))
            kids = [(jnp.logical_and(even, c), (*k, q)) for c, k in kids]
            kids.append((even, (y, x, h, q + 1)))
            is_root = jnp.logical_and(even, is_root)
            depth = depth + 1 - even.astype(jnp.int32)
        else:
            root = 4 * q + (j - N_BLOCKS // 2)
            is_root, parent, kids, depth = wide_tree(y, x, h, root, ny, nx)
            active = q > 0
            parent = (*parent, q)
            kids = [(c, (*k, q)) for c, k in kids]
            kids.append((q < 0, (y, x, h, q)))
        trees.append((active, is_root, parent, kids, depth))

    barrier = pltpu.get_barrier_semaphore()

    @pl.when(n_has_parent)
    def _():
        pl.semaphore_signal(barrier, 1, device_id=(y, x, h, n_parent), device_id_type=MESH_ID)

    peers = n_has_parent.astype(jnp.int32)
    for cond, kid in n_kids:
        peers = peers + cond.astype(jnp.int32)

        @pl.when(cond)
        def _():
            pl.semaphore_signal(barrier, 1, device_id=(y, x, h, kid), device_id_type=MESH_ID)

    for active, is_root, parent, kids, depth in trees:
        has_parent = jnp.logical_and(active, jnp.logical_not(is_root))
        peers = peers + has_parent.astype(jnp.int32)

        @pl.when(has_parent)
        def _():
            pl.semaphore_signal(barrier, 1, device_id=parent, device_id_type=MESH_ID)

        for cond, kid in kids:
            go = jnp.logical_and(active, cond)
            peers = peers + go.astype(jnp.int32)

            @pl.when(go)
            def _():
                pl.semaphore_signal(barrier, 1, device_id=kid, device_id_type=MESH_ID)

    pl.semaphore_wait(barrier, peers)

    def narrow_copy(src, c, k, kid):
        part = pl.ds(c * rows, rows)
        return pltpu.make_async_remote_copy(
            src_ref=src.at[part],
            dst_ref=panel_ref.at[part],
            send_sem=nsend.at[c, k],
            recv_sem=nrecv.at[c],
            device_id=(y, x, h, kid),
            device_id_type=MESH_ID,
        )

    def narrow_step(c):
        @pl.when(n_has_parent)
        def _():
            narrow_copy(panel_ref, c, 0, q).wait_recv()

        for k, (cond, kid) in enumerate(n_kids):
            @pl.when(jnp.logical_and(cond, q == 0))
            def _():
                narrow_copy(src_ref, c, k, kid).start()

            @pl.when(jnp.logical_and(cond, q != 0))
            def _():
                narrow_copy(panel_ref, c, k, kid).start()

    def wide_copy(src, j, k, kid):
        return pltpu.make_async_remote_copy(
            src_ref=src,
            dst_ref=blocks_ref.at[j],
            send_sem=wsend.at[j, k],
            recv_sem=wrecv.at[j],
            device_id=kid,
            device_id_type=MESH_ID,
        )

    @pl.when(q == 0)
    def _():
        for c in range(N_CHUNKS):
            narrow_step(c)
        panel_ref[...] = src_ref[...]

    @pl.when(q != 0)
    def _():
        narrow_step(0)

    for j, (active, is_root, parent, kids, depth) in enumerate(trees):
        root_here = jnp.logical_and(active, is_root)
        for k, (cond, kid) in enumerate(kids):
            @pl.when(jnp.logical_and(jnp.logical_and(root_here, cond), q == 0))
            def _():
                wide_copy(src_ref.at[pl.ds(0, rows)], j, k, kid).start()

            @pl.when(jnp.logical_and(jnp.logical_and(root_here, cond), q != 0))
            def _():
                wide_copy(panel_ref.at[pl.ds(0, rows)], j, k, kid).start()

        @pl.when(jnp.logical_and(root_here, q == 0))
        def _():
            blocks_ref[j] = src_ref[pl.ds(0, rows)]

        @pl.when(jnp.logical_and(root_here, q != 0))
        def _():
            blocks_ref[j] = panel_ref[pl.ds(0, rows)]

    for level in range(1, MAX_DEPTH):
        for j, (active, is_root, parent, kids, depth) in enumerate(trees):
            here = jnp.logical_and(active, depth == level)

            @pl.when(here)
            def _():
                wide_copy(blocks_ref.at[j], j, 0, (y, x, h, q)).wait_recv()

            for k, (cond, kid) in enumerate(kids):
                @pl.when(jnp.logical_and(here, cond))
                def _():
                    wide_copy(blocks_ref.at[j], j, k, kid).start()

        c = level - NARROW_LAG
        if 1 <= c < N_CHUNKS:
            @pl.when(q != 0)
            def _():
                narrow_step(c)

    for c in range(N_CHUNKS):
        for k, (cond, kid) in enumerate(n_kids):
            @pl.when(cond)
            def _():
                narrow_copy(panel_ref, c, k, kid).wait_send()

    for j, (active, is_root, parent, kids, depth) in enumerate(trees):
        for k, (cond, kid) in enumerate(kids):
            @pl.when(jnp.logical_and(active, cond))
            def _():
                wide_copy(blocks_ref.at[j], j, k, kid).wait_send()


def broadcast(panel):
    rows = panel.shape[0] // N_CHUNKS
    vmem = pl.BlockSpec(memory_space=pltpu.VMEM)
    return pl.pallas_call(
        bcast_kernel,
        out_shape=(
            jax.ShapeDtypeStruct(panel.shape, panel.dtype),
            jax.ShapeDtypeStruct((N_BLOCKS, rows, panel.shape[1]), panel.dtype),
        ),
        in_specs=[vmem],
        out_specs=(vmem, vmem),
        scratch_shapes=[
            pltpu.SemaphoreType.DMA((N_CHUNKS, 2)),
            pltpu.SemaphoreType.DMA((N_CHUNKS,)),
            pltpu.SemaphoreType.DMA((N_BLOCKS, N_SLOTS)),
            pltpu.SemaphoreType.DMA((N_BLOCKS,)),
        ],
        compiler_params=pltpu.CompilerParams(collective_id=0, has_side_effects=True),
    )(panel)


def mm_t(a, b):
    return lax.dot_general(
        a, b, (((1,), (1,)), ((), ())),
        precision=HIGHEST_PRECISION, preferred_element_type=jnp.float32,
    )


def mm(a, b):
    return jnp.dot(a, b, precision=HIGHEST_PRECISION, preferred_element_type=jnp.float32)


def newton_inverse(lower, start, steps):
    inverse = start
    for _ in range(steps):
        inverse = 2 * inverse - mm(inverse, mm(lower, inverse))
    return inverse


def diagonal_inverse(lower):
    n = lower.shape[0]
    on_diag = lax.broadcasted_iota(jnp.int32, (n, n), 0) == lax.broadcasted_iota(jnp.int32, (n, n), 1)
    diag = jnp.sum(jnp.where(on_diag, lower, 0.0), axis=1, keepdims=True)
    return jnp.where(on_diag, 1.0 / diag, 0.0)


def cholesky_and_inverse(symmetric):
    n = symmetric.shape[0]
    nb = n // BS
    work = symmetric
    cols = []
    block_inverses = []
    for b in range(nb):
        head = work[:BS, :BS]
        diag = jnp.tril(jnp.linalg.cholesky(head, symmetrize_input=False))
        inv = newton_inverse(diag, diagonal_inverse(diag), (BS - 1).bit_length())
        block_inverses.append(inv)
        if b + 1 < nb:
            below = mm_t(work[BS:, :BS], inv)
            work = work[BS:, BS:] - mm_t(below, below)
            cols.append(jnp.concatenate([jnp.zeros((b * BS, BS), jnp.float32), diag, below], 0))
        else:
            cols.append(jnp.concatenate([jnp.zeros((b * BS, BS), jnp.float32), diag], 0))
    factor = jnp.concatenate(cols, 1)
    start = jnp.zeros((n, n), jnp.float32)
    for b in range(nb):
        start = lax.dynamic_update_slice(start, block_inverses[b], (b * BS, b * BS))
    inverse = newton_inverse(factor, start, max(1, (nb - 1).bit_length()))
    return factor, inverse


def shards(front, child_update, child_map):
    wide_count = lax.axis_size(WIDE)
    narrow_count = lax.axis_size("narrow")
    wide_index = lax.axis_index(WIDE)
    narrow_index = lax.axis_index("narrow")
    half_count = wide_count // 2
    local_rows, local_cols = front.shape
    front_slots = local_rows // BS
    block_total = front_slots * wide_count
    child_side = wide_index // half_count
    row_local = jnp.arange(local_rows, dtype=jnp.int32)
    global_row = (row_local // BS * wide_count + wide_index) * BS + row_local % BS
    col_local = jnp.arange(local_cols, dtype=jnp.int32)
    global_col = (col_local // PW * narrow_count + narrow_index) * PW + col_local % PW
    groups = child_update.reshape(2, front_slots, BS, local_cols)
    leaving = lax.dynamic_index_in_dim(groups, 1 - child_side, 0, keepdims=False)
    arrived = from_partner(leaving, WIDE, half_count.bit_length() - 1)

    def named_cols(side):
        names = lax.dynamic_slice_in_dim(child_map, side * block_total, block_total)
        return jnp.any(names[:, None] == (global_col // BS)[None, :], axis=0)

    kept_rows = lax.dynamic_index_in_dim(groups, child_side, 0, keepdims=False)
    kept_rows = jnp.where(named_cols(child_side)[None, None, :], kept_rows, 0.0)
    arrived = jnp.where(named_cols(1 - child_side)[None, None, :], arrived, 0.0)
    partner = (wide_index + half_count) % wide_count
    own_map = lax.dynamic_slice_in_dim(
        child_map, (wide_index * 2 + child_side) * front_slots, front_slots
    )
    got_map = lax.dynamic_slice_in_dim(
        child_map, (partner * 2 + child_side) * front_slots, front_slots
    )
    target = wide_index + wide_count * jnp.arange(front_slots, dtype=jnp.int32)
    own_select = (own_map[None, :] == target[:, None]).astype(jnp.float32)
    got_select = (got_map[None, :] == target[:, None]).astype(jnp.float32)
    own_part = jnp.dot(
        own_select,
        kept_rows.reshape(front_slots, BS * local_cols),
        precision=HIGHEST_PRECISION,
        preferred_element_type=jnp.float32,
    )
    got_part = jnp.dot(
        got_select,
        arrived.reshape(front_slots, BS * local_cols),
        precision=HIGHEST_PRECISION,
        preferred_element_type=jnp.float32,
    )
    matrix = front + (own_part + got_part).reshape(local_rows, local_cols)

    panel, blocks = broadcast(matrix)
    diag_block = blocks[: N_BLOCKS // 2].reshape(PW, PW)
    col_rows = blocks[N_BLOCKS // 2 :].reshape(PW, PW)

    factor_diag, inverse = cholesky_and_inverse(diag_block)
    own_factor = mm_t(panel, inverse)
    diag_rows = lax.dynamic_slice_in_dim(factor_diag, jnp.minimum(wide_index, 3) * BS, BS)
    top = jnp.where(wide_index * BS < PW, diag_rows, own_factor[:BS])
    own_factor = jnp.concatenate([top, own_factor[BS:]], 0)
    col_factor = mm_t(col_rows, inverse)
    update = mm_t(own_factor, col_factor)
    renewed = jnp.where(narrow_index == 0, own_factor, matrix - update)
    on_or_below = global_row[:, None] >= global_col[None, :]
    return jnp.where(on_or_below, renewed, jnp.zeros_like(renewed))


def solution(mesh):
    torus = Mesh(
        mesh.devices.reshape(8, 4, 2, mesh.shape["narrow"]),
        AXES,
    )
    placed = (P(WIDE, "narrow"), P(WIDE, "narrow"), P())
    return jax.shard_map(
        shards, mesh=torus, in_specs=placed, out_specs=P(WIDE, "narrow"), check_vma=False
    )
```

```python
import functools

import jax
import jax.numpy as jnp
from jax import lax
from jax.experimental import pallas as pl
from jax.experimental.pallas import tpu as pltpu
from jax.sharding import Mesh
from jax.sharding import PartitionSpec as P

BS = 128
PW = 512
WIDE = ("wide_0", "wide_1", "wide_2")
AXES = ("wide_0", "wide_1", "wide_2", "narrow")
MESH_ID = pl.DeviceIdType.MESH

HIGHEST_PRECISION = lax.Precision.HIGHEST


def from_partner(value, axis, distance):
    return lax.ppermute(value, axis, [(i, i ^ 1 << distance) for i in range(lax.axis_size(axis))])


def positions():
    return tuple(lax.axis_index(a) for a in AXES)


def narrow_tree(q, n):
    even = q % 2 == 0
    parent = jnp.where(even, q - 2, q - 1)
    kids = [(even, q + 1), (jnp.logical_and(even, q + 2 < n), q + 2)]
    return q > 0, parent, kids


def wide_tree(y, x, h, root, ny, nx):
    y0 = root // (2 * nx)
    x0 = (root // 2) % nx
    h0 = root % 2
    dy = (y - y0 + ny) % ny
    dx = (x - x0 + nx) % nx
    dh = (h - h0 + 2) % 2
    half = ny // 2
    at_y0 = dy == 0
    at_x0 = jnp.logical_and(at_y0, dx == 0)
    is_root = jnp.logical_and(at_x0, dh == 0)
    up = jnp.logical_and(dy >= 1, dy <= half)
    py = jnp.where(up, (y + ny - 1) % ny, (y + 1) % ny)
    px = jnp.where(dx == 2, (x + nx - 1) % nx, x0)
    parent_y = jnp.where(at_y0, y, py)
    parent_x = jnp.where(jnp.logical_and(at_y0, dx != 0), px, x)
    parent_h = jnp.where(at_x0, h0, h)
    parent = (parent_y, parent_x, parent_h)
    kids = [
        (is_root, (y, x, 1 - h)),
        (at_x0, (y, (x + 1) % nx, h)),
        (at_x0, (y, (x + nx - 1) % nx, h)),
        (jnp.logical_and(at_y0, dx == 1), (y, (x + 1) % nx, h)),
        (dy < half, ((y + 1) % ny, x, h)),
        (jnp.logical_or(at_y0, dy > half + 1), ((y + ny - 1) % ny, x, h)),
    ]
    x_depth = jnp.where(dx == 0, 0, jnp.where(dx == 2, 2, 1))
    y_depth = jnp.where(dy <= half, dy, ny - dy)
    return is_root, parent, kids, dh + x_depth + y_depth


N_CHUNKS = 4
N_BLOCKS = 8
N_SLOTS = 7
MAX_DEPTH = 9
NARROW_LAG = 2


def bcast_kernel(src_ref, panel_ref, blocks_ref, nsend, nrecv, wsend, wrecv):
    y, x, h, q = positions()
    n = lax.axis_size("narrow")
    ny = lax.axis_size("wide_0")
    nx = lax.axis_size("wide_1")
    rows = panel_ref.shape[0] // N_CHUNKS
    even = q % 2 == 0
    n_has_parent, n_parent, n_kids = narrow_tree(q, n)

    trees = []
    for j in range(N_BLOCKS):
        if j < N_BLOCKS // 2:
            is_root, parent, kids, depth = wide_tree(y, x, h, j, ny, nx)
            active = q >= 0
            parent = tuple(jnp.where(even, p, o) for p, o in zip((*parent, q), (y, x, h, q - 1)))
            kids = [(jnp.logical_and(even, c), (*k, q)) for c, k in kids]
            kids.append((even, (y, x, h, q + 1)))
            is_root = jnp.logical_and(even, is_root)
            depth = depth + 1 - even.astype(jnp.int32)
        else:
            root = 4 * q + (j - N_BLOCKS // 2)
            is_root, parent, kids, depth = wide_tree(y, x, h, root, ny, nx)
            active = q > 0
            parent = (*parent, q)
            kids = [(c, (*k, q)) for c, k in kids]
            kids.append((q < 0, (y, x, h, q)))
        trees.append((active, is_root, parent, kids, depth))

    barrier = pltpu.get_barrier_semaphore()

    @pl.when(n_has_parent)
    def _():
        pl.semaphore_signal(barrier, 1, device_id=(y, x, h, n_parent), device_id_type=MESH_ID)

    peers = n_has_parent.astype(jnp.int32)
    for cond, kid in n_kids:
        peers = peers + cond.astype(jnp.int32)

        @pl.when(cond)
        def _():
            pl.semaphore_signal(barrier, 1, device_id=(y, x, h, kid), device_id_type=MESH_ID)

    for active, is_root, parent, kids, depth in trees:
        has_parent = jnp.logical_and(active, jnp.logical_not(is_root))
        peers = peers + has_parent.astype(jnp.int32)

        @pl.when(has_parent)
        def _():
            pl.semaphore_signal(barrier, 1, device_id=parent, device_id_type=MESH_ID)

        for cond, kid in kids:
            go = jnp.logical_and(active, cond)
            peers = peers + go.astype(jnp.int32)

            @pl.when(go)
            def _():
                pl.semaphore_signal(barrier, 1, device_id=kid, device_id_type=MESH_ID)

    pl.semaphore_wait(barrier, peers)

    def narrow_copy(src, c, k, kid):
        part = pl.ds(c * rows, rows)
        return pltpu.make_async_remote_copy(
            src_ref=src.at[part],
            dst_ref=panel_ref.at[part],
            send_sem=nsend.at[c, k],
            recv_sem=nrecv.at[c],
            device_id=(y, x, h, kid),
            device_id_type=MESH_ID,
        )

    def narrow_step(c):
        @pl.when(n_has_parent)
        def _():
            narrow_copy(panel_ref, c, 0, q).wait_recv()

        for k, (cond, kid) in enumerate(n_kids):
            @pl.when(jnp.logical_and(cond, q == 0))
            def _():
                narrow_copy(src_ref, c, k, kid).start()

            @pl.when(jnp.logical_and(cond, q != 0))
            def _():
                narrow_copy(panel_ref, c, k, kid).start()

    def wide_copy(src, j, k, kid):
        if j < N_BLOCKS // 2:
            cols = pl.ds(0, (j + 1) * rows)
            src, dst = src.at[:, cols], blocks_ref.at[j, :, cols]
        else:
            dst = blocks_ref.at[j]
        return pltpu.make_async_remote_copy(
            src_ref=src,
            dst_ref=dst,
            send_sem=wsend.at[j, k],
            recv_sem=wrecv.at[j],
            device_id=kid,
            device_id_type=MESH_ID,
        )

    @pl.when(q == 0)
    def _():
        for c in range(N_CHUNKS):
            narrow_step(c)
        panel_ref[...] = src_ref[...]

    @pl.when(q != 0)
    def _():
        narrow_step(0)

    for j, (active, is_root, parent, kids, depth) in enumerate(trees):
        root_here = jnp.logical_and(active, is_root)
        for k, (cond, kid) in enumerate(kids):
            @pl.when(jnp.logical_and(jnp.logical_and(root_here, cond), q == 0))
            def _():
                wide_copy(src_ref.at[pl.ds(0, rows)], j, k, kid).start()

            @pl.when(jnp.logical_and(jnp.logical_and(root_here, cond), q != 0))
            def _():
                wide_copy(panel_ref.at[pl.ds(0, rows)], j, k, kid).start()

        @pl.when(jnp.logical_and(root_here, q == 0))
        def _():
            blocks_ref[j] = src_ref[pl.ds(0, rows)]

        @pl.when(jnp.logical_and(root_here, q != 0))
        def _():
            blocks_ref[j] = panel_ref[pl.ds(0, rows)]

    for level in range(1, MAX_DEPTH):
        for j, (active, is_root, parent, kids, depth) in enumerate(trees):
            here = jnp.logical_and(active, depth == level)

            @pl.when(here)
            def _():
                wide_copy(blocks_ref.at[j], j, 0, (y, x, h, q)).wait_recv()

            for k, (cond, kid) in enumerate(kids):
                @pl.when(jnp.logical_and(here, cond))
                def _():
                    wide_copy(blocks_ref.at[j], j, k, kid).start()

        c = level - NARROW_LAG
        if 1 <= c < N_CHUNKS:
            @pl.when(q != 0)
            def _():
                narrow_step(c)

    for c in range(N_CHUNKS):
        for k, (cond, kid) in enumerate(n_kids):
            @pl.when(cond)
            def _():
                narrow_copy(panel_ref, c, k, kid).wait_send()

    for j, (active, is_root, parent, kids, depth) in enumerate(trees):
        for k, (cond, kid) in enumerate(kids):
            @pl.when(jnp.logical_and(active, cond))
            def _():
                wide_copy(blocks_ref.at[j], j, k, kid).wait_send()


def broadcast(panel):
    rows = panel.shape[0] // N_CHUNKS
    vmem = pl.BlockSpec(memory_space=pltpu.VMEM)
    return pl.pallas_call(
        bcast_kernel,
        out_shape=(
            jax.ShapeDtypeStruct(panel.shape, panel.dtype),
            jax.ShapeDtypeStruct((N_BLOCKS, rows, panel.shape[1]), panel.dtype),
        ),
        in_specs=[vmem],
        out_specs=(vmem, vmem),
        scratch_shapes=[
            pltpu.SemaphoreType.DMA((N_CHUNKS, 2)),
            pltpu.SemaphoreType.DMA((N_CHUNKS,)),
            pltpu.SemaphoreType.DMA((N_BLOCKS, N_SLOTS)),
            pltpu.SemaphoreType.DMA((N_BLOCKS,)),
        ],
        compiler_params=pltpu.CompilerParams(collective_id=0, has_side_effects=True),
    )(panel)


def mm_t(a, b):
    return lax.dot_general(
        a, b, (((1,), (1,)), ((), ())),
        precision=HIGHEST_PRECISION, preferred_element_type=jnp.float32,
    )


def mm(a, b):
    return jnp.dot(a, b, precision=HIGHEST_PRECISION, preferred_element_type=jnp.float32)


def newton_inverse(lower, start, steps):
    inverse = start
    for _ in range(steps):
        inverse = 2 * inverse - mm(inverse, mm(lower, inverse))
    return inverse


def diagonal_inverse(lower):
    n = lower.shape[0]
    on_diag = lax.broadcasted_iota(jnp.int32, (n, n), 0) == lax.broadcasted_iota(jnp.int32, (n, n), 1)
    diag = jnp.sum(jnp.where(on_diag, lower, 0.0), axis=1, keepdims=True)
    return jnp.where(on_diag, 1.0 / diag, 0.0)


def cholesky_and_inverse(symmetric):
    n = symmetric.shape[0]
    nb = n // BS
    work = symmetric
    cols = []
    block_inverses = []
    for b in range(nb):
        head = work[:BS, :BS]
        diag = jnp.tril(jnp.linalg.cholesky(head, symmetrize_input=False))
        inv = newton_inverse(diag, diagonal_inverse(diag), (BS - 1).bit_length())
        block_inverses.append(inv)
        if b + 1 < nb:
            below = mm_t(work[BS:, :BS], inv)
            work = work[BS:, BS:] - mm_t(below, below)
            cols.append(jnp.concatenate([jnp.zeros((b * BS, BS), jnp.float32), diag, below], 0))
        else:
            cols.append(jnp.concatenate([jnp.zeros((b * BS, BS), jnp.float32), diag], 0))
    factor = jnp.concatenate(cols, 1)
    start = jnp.zeros((n, n), jnp.float32)
    for b in range(nb):
        start = lax.dynamic_update_slice(start, block_inverses[b], (b * BS, b * BS))
    inverse = newton_inverse(factor, start, max(1, (nb - 1).bit_length()))
    return factor, inverse


def shards(front, child_update, child_map):
    wide_count = lax.axis_size(WIDE)
    narrow_count = lax.axis_size("narrow")
    wide_index = lax.axis_index(WIDE)
    narrow_index = lax.axis_index("narrow")
    half_count = wide_count // 2
    local_rows, local_cols = front.shape
    front_slots = local_rows // BS
    block_total = front_slots * wide_count
    child_side = wide_index // half_count
    row_local = jnp.arange(local_rows, dtype=jnp.int32)
    global_row = (row_local // BS * wide_count + wide_index) * BS + row_local % BS
    col_local = jnp.arange(local_cols, dtype=jnp.int32)
    global_col = (col_local // PW * narrow_count + narrow_index) * PW + col_local % PW
    groups = child_update.reshape(2, front_slots, BS, local_cols)
    leaving = lax.dynamic_index_in_dim(groups, 1 - child_side, 0, keepdims=False)
    arrived = from_partner(leaving, WIDE, half_count.bit_length() - 1)

    def named_cols(side):
        names = lax.dynamic_slice_in_dim(child_map, side * block_total, block_total)
        return jnp.any(names[:, None] == (global_col // BS)[None, :], axis=0)

    kept_rows = lax.dynamic_index_in_dim(groups, child_side, 0, keepdims=False)
    kept_rows = jnp.where(named_cols(child_side)[None, None, :], kept_rows, 0.0)
    arrived = jnp.where(named_cols(1 - child_side)[None, None, :], arrived, 0.0)
    partner = (wide_index + half_count) % wide_count
    own_map = lax.dynamic_slice_in_dim(
        child_map, (wide_index * 2 + child_side) * front_slots, front_slots
    )
    got_map = lax.dynamic_slice_in_dim(
        child_map, (partner * 2 + child_side) * front_slots, front_slots
    )
    target = wide_index + wide_count * jnp.arange(front_slots, dtype=jnp.int32)
    own_select = (own_map[None, :] == target[:, None]).astype(jnp.float32)
    got_select = (got_map[None, :] == target[:, None]).astype(jnp.float32)
    own_part = jnp.dot(
        own_select,
        kept_rows.reshape(front_slots, BS * local_cols),
        precision=HIGHEST_PRECISION,
        preferred_element_type=jnp.float32,
    )
    got_part = jnp.dot(
        got_select,
        arrived.reshape(front_slots, BS * local_cols),
        precision=HIGHEST_PRECISION,
        preferred_element_type=jnp.float32,
    )
    matrix = front + (own_part + got_part).reshape(local_rows, local_cols)

    panel, blocks = broadcast(matrix)
    diag_block = blocks[: N_BLOCKS // 2].reshape(PW, PW)
    diag_block = jnp.where(
        lax.broadcasted_iota(jnp.int32, (PW, PW), 1) < (lax.broadcasted_iota(jnp.int32, (PW, PW), 0) // BS + 1) * BS,
        diag_block,
        0.0,
    )
    col_rows = blocks[N_BLOCKS // 2 :].reshape(PW, PW)

    factor_diag, inverse = cholesky_and_inverse(diag_block)
    own_factor = mm_t(panel, inverse)
    diag_rows = lax.dynamic_slice_in_dim(factor_diag, jnp.minimum(wide_index, 3) * BS, BS)
    top = jnp.where(wide_index * BS < PW, diag_rows, own_factor[:BS])
    own_factor = jnp.concatenate([top, own_factor[BS:]], 0)
    col_factor = mm_t(col_rows, inverse)
    update = mm_t(own_factor, col_factor)
    renewed = jnp.where(narrow_index == 0, own_factor, matrix - update)
    on_or_below = global_row[:, None] >= global_col[None, :]
    return jnp.where(on_or_below, renewed, jnp.zeros_like(renewed))


def solution(mesh):
    torus = Mesh(
        mesh.devices.reshape(8, 4, 2, mesh.shape["narrow"]),
        AXES,
    )
    placed = (P(WIDE, "narrow"), P(WIDE, "narrow"), P())
    return jax.shard_map(
        shards, mesh=torus, in_specs=placed, out_specs=P(WIDE, "narrow"), check_vma=False
    )
```

```python
import functools

import jax
import jax.numpy as jnp
from jax import lax
from jax.experimental import pallas as pl
from jax.experimental.pallas import tpu as pltpu
from jax.sharding import Mesh
from jax.sharding import PartitionSpec as P

BS = 128
PW = 512
WIDE = ("wide_0", "wide_1", "wide_2")
AXES = ("wide_0", "wide_1", "wide_2", "narrow")
MESH_ID = pl.DeviceIdType.MESH

HIGHEST_PRECISION = lax.Precision.HIGHEST


def from_partner(value, axis, distance):
    return lax.ppermute(value, axis, [(i, i ^ 1 << distance) for i in range(lax.axis_size(axis))])


def positions():
    return tuple(lax.axis_index(a) for a in AXES)


def narrow_tree(q, n):
    even = q % 2 == 0
    parent = jnp.where(even, q - 2, q - 1)
    kids = [(even, q + 1), (jnp.logical_and(even, q + 2 < n), q + 2)]
    return q > 0, parent, kids


def wide_tree(y, x, h, root, ny, nx):
    y0 = root // (2 * nx)
    x0 = (root // 2) % nx
    h0 = root % 2
    dy = (y - y0 + ny) % ny
    dx = (x - x0 + nx) % nx
    dh = (h - h0 + 2) % 2
    half = ny // 2
    at_y0 = dy == 0
    at_x0 = jnp.logical_and(at_y0, dx == 0)
    is_root = jnp.logical_and(at_x0, dh == 0)
    up = jnp.logical_and(dy >= 1, dy <= half)
    py = jnp.where(up, (y + ny - 1) % ny, (y + 1) % ny)
    px = jnp.where(dx == 2, (x + nx - 1) % nx, x0)
    parent_y = jnp.where(at_y0, y, py)
    parent_x = jnp.where(jnp.logical_and(at_y0, dx != 0), px, x)
    parent_h = jnp.where(at_x0, h0, h)
    parent = (parent_y, parent_x, parent_h)
    kids = [
        (is_root, (y, x, 1 - h)),
        (at_x0, (y, (x + 1) % nx, h)),
        (at_x0, (y, (x + nx - 1) % nx, h)),
        (jnp.logical_and(at_y0, dx == 1), (y, (x + 1) % nx, h)),
        (dy < half, ((y + 1) % ny, x, h)),
        (jnp.logical_or(at_y0, dy > half + 1), ((y + ny - 1) % ny, x, h)),
    ]
    x_depth = jnp.where(dx == 0, 0, jnp.where(dx == 2, 2, 1))
    y_depth = jnp.where(dy <= half, dy, ny - dy)
    return is_root, parent, kids, dh + x_depth + y_depth


N_CHUNKS = 4
N_BLOCKS = 8
N_SLOTS = 7
MAX_DEPTH = 9
NARROW_LAG = 2
W_CHUNKS = 2


def bcast_kernel(src_ref, panel_ref, blocks_ref, nsend, nrecv, wsend, wrecv):
    y, x, h, q = positions()
    n = lax.axis_size("narrow")
    ny = lax.axis_size("wide_0")
    nx = lax.axis_size("wide_1")
    rows = panel_ref.shape[0] // N_CHUNKS
    even = q % 2 == 0
    n_has_parent, n_parent, n_kids = narrow_tree(q, n)

    trees = []
    for j in range(N_BLOCKS):
        if j < N_BLOCKS // 2:
            is_root, parent, kids, depth = wide_tree(y, x, h, j, ny, nx)
            active = q >= 0
            parent = tuple(jnp.where(even, p, o) for p, o in zip((*parent, q), (y, x, h, q - 1)))
            kids = [(jnp.logical_and(even, c), (*k, q)) for c, k in kids]
            kids.append((even, (y, x, h, q + 1)))
            is_root = jnp.logical_and(even, is_root)
            depth = depth + 1 - even.astype(jnp.int32)
        else:
            root = 4 * q + (j - N_BLOCKS // 2)
            is_root, parent, kids, depth = wide_tree(y, x, h, root, ny, nx)
            active = q > 0
            parent = (*parent, q)
            kids = [(c, (*k, q)) for c, k in kids]
            kids.append((q < 0, (y, x, h, q)))
        trees.append((active, is_root, parent, kids, depth))

    barrier = pltpu.get_barrier_semaphore()

    @pl.when(n_has_parent)
    def _():
        pl.semaphore_signal(barrier, 1, device_id=(y, x, h, n_parent), device_id_type=MESH_ID)

    peers = n_has_parent.astype(jnp.int32)
    for cond, kid in n_kids:
        peers = peers + cond.astype(jnp.int32)

        @pl.when(cond)
        def _():
            pl.semaphore_signal(barrier, 1, device_id=(y, x, h, kid), device_id_type=MESH_ID)

    for active, is_root, parent, kids, depth in trees:
        has_parent = jnp.logical_and(active, jnp.logical_not(is_root))
        peers = peers + has_parent.astype(jnp.int32)

        @pl.when(has_parent)
        def _():
            pl.semaphore_signal(barrier, 1, device_id=parent, device_id_type=MESH_ID)

        for cond, kid in kids:
            go = jnp.logical_and(active, cond)
            peers = peers + go.astype(jnp.int32)

            @pl.when(go)
            def _():
                pl.semaphore_signal(barrier, 1, device_id=kid, device_id_type=MESH_ID)

    pl.semaphore_wait(barrier, peers)

    def narrow_copy(src, c, k, kid):
        part = pl.ds(c * rows, rows)
        return pltpu.make_async_remote_copy(
            src_ref=src.at[part],
            dst_ref=panel_ref.at[part],
            send_sem=nsend.at[c, k],
            recv_sem=nrecv.at[c],
            device_id=(y, x, h, kid),
            device_id_type=MESH_ID,
        )

    def narrow_step(c):
        @pl.when(n_has_parent)
        def _():
            narrow_copy(panel_ref, c, 0, q).wait_recv()

        for k, (cond, kid) in enumerate(n_kids):
            @pl.when(jnp.logical_and(cond, q == 0))
            def _():
                narrow_copy(src_ref, c, k, kid).start()

            @pl.when(jnp.logical_and(cond, q != 0))
            def _():
                narrow_copy(panel_ref, c, k, kid).start()

    piece = rows // W_CHUNKS

    def wide_copy(src, j, c, k, kid):
        part = pl.ds(c * piece, piece)
        cols = pl.ds(0, (j + 1) * rows if j < N_BLOCKS // 2 else src.shape[1])
        return pltpu.make_async_remote_copy(
            src_ref=src.at[part, cols],
            dst_ref=blocks_ref.at[j, part, cols],
            send_sem=wsend.at[j, c, k],
            recv_sem=wrecv.at[j, c],
            device_id=kid,
            device_id_type=MESH_ID,
        )

    @pl.when(q == 0)
    def _():
        for c in range(N_CHUNKS):
            narrow_step(c)
        panel_ref[...] = src_ref[...]

    @pl.when(q != 0)
    def _():
        narrow_step(0)

    for j, (active, is_root, parent, kids, depth) in enumerate(trees):
        root_here = jnp.logical_and(active, is_root)
        for c in range(W_CHUNKS):
            for k, (cond, kid) in enumerate(kids):
                @pl.when(jnp.logical_and(jnp.logical_and(root_here, cond), q == 0))
                def _():
                    wide_copy(src_ref.at[pl.ds(0, rows)], j, c, k, kid).start()

                @pl.when(jnp.logical_and(jnp.logical_and(root_here, cond), q != 0))
                def _():
                    wide_copy(panel_ref.at[pl.ds(0, rows)], j, c, k, kid).start()

        @pl.when(jnp.logical_and(root_here, q == 0))
        def _():
            blocks_ref[j] = src_ref[pl.ds(0, rows)]

        @pl.when(jnp.logical_and(root_here, q != 0))
        def _():
            blocks_ref[j] = panel_ref[pl.ds(0, rows)]

    for level in range(1, MAX_DEPTH + W_CHUNKS - 1):
        for c in range(W_CHUNKS):
            for j, (active, is_root, parent, kids, depth) in enumerate(trees):
                here = jnp.logical_and(jnp.logical_and(active, jnp.logical_not(is_root)), depth + c == level)

                @pl.when(here)
                def _():
                    wide_copy(blocks_ref.at[j], j, c, 0, (y, x, h, q)).wait_recv()

                for k, (cond, kid) in enumerate(kids):
                    @pl.when(jnp.logical_and(here, cond))
                    def _():
                        wide_copy(blocks_ref.at[j], j, c, k, kid).start()

        c = level - NARROW_LAG
        if 1 <= c < N_CHUNKS:
            @pl.when(q != 0)
            def _():
                narrow_step(c)

    for c in range(N_CHUNKS):
        for k, (cond, kid) in enumerate(n_kids):
            @pl.when(cond)
            def _():
                narrow_copy(panel_ref, c, k, kid).wait_send()

    for j, (active, is_root, parent, kids, depth) in enumerate(trees):
        for c in range(W_CHUNKS):
            for k, (cond, kid) in enumerate(kids):
                @pl.when(jnp.logical_and(active, cond))
                def _():
                    wide_copy(blocks_ref.at[j], j, c, k, kid).wait_send()


def broadcast(panel):
    rows = panel.shape[0] // N_CHUNKS
    vmem = pl.BlockSpec(memory_space=pltpu.VMEM)
    return pl.pallas_call(
        bcast_kernel,
        out_shape=(
            jax.ShapeDtypeStruct(panel.shape, panel.dtype),
            jax.ShapeDtypeStruct((N_BLOCKS, rows, panel.shape[1]), panel.dtype),
        ),
        in_specs=[vmem],
        out_specs=(vmem, vmem),
        scratch_shapes=[
            pltpu.SemaphoreType.DMA((N_CHUNKS, 2)),
            pltpu.SemaphoreType.DMA((N_CHUNKS,)),
            pltpu.SemaphoreType.DMA((N_BLOCKS, W_CHUNKS, N_SLOTS)),
            pltpu.SemaphoreType.DMA((N_BLOCKS, W_CHUNKS)),
        ],
        compiler_params=pltpu.CompilerParams(collective_id=0, has_side_effects=True),
    )(panel)


def mm_t(a, b):
    return lax.dot_general(
        a, b, (((1,), (1,)), ((), ())),
        precision=HIGHEST_PRECISION, preferred_element_type=jnp.float32,
    )


def mm(a, b):
    return jnp.dot(a, b, precision=HIGHEST_PRECISION, preferred_element_type=jnp.float32)


def newton_inverse(lower, start, steps):
    inverse = start
    for _ in range(steps):
        inverse = 2 * inverse - mm(inverse, mm(lower, inverse))
    return inverse


def diagonal_inverse(lower):
    n = lower.shape[0]
    on_diag = lax.broadcasted_iota(jnp.int32, (n, n), 0) == lax.broadcasted_iota(jnp.int32, (n, n), 1)
    diag = jnp.sum(jnp.where(on_diag, lower, 0.0), axis=1, keepdims=True)
    return jnp.where(on_diag, 1.0 / diag, 0.0)


def cholesky_and_inverse(symmetric):
    n = symmetric.shape[0]
    nb = n // BS
    work = symmetric
    cols = []
    block_inverses = []
    for b in range(nb):
        head = work[:BS, :BS]
        diag = jnp.tril(jnp.linalg.cholesky(head, symmetrize_input=False))
        inv = newton_inverse(diag, diagonal_inverse(diag), (BS - 1).bit_length())
        block_inverses.append(inv)
        if b + 1 < nb:
            below = mm_t(work[BS:, :BS], inv)
            work = work[BS:, BS:] - mm_t(below, below)
            cols.append(jnp.concatenate([jnp.zeros((b * BS, BS), jnp.float32), diag, below], 0))
        else:
            cols.append(jnp.concatenate([jnp.zeros((b * BS, BS), jnp.float32), diag], 0))
    factor = jnp.concatenate(cols, 1)
    start = jnp.zeros((n, n), jnp.float32)
    for b in range(nb):
        start = lax.dynamic_update_slice(start, block_inverses[b], (b * BS, b * BS))
    inverse = newton_inverse(factor, start, max(1, (nb - 1).bit_length()))
    return factor, inverse


def shards(front, child_update, child_map):
    wide_count = lax.axis_size(WIDE)
    narrow_count = lax.axis_size("narrow")
    wide_index = lax.axis_index(WIDE)
    narrow_index = lax.axis_index("narrow")
    half_count = wide_count // 2
    local_rows, local_cols = front.shape
    front_slots = local_rows // BS
    block_total = front_slots * wide_count
    child_side = wide_index // half_count
    row_local = jnp.arange(local_rows, dtype=jnp.int32)
    global_row = (row_local // BS * wide_count + wide_index) * BS + row_local % BS
    col_local = jnp.arange(local_cols, dtype=jnp.int32)
    global_col = (col_local // PW * narrow_count + narrow_index) * PW + col_local % PW
    groups = child_update.reshape(2, front_slots, BS, local_cols)
    leaving = lax.dynamic_index_in_dim(groups, 1 - child_side, 0, keepdims=False)
    arrived = from_partner(leaving, WIDE, half_count.bit_length() - 1)

    def named_cols(side):
        names = lax.dynamic_slice_in_dim(child_map, side * block_total, block_total)
        return jnp.any(names[:, None] == (global_col // BS)[None, :], axis=0)

    kept_rows = lax.dynamic_index_in_dim(groups, child_side, 0, keepdims=False)
    kept_rows = jnp.where(named_cols(child_side)[None, None, :], kept_rows, 0.0)
    arrived = jnp.where(named_cols(1 - child_side)[None, None, :], arrived, 0.0)
    partner = (wide_index + half_count) % wide_count
    own_map = lax.dynamic_slice_in_dim(
        child_map, (wide_index * 2 + child_side) * front_slots, front_slots
    )
    got_map = lax.dynamic_slice_in_dim(
        child_map, (partner * 2 + child_side) * front_slots, front_slots
    )
    target = wide_index + wide_count * jnp.arange(front_slots, dtype=jnp.int32)
    own_select = (own_map[None, :] == target[:, None]).astype(jnp.float32)
    got_select = (got_map[None, :] == target[:, None]).astype(jnp.float32)
    own_part = jnp.dot(
        own_select,
        kept_rows.reshape(front_slots, BS * local_cols),
        precision=HIGHEST_PRECISION,
        preferred_element_type=jnp.float32,
    )
    got_part = jnp.dot(
        got_select,
        arrived.reshape(front_slots, BS * local_cols),
        precision=HIGHEST_PRECISION,
        preferred_element_type=jnp.float32,
    )
    matrix = front + (own_part + got_part).reshape(local_rows, local_cols)

    panel, blocks = broadcast(matrix)
    diag_block = blocks[: N_BLOCKS // 2].reshape(PW, PW)
    diag_block = jnp.where(
        lax.broadcasted_iota(jnp.int32, (PW, PW), 1) < (lax.broadcasted_iota(jnp.int32, (PW, PW), 0) // BS + 1) * BS,
        diag_block,
        0.0,
    )
    col_rows = blocks[N_BLOCKS // 2 :].reshape(PW, PW)

    factor_diag, inverse = cholesky_and_inverse(diag_block)
    own_factor = mm_t(panel, inverse)
    diag_rows = lax.dynamic_slice_in_dim(factor_diag, jnp.minimum(wide_index, 3) * BS, BS)
    top = jnp.where(wide_index * BS < PW, diag_rows, own_factor[:BS])
    own_factor = jnp.concatenate([top, own_factor[BS:]], 0)
    col_factor = mm_t(col_rows, inverse)
    update = mm_t(own_factor, col_factor)
    renewed = jnp.where(narrow_index == 0, own_factor, matrix - update)
    on_or_below = global_row[:, None] >= global_col[None, :]
    return jnp.where(on_or_below, renewed, jnp.zeros_like(renewed))


def solution(mesh):
    torus = Mesh(
        mesh.devices.reshape(8, 4, 2, mesh.shape["narrow"]),
        AXES,
    )
    placed = (P(WIDE, "narrow"), P(WIDE, "narrow"), P())
    return jax.shard_map(
        shards, mesh=torus, in_specs=placed, out_specs=P(WIDE, "narrow"), check_vma=False
    )
```

```python
import functools

import jax
import jax.numpy as jnp
from jax import lax
from jax.experimental import pallas as pl
from jax.experimental.pallas import tpu as pltpu
from jax.sharding import Mesh
from jax.sharding import PartitionSpec as P

BS = 128
PW = 512
WIDE = ("wide_0", "wide_1", "wide_2")
AXES = ("wide_0", "wide_1", "wide_2", "narrow")
MESH_ID = pl.DeviceIdType.MESH

HIGHEST_PRECISION = lax.Precision.HIGHEST


def from_partner(value, axis, distance):
    return lax.ppermute(value, axis, [(i, i ^ 1 << distance) for i in range(lax.axis_size(axis))])


def positions():
    return tuple(lax.axis_index(a) for a in AXES)


def narrow_tree(q, n):
    even = q % 2 == 0
    parent = jnp.where(even, q - 2, q - 1)
    kids = [(even, q + 1), (jnp.logical_and(even, q + 2 < n), q + 2)]
    return q > 0, parent, kids


def wide_tree(y, x, h, root, ny, nx):
    y0 = root // (2 * nx)
    x0 = (root // 2) % nx
    h0 = root % 2
    dy = (y - y0 + ny) % ny
    dx = (x - x0 + nx) % nx
    dh = (h - h0 + 2) % 2
    half = ny // 2
    at_y0 = dy == 0
    at_x0 = jnp.logical_and(at_y0, dx == 0)
    is_root = jnp.logical_and(at_x0, dh == 0)
    up = jnp.logical_and(dy >= 1, dy <= half)
    py = jnp.where(up, (y + ny - 1) % ny, (y + 1) % ny)
    px = jnp.where(dx == 2, (x + nx - 1) % nx, x0)
    parent_y = jnp.where(at_y0, y, py)
    parent_x = jnp.where(jnp.logical_and(at_y0, dx != 0), px, x)
    parent_h = jnp.where(at_x0, h0, h)
    parent = (parent_y, parent_x, parent_h)
    kids = [
        (is_root, (y, x, 1 - h)),
        (at_x0, (y, (x + 1) % nx, h)),
        (at_x0, (y, (x + nx - 1) % nx, h)),
        (jnp.logical_and(at_y0, dx == 1), (y, (x + 1) % nx, h)),
        (dy < half, ((y + 1) % ny, x, h)),
        (jnp.logical_or(at_y0, dy > half + 1), ((y + ny - 1) % ny, x, h)),
    ]
    x_depth = jnp.where(dx == 0, 0, jnp.where(dx == 2, 2, 1))
    y_depth = jnp.where(dy <= half, dy, ny - dy)
    return is_root, parent, kids, dh + x_depth + y_depth


N_CHUNKS = 4
N_BLOCKS = 8
N_SLOTS = 7
MAX_DEPTH = 9
NARROW_LAG = 2
W_CHUNKS = 2


def bcast_kernel(src_ref, panel_ref, blocks_ref, nsend, nrecv, wsend, wrecv):
    y, x, h, q = positions()
    n = lax.axis_size("narrow")
    ny = lax.axis_size("wide_0")
    nx = lax.axis_size("wide_1")
    rows = panel_ref.shape[0] // N_CHUNKS
    even = q % 2 == 0
    n_has_parent, n_parent, n_kids = narrow_tree(q, n)

    trees = []
    for j in range(N_BLOCKS):
        if j < N_BLOCKS // 2:
            is_root, parent, kids, depth = wide_tree(y, x, h, j, ny, nx)
            active = q >= 0
            parent = tuple(jnp.where(even, p, o) for p, o in zip((*parent, q), (y, x, h, q - 1)))
            kids = [(jnp.logical_and(even, c), (*k, q)) for c, k in kids]
            kids.append((even, (y, x, h, q + 1)))
            is_root = jnp.logical_and(even, is_root)
            depth = depth + 1 - even.astype(jnp.int32)
        else:
            root = 4 * q + (j - N_BLOCKS // 2)
            is_root, parent, kids, depth = wide_tree(y, x, h, root, ny, nx)
            active = q > 0
            parent = (*parent, q)
            kids = [(c, (*k, q)) for c, k in kids]
            kids.append((q < 0, (y, x, h, q)))
        trees.append((active, is_root, parent, kids, depth))

    barrier = pltpu.get_barrier_semaphore()

    @pl.when(n_has_parent)
    def _():
        pl.semaphore_signal(barrier, 1, device_id=(y, x, h, n_parent), device_id_type=MESH_ID)

    peers = n_has_parent.astype(jnp.int32)
    for cond, kid in n_kids:
        peers = peers + cond.astype(jnp.int32)

        @pl.when(cond)
        def _():
            pl.semaphore_signal(barrier, 1, device_id=(y, x, h, kid), device_id_type=MESH_ID)

    for active, is_root, parent, kids, depth in trees:
        has_parent = jnp.logical_and(active, jnp.logical_not(is_root))
        peers = peers + has_parent.astype(jnp.int32)

        @pl.when(has_parent)
        def _():
            pl.semaphore_signal(barrier, 1, device_id=parent, device_id_type=MESH_ID)

        for cond, kid in kids:
            go = jnp.logical_and(active, cond)
            peers = peers + go.astype(jnp.int32)

            @pl.when(go)
            def _():
                pl.semaphore_signal(barrier, 1, device_id=kid, device_id_type=MESH_ID)

    pl.semaphore_wait(barrier, peers)

    def narrow_copy(src, c, k, kid):
        part = pl.ds(c * rows, rows)
        return pltpu.make_async_remote_copy(
            src_ref=src.at[part],
            dst_ref=panel_ref.at[part],
            send_sem=nsend.at[c, k],
            recv_sem=nrecv.at[c],
            device_id=(y, x, h, kid),
            device_id_type=MESH_ID,
        )

    def narrow_step(c):
        @pl.when(n_has_parent)
        def _():
            narrow_copy(panel_ref, c, 0, q).wait_recv()

        for k, (cond, kid) in enumerate(n_kids):
            @pl.when(jnp.logical_and(cond, q == 0))
            def _():
                narrow_copy(src_ref, c, k, kid).start()

            @pl.when(jnp.logical_and(cond, q != 0))
            def _():
                narrow_copy(panel_ref, c, k, kid).start()

    piece = rows // W_CHUNKS

    def wide_copy(src, j, c, k, kid):
        part = pl.ds(c * piece, piece)
        cols = pl.ds(0, (j + 1) * rows if j < N_BLOCKS // 2 else src.shape[1])
        return pltpu.make_async_remote_copy(
            src_ref=src.at[part, cols],
            dst_ref=blocks_ref.at[j, part, cols],
            send_sem=wsend.at[j, c, k],
            recv_sem=wrecv.at[j, c],
            device_id=kid,
            device_id_type=MESH_ID,
        )

    @pl.when(q == 0)
    def _():
        for c in range(N_CHUNKS):
            narrow_step(c)
        panel_ref[...] = src_ref[...]

    @pl.when(q != 0)
    def _():
        narrow_step(0)

    for j, (active, is_root, parent, kids, depth) in enumerate(trees):
        root_here = jnp.logical_and(active, is_root)
        for c in range(W_CHUNKS):
            for k, (cond, kid) in enumerate(kids):
                @pl.when(jnp.logical_and(jnp.logical_and(root_here, cond), q == 0))
                def _():
                    wide_copy(src_ref.at[pl.ds(0, rows)], j, c, k, kid).start()

                @pl.when(jnp.logical_and(jnp.logical_and(root_here, cond), q != 0))
                def _():
                    wide_copy(panel_ref.at[pl.ds(0, rows)], j, c, k, kid).start()

        @pl.when(jnp.logical_and(root_here, q == 0))
        def _():
            blocks_ref[j] = src_ref[pl.ds(0, rows)]

        @pl.when(jnp.logical_and(root_here, q != 0))
        def _():
            blocks_ref[j] = panel_ref[pl.ds(0, rows)]

    for level in range(1, MAX_DEPTH + W_CHUNKS - 1):
        for c in range(W_CHUNKS):
            for j, (active, is_root, parent, kids, depth) in enumerate(trees):
                here = jnp.logical_and(jnp.logical_and(active, jnp.logical_not(is_root)), depth + c == level)

                @pl.when(here)
                def _():
                    wide_copy(blocks_ref.at[j], j, c, 0, (y, x, h, q)).wait_recv()

                for k, (cond, kid) in enumerate(kids):
                    @pl.when(jnp.logical_and(here, cond))
                    def _():
                        wide_copy(blocks_ref.at[j], j, c, k, kid).start()

        c = level - NARROW_LAG
        if 1 <= c < N_CHUNKS:
            @pl.when(q != 0)
            def _():
                narrow_step(c)

    for c in range(N_CHUNKS):
        for k, (cond, kid) in enumerate(n_kids):
            @pl.when(cond)
            def _():
                narrow_copy(panel_ref, c, k, kid).wait_send()

    for j, (active, is_root, parent, kids, depth) in enumerate(trees):
        for c in range(W_CHUNKS):
            for k, (cond, kid) in enumerate(kids):
                @pl.when(jnp.logical_and(active, cond))
                def _():
                    wide_copy(blocks_ref.at[j], j, c, k, kid).wait_send()


def broadcast(panel):
    rows = panel.shape[0] // N_CHUNKS
    vmem = pl.BlockSpec(memory_space=pltpu.VMEM)
    return pl.pallas_call(
        bcast_kernel,
        out_shape=(
            jax.ShapeDtypeStruct(panel.shape, panel.dtype),
            jax.ShapeDtypeStruct((N_BLOCKS, rows, panel.shape[1]), panel.dtype),
        ),
        in_specs=[vmem],
        out_specs=(vmem, vmem),
        scratch_shapes=[
            pltpu.SemaphoreType.DMA((N_CHUNKS, 2)),
            pltpu.SemaphoreType.DMA((N_CHUNKS,)),
            pltpu.SemaphoreType.DMA((N_BLOCKS, W_CHUNKS, N_SLOTS)),
            pltpu.SemaphoreType.DMA((N_BLOCKS, W_CHUNKS)),
        ],
        compiler_params=pltpu.CompilerParams(collective_id=0, has_side_effects=True),
    )(panel)


def mm_t(a, b):
    return lax.dot_general(
        a, b, (((1,), (1,)), ((), ())),
        precision=HIGHEST_PRECISION, preferred_element_type=jnp.float32,
    )


def mm(a, b):
    return jnp.dot(a, b, precision=HIGHEST_PRECISION, preferred_element_type=jnp.float32)


def newton_inverse(lower, start, steps):
    inverse = start
    for _ in range(steps):
        inverse = 2 * inverse - mm(inverse, mm(lower, inverse))
    return inverse


def diagonal_inverse(lower):
    n = lower.shape[0]
    on_diag = lax.broadcasted_iota(jnp.int32, (n, n), 0) == lax.broadcasted_iota(jnp.int32, (n, n), 1)
    diag = jnp.sum(jnp.where(on_diag, lower, 0.0), axis=1, keepdims=True)
    return jnp.where(on_diag, 1.0 / diag, 0.0)


def blocked_cholesky(symmetric):
    n = symmetric.shape[0]
    nb = n // BS
    work = symmetric
    cols = []
    block_inverses = []
    for b in range(nb):
        head = work[:BS, :BS]
        diag = jnp.tril(jnp.linalg.cholesky(head, symmetrize_input=False))
        inv = newton_inverse(diag, diagonal_inverse(diag), (BS - 1).bit_length())
        block_inverses.append(inv)
        if b + 1 < nb:
            below = mm_t(work[BS:, :BS], inv)
            work = work[BS:, BS:] - mm_t(below, below)
            cols.append(jnp.concatenate([jnp.zeros((b * BS, BS), jnp.float32), diag, below], 0))
        else:
            cols.append(jnp.concatenate([jnp.zeros((b * BS, BS), jnp.float32), diag], 0))
    factor = jnp.concatenate(cols, 1)
    return factor, block_inverses


def right_solve(rows_in, factor, block_inverses):
    parts = []
    for b, inv in enumerate(block_inverses):
        acc = rows_in[:, b * BS : (b + 1) * BS]
        if b:
            acc = acc - mm_t(jnp.concatenate(parts, 1), factor[b * BS : (b + 1) * BS, : b * BS])
        parts.append(mm_t(acc, inv))
    return jnp.concatenate(parts, 1)


def shards(front, child_update, child_map):
    wide_count = lax.axis_size(WIDE)
    narrow_count = lax.axis_size("narrow")
    wide_index = lax.axis_index(WIDE)
    narrow_index = lax.axis_index("narrow")
    half_count = wide_count // 2
    local_rows, local_cols = front.shape
    front_slots = local_rows // BS
    block_total = front_slots * wide_count
    child_side = wide_index // half_count
    row_local = jnp.arange(local_rows, dtype=jnp.int32)
    global_row = (row_local // BS * wide_count + wide_index) * BS + row_local % BS
    col_local = jnp.arange(local_cols, dtype=jnp.int32)
    global_col = (col_local // PW * narrow_count + narrow_index) * PW + col_local % PW
    groups = child_update.reshape(2, front_slots, BS, local_cols)
    leaving = lax.dynamic_index_in_dim(groups, 1 - child_side, 0, keepdims=False)
    arrived = from_partner(leaving, WIDE, half_count.bit_length() - 1)

    def named_cols(side):
        names = lax.dynamic_slice_in_dim(child_map, side * block_total, block_total)
        return jnp.any(names[:, None] == (global_col // BS)[None, :], axis=0)

    kept_rows = lax.dynamic_index_in_dim(groups, child_side, 0, keepdims=False)
    kept_rows = jnp.where(named_cols(child_side)[None, None, :], kept_rows, 0.0)
    arrived = jnp.where(named_cols(1 - child_side)[None, None, :], arrived, 0.0)
    partner = (wide_index + half_count) % wide_count
    own_map = lax.dynamic_slice_in_dim(
        child_map, (wide_index * 2 + child_side) * front_slots, front_slots
    )
    got_map = lax.dynamic_slice_in_dim(
        child_map, (partner * 2 + child_side) * front_slots, front_slots
    )
    target = wide_index + wide_count * jnp.arange(front_slots, dtype=jnp.int32)
    own_select = (own_map[None, :] == target[:, None]).astype(jnp.float32)
    got_select = (got_map[None, :] == target[:, None]).astype(jnp.float32)
    own_part = jnp.dot(
        own_select,
        kept_rows.reshape(front_slots, BS * local_cols),
        precision=HIGHEST_PRECISION,
        preferred_element_type=jnp.float32,
    )
    got_part = jnp.dot(
        got_select,
        arrived.reshape(front_slots, BS * local_cols),
        precision=HIGHEST_PRECISION,
        preferred_element_type=jnp.float32,
    )
    matrix = front + (own_part + got_part).reshape(local_rows, local_cols)

    panel, blocks = broadcast(matrix)
    diag_block = blocks[: N_BLOCKS // 2].reshape(PW, PW)
    diag_block = jnp.where(
        lax.broadcasted_iota(jnp.int32, (PW, PW), 1) < (lax.broadcasted_iota(jnp.int32, (PW, PW), 0) // BS + 1) * BS,
        diag_block,
        0.0,
    )
    col_rows = blocks[N_BLOCKS // 2 :].reshape(PW, PW)

    factor_diag, block_inverses = blocked_cholesky(diag_block)
    solved = right_solve(jnp.concatenate([panel, col_rows], 0), factor_diag, block_inverses)
    own_factor = solved[: panel.shape[0]]
    diag_rows = lax.dynamic_slice_in_dim(factor_diag, jnp.minimum(wide_index, 3) * BS, BS)
    top = jnp.where(wide_index * BS < PW, diag_rows, own_factor[:BS])
    own_factor = jnp.concatenate([top, own_factor[BS:]], 0)
    col_factor = solved[panel.shape[0] :]
    update = mm_t(own_factor, col_factor)
    renewed = jnp.where(narrow_index == 0, own_factor, matrix - update)
    on_or_below = global_row[:, None] >= global_col[None, :]
    return jnp.where(on_or_below, renewed, jnp.zeros_like(renewed))


def solution(mesh):
    torus = Mesh(
        mesh.devices.reshape(8, 4, 2, mesh.shape["narrow"]),
        AXES,
    )
    placed = (P(WIDE, "narrow"), P(WIDE, "narrow"), P())
    return jax.shard_map(
        shards, mesh=torus, in_specs=placed, out_specs=P(WIDE, "narrow"), check_vma=False
    )
```

```python
import functools

import jax
import jax.numpy as jnp
from jax import lax
from jax.experimental import pallas as pl
from jax.experimental.pallas import tpu as pltpu
from jax.sharding import Mesh
from jax.sharding import PartitionSpec as P

BS = 128
PW = 512
WIDE = ("wide_0", "wide_1", "wide_2")
AXES = ("wide_0", "wide_1", "wide_2", "narrow")
MESH_ID = pl.DeviceIdType.MESH

HIGHEST_PRECISION = lax.Precision.HIGHEST


def from_partner(value, axis, distance):
    return lax.ppermute(value, axis, [(i, i ^ 1 << distance) for i in range(lax.axis_size(axis))])


def positions():
    return tuple(lax.axis_index(a) for a in AXES)


def narrow_tree(q, n):
    even = q % 2 == 0
    parent = jnp.where(even, q - 2, q - 1)
    kids = [(even, q + 1), (jnp.logical_and(even, q + 2 < n), q + 2)]
    return q > 0, parent, kids


def wide_tree(y, x, h, root, ny, nx):
    y0 = root // (2 * nx)
    x0 = (root // 2) % nx
    h0 = root % 2
    dy = (y - y0 + ny) % ny
    dx = (x - x0 + nx) % nx
    dh = (h - h0 + 2) % 2
    half = ny // 2
    at_y0 = dy == 0
    at_x0 = jnp.logical_and(at_y0, dx == 0)
    is_root = jnp.logical_and(at_x0, dh == 0)
    up = jnp.logical_and(dy >= 1, dy <= half)
    py = jnp.where(up, (y + ny - 1) % ny, (y + 1) % ny)
    px = jnp.where(dx == 2, (x + nx - 1) % nx, x0)
    parent_y = jnp.where(at_y0, y, py)
    parent_x = jnp.where(jnp.logical_and(at_y0, dx != 0), px, x)
    parent_h = jnp.where(at_x0, h0, h)
    parent = (parent_y, parent_x, parent_h)
    kids = [
        (is_root, (y, x, 1 - h)),
        (at_x0, (y, (x + 1) % nx, h)),
        (at_x0, (y, (x + nx - 1) % nx, h)),
        (jnp.logical_and(at_y0, dx == 1), (y, (x + 1) % nx, h)),
        (dy < half, ((y + 1) % ny, x, h)),
        (jnp.logical_or(at_y0, dy > half + 1), ((y + ny - 1) % ny, x, h)),
    ]
    x_depth = jnp.where(dx == 0, 0, jnp.where(dx == 2, 2, 1))
    y_depth = jnp.where(dy <= half, dy, ny - dy)
    return is_root, parent, kids, dh + x_depth + y_depth


N_CHUNKS = 4
N_BLOCKS = 8
N_SLOTS = 7
MAX_DEPTH = 9
NARROW_LAG = 2
W_CHUNKS = 2


def bcast_kernel(src_ref, panel_ref, blocks_ref, nsend, nrecv, wsend, wrecv, root_rows, fsend, frecv):
    y, x, h, q = positions()
    n = lax.axis_size("narrow")
    ny = lax.axis_size("wide_0")
    nx = lax.axis_size("wide_1")
    rows = panel_ref.shape[0] // N_CHUNKS
    even = q % 2 == 0
    n_has_parent, n_parent, n_kids = narrow_tree(q, n)

    trees = []
    for j in range(N_BLOCKS):
        if j < N_BLOCKS // 2:
            is_root, parent, kids, depth = wide_tree(y, x, h, j, ny, nx)
            active = q >= 0
            parent = tuple(jnp.where(even, p, o) for p, o in zip((*parent, q), (y, x, h, q - 1)))
            kids = [(jnp.logical_and(even, c), (*k, q)) for c, k in kids]
            kids.append((even, (y, x, h, q + 1)))
            is_root = jnp.logical_and(even, is_root)
            depth = depth + 1 - even.astype(jnp.int32)
        else:
            root = 4 * q + (j - N_BLOCKS // 2)
            is_root, parent, kids, depth = wide_tree(y, x, h, root, ny, nx)
            active = q > 0
            parent = (*parent, q)
            kids = [(c, (*k, q)) for c, k in kids]
            kids.append((q < 0, (y, x, h, q)))
        trees.append((active, is_root, parent, kids, depth))

    w = (y * nx + x) * 2 + h
    roots_per_q = N_BLOCKS // 2
    fed = jnp.logical_and(
        q > 0,
        jnp.logical_or(w // roots_per_q == q, jnp.logical_and(w < roots_per_q, even)),
    )
    feeds = [
        (jnp.logical_and(q == 0, w < roots_per_q), jnp.int32(t)) for t in range(2, 8, 2)
    ]
    feeds.append((jnp.logical_and(q == 0, jnp.logical_and(w >= roots_per_q, w // roots_per_q < n)), w // roots_per_q))

    barrier = pltpu.get_barrier_semaphore()

    peers = fed.astype(jnp.int32)

    @pl.when(fed)
    def _():
        pl.semaphore_signal(barrier, 1, device_id=(y, x, h, 0), device_id_type=MESH_ID)

    for cond, target in feeds:
        peers = peers + cond.astype(jnp.int32)

        @pl.when(cond)
        def _():
            pl.semaphore_signal(barrier, 1, device_id=(y, x, h, target), device_id_type=MESH_ID)

    @pl.when(n_has_parent)
    def _():
        pl.semaphore_signal(barrier, 1, device_id=(y, x, h, n_parent), device_id_type=MESH_ID)

    peers = peers + n_has_parent.astype(jnp.int32)
    for cond, kid in n_kids:
        peers = peers + cond.astype(jnp.int32)

        @pl.when(cond)
        def _():
            pl.semaphore_signal(barrier, 1, device_id=(y, x, h, kid), device_id_type=MESH_ID)

    for active, is_root, parent, kids, depth in trees:
        has_parent = jnp.logical_and(active, jnp.logical_not(is_root))
        peers = peers + has_parent.astype(jnp.int32)

        @pl.when(has_parent)
        def _():
            pl.semaphore_signal(barrier, 1, device_id=parent, device_id_type=MESH_ID)

        for cond, kid in kids:
            go = jnp.logical_and(active, cond)
            peers = peers + go.astype(jnp.int32)

            @pl.when(go)
            def _():
                pl.semaphore_signal(barrier, 1, device_id=kid, device_id_type=MESH_ID)

    pl.semaphore_wait(barrier, peers)

    def narrow_copy(src, c, k, kid):
        part = pl.ds(c * rows, rows)
        return pltpu.make_async_remote_copy(
            src_ref=src.at[part],
            dst_ref=panel_ref.at[part],
            send_sem=nsend.at[c, k],
            recv_sem=nrecv.at[c],
            device_id=(y, x, h, kid),
            device_id_type=MESH_ID,
        )

    def narrow_step(c):
        @pl.when(n_has_parent)
        def _():
            narrow_copy(panel_ref, c, 0, q).wait_recv()

        for k, (cond, kid) in enumerate(n_kids):
            @pl.when(jnp.logical_and(cond, q == 0))
            def _():
                narrow_copy(src_ref, c, k, kid).start()

            @pl.when(jnp.logical_and(cond, q != 0))
            def _():
                narrow_copy(panel_ref, c, k, kid).start()

    piece = rows // W_CHUNKS

    def wide_copy(src, j, c, k, kid):
        part = pl.ds(c * piece, piece)
        cols = pl.ds(0, (j + 1) * rows if j < N_BLOCKS // 2 else src.shape[1])
        return pltpu.make_async_remote_copy(
            src_ref=src.at[part, cols],
            dst_ref=blocks_ref.at[j, part, cols],
            send_sem=wsend.at[j, c, k],
            recv_sem=wrecv.at[j, c],
            device_id=kid,
            device_id_type=MESH_ID,
        )

    def feed_copy(k, target):
        return pltpu.make_async_remote_copy(
            src_ref=src_ref.at[pl.ds(0, rows)],
            dst_ref=root_rows,
            send_sem=fsend.at[k],
            recv_sem=frecv.at[0],
            device_id=(y, x, h, target),
            device_id_type=MESH_ID,
        )

    @pl.when(q == 0)
    def _():
        for k, (cond, target) in enumerate(feeds):
            @pl.when(cond)
            def _():
                feed_copy(k, target).start()

        for c in range(N_CHUNKS):
            narrow_step(c)
        panel_ref[...] = src_ref[...]

    @pl.when(fed)
    def _():
        feed_copy(0, q).wait_recv()

    for j, (active, is_root, parent, kids, depth) in enumerate(trees):
        root_here = jnp.logical_and(active, is_root)
        for c in range(W_CHUNKS):
            for k, (cond, kid) in enumerate(kids):
                @pl.when(jnp.logical_and(jnp.logical_and(root_here, cond), q == 0))
                def _():
                    wide_copy(src_ref.at[pl.ds(0, rows)], j, c, k, kid).start()

                @pl.when(jnp.logical_and(jnp.logical_and(root_here, cond), q != 0))
                def _():
                    wide_copy(root_rows, j, c, k, kid).start()

        @pl.when(jnp.logical_and(root_here, q == 0))
        def _():
            blocks_ref[j] = src_ref[pl.ds(0, rows)]

        @pl.when(jnp.logical_and(root_here, q != 0))
        def _():
            blocks_ref[j] = root_rows[...]

    @pl.when(q != 0)
    def _():
        narrow_step(0)

    for level in range(1, MAX_DEPTH + W_CHUNKS - 1):
        for c in range(W_CHUNKS):
            for j, (active, is_root, parent, kids, depth) in enumerate(trees):
                here = jnp.logical_and(jnp.logical_and(active, jnp.logical_not(is_root)), depth + c == level)

                @pl.when(here)
                def _():
                    wide_copy(blocks_ref.at[j], j, c, 0, (y, x, h, q)).wait_recv()

                for k, (cond, kid) in enumerate(kids):
                    @pl.when(jnp.logical_and(here, cond))
                    def _():
                        wide_copy(blocks_ref.at[j], j, c, k, kid).start()

        c = level - NARROW_LAG
        if 1 <= c < N_CHUNKS:
            @pl.when(q != 0)
            def _():
                narrow_step(c)

    for c in range(N_CHUNKS):
        for k, (cond, kid) in enumerate(n_kids):
            @pl.when(cond)
            def _():
                narrow_copy(panel_ref, c, k, kid).wait_send()

    for j, (active, is_root, parent, kids, depth) in enumerate(trees):
        for c in range(W_CHUNKS):
            for k, (cond, kid) in enumerate(kids):
                @pl.when(jnp.logical_and(active, cond))
                def _():
                    wide_copy(blocks_ref.at[j], j, c, k, kid).wait_send()

    for k, (cond, target) in enumerate(feeds):
        @pl.when(cond)
        def _():
            feed_copy(k, target).wait_send()


def broadcast(panel):
    rows = panel.shape[0] // N_CHUNKS
    vmem = pl.BlockSpec(memory_space=pltpu.VMEM)
    return pl.pallas_call(
        bcast_kernel,
        out_shape=(
            jax.ShapeDtypeStruct(panel.shape, panel.dtype),
            jax.ShapeDtypeStruct((N_BLOCKS, rows, panel.shape[1]), panel.dtype),
        ),
        in_specs=[vmem],
        out_specs=(vmem, vmem),
        scratch_shapes=[
            pltpu.SemaphoreType.DMA((N_CHUNKS, 2)),
            pltpu.SemaphoreType.DMA((N_CHUNKS,)),
            pltpu.SemaphoreType.DMA((N_BLOCKS, W_CHUNKS, N_SLOTS)),
            pltpu.SemaphoreType.DMA((N_BLOCKS, W_CHUNKS)),
            pltpu.VMEM((rows, panel.shape[1]), panel.dtype),
            pltpu.SemaphoreType.DMA((4,)),
            pltpu.SemaphoreType.DMA((1,)),
        ],
        compiler_params=pltpu.CompilerParams(collective_id=0, has_side_effects=True),
    )(panel)


def mm_t(a, b):
    return lax.dot_general(
        a, b, (((1,), (1,)), ((), ())),
        precision=HIGHEST_PRECISION, preferred_element_type=jnp.float32,
    )


def mm(a, b):
    return jnp.dot(a, b, precision=HIGHEST_PRECISION, preferred_element_type=jnp.float32)


def newton_inverse(lower, start, steps):
    inverse = start
    for _ in range(steps):
        inverse = 2 * inverse - mm(inverse, mm(lower, inverse))
    return inverse


def diagonal_inverse(lower):
    n = lower.shape[0]
    on_diag = lax.broadcasted_iota(jnp.int32, (n, n), 0) == lax.broadcasted_iota(jnp.int32, (n, n), 1)
    diag = jnp.sum(jnp.where(on_diag, lower, 0.0), axis=1, keepdims=True)
    return jnp.where(on_diag, 1.0 / diag, 0.0)


def cholesky_and_inverse(symmetric):
    n = symmetric.shape[0]
    nb = n // BS
    work = symmetric
    cols = []
    block_inverses = []
    for b in range(nb):
        head = work[:BS, :BS]
        diag = jnp.tril(jnp.linalg.cholesky(head, symmetrize_input=False))
        inv = newton_inverse(diag, diagonal_inverse(diag), (BS - 1).bit_length())
        block_inverses.append(inv)
        if b + 1 < nb:
            below = mm_t(work[BS:, :BS], inv)
            work = work[BS:, BS:] - mm_t(below, below)
            cols.append(jnp.concatenate([jnp.zeros((b * BS, BS), jnp.float32), diag, below], 0))
        else:
            cols.append(jnp.concatenate([jnp.zeros((b * BS, BS), jnp.float32), diag], 0))
    factor = jnp.concatenate(cols, 1)
    start = jnp.zeros((n, n), jnp.float32)
    for b in range(nb):
        start = lax.dynamic_update_slice(start, block_inverses[b], (b * BS, b * BS))
    inverse = newton_inverse(factor, start, max(1, (nb - 1).bit_length()))
    return factor, inverse


def shards(front, child_update, child_map):
    wide_count = lax.axis_size(WIDE)
    narrow_count = lax.axis_size("narrow")
    wide_index = lax.axis_index(WIDE)
    narrow_index = lax.axis_index("narrow")
    half_count = wide_count // 2
    local_rows, local_cols = front.shape
    front_slots = local_rows // BS
    block_total = front_slots * wide_count
    child_side = wide_index // half_count
    row_local = jnp.arange(local_rows, dtype=jnp.int32)
    global_row = (row_local // BS * wide_count + wide_index) * BS + row_local % BS
    col_local = jnp.arange(local_cols, dtype=jnp.int32)
    global_col = (col_local // PW * narrow_count + narrow_index) * PW + col_local % PW
    groups = child_update.reshape(2, front_slots, BS, local_cols)
    leaving = lax.dynamic_index_in_dim(groups, 1 - child_side, 0, keepdims=False)
    arrived = from_partner(leaving, WIDE, half_count.bit_length() - 1)

    def named_cols(side):
        names = lax.dynamic_slice_in_dim(child_map, side * block_total, block_total)
        return jnp.any(names[:, None] == (global_col // BS)[None, :], axis=0)

    kept_rows = lax.dynamic_index_in_dim(groups, child_side, 0, keepdims=False)
    kept_rows = jnp.where(named_cols(child_side)[None, None, :], kept_rows, 0.0)
    arrived = jnp.where(named_cols(1 - child_side)[None, None, :], arrived, 0.0)
    partner = (wide_index + half_count) % wide_count
    own_map = lax.dynamic_slice_in_dim(
        child_map, (wide_index * 2 + child_side) * front_slots, front_slots
    )
    got_map = lax.dynamic_slice_in_dim(
        child_map, (partner * 2 + child_side) * front_slots, front_slots
    )
    target = wide_index + wide_count * jnp.arange(front_slots, dtype=jnp.int32)
    own_select = (own_map[None, :] == target[:, None]).astype(jnp.float32)
    got_select = (got_map[None, :] == target[:, None]).astype(jnp.float32)
    own_part = jnp.dot(
        own_select,
        kept_rows.reshape(front_slots, BS * local_cols),
        precision=HIGHEST_PRECISION,
        preferred_element_type=jnp.float32,
    )
    got_part = jnp.dot(
        got_select,
        arrived.reshape(front_slots, BS * local_cols),
        precision=HIGHEST_PRECISION,
        preferred_element_type=jnp.float32,
    )
    matrix = front + (own_part + got_part).reshape(local_rows, local_cols)

    panel, blocks = broadcast(matrix)
    diag_block = blocks[: N_BLOCKS // 2].reshape(PW, PW)
    diag_block = jnp.where(
        lax.broadcasted_iota(jnp.int32, (PW, PW), 1) < (lax.broadcasted_iota(jnp.int32, (PW, PW), 0) // BS + 1) * BS,
        diag_block,
        0.0,
    )
    col_rows = blocks[N_BLOCKS // 2 :].reshape(PW, PW)

    factor_diag, inverse = cholesky_and_inverse(diag_block)
    own_factor = mm_t(panel, inverse)
    diag_rows = lax.dynamic_slice_in_dim(factor_diag, jnp.minimum(wide_index, 3) * BS, BS)
    top = jnp.where(wide_index * BS < PW, diag_rows, own_factor[:BS])
    own_factor = jnp.concatenate([top, own_factor[BS:]], 0)
    col_factor = mm_t(col_rows, inverse)
    update = mm_t(own_factor, col_factor)
    renewed = jnp.where(narrow_index == 0, own_factor, matrix - update)
    on_or_below = global_row[:, None] >= global_col[None, :]
    return jnp.where(on_or_below, renewed, jnp.zeros_like(renewed))


def solution(mesh):
    torus = Mesh(
        mesh.devices.reshape(8, 4, 2, mesh.shape["narrow"]),
        AXES,
    )
    placed = (P(WIDE, "narrow"), P(WIDE, "narrow"), P())
    return jax.shard_map(
        shards, mesh=torus, in_specs=placed, out_specs=P(WIDE, "narrow"), check_vma=False
    )
```

```python
import functools

import jax
import jax.numpy as jnp
from jax import lax
from jax.experimental import pallas as pl
from jax.experimental.pallas import tpu as pltpu
from jax.sharding import Mesh
from jax.sharding import PartitionSpec as P

BS = 128
PW = 512
WIDE = ("wide_0", "wide_1", "wide_2")
AXES = ("wide_0", "wide_1", "wide_2", "narrow")
MESH_ID = pl.DeviceIdType.MESH

HIGHEST_PRECISION = lax.Precision.HIGHEST


def from_partner(value, axis, distance):
    return lax.ppermute(value, axis, [(i, i ^ 1 << distance) for i in range(lax.axis_size(axis))])


def positions():
    return tuple(lax.axis_index(a) for a in AXES)


def narrow_tree(q, n):
    even = q % 2 == 0
    parent = jnp.where(even, q - 2, q - 1)
    kids = [(even, q + 1), (jnp.logical_and(even, q + 2 < n), q + 2)]
    return q > 0, parent, kids


def wide_tree(y, x, h, root, ny, nx, cw=None):
    y0 = root // (2 * nx)
    x0 = (root // 2) % nx
    h0 = root % 2
    dy = (y - y0 + ny) % ny
    dx = (x - x0 + nx) % nx
    dh = (h - h0 + 2) % 2
    half = ny // 2 if cw is None else cw
    at_y0 = dy == 0
    at_x0 = jnp.logical_and(at_y0, dx == 0)
    is_root = jnp.logical_and(at_x0, dh == 0)
    up = jnp.logical_and(dy >= 1, dy <= half)
    py = jnp.where(up, (y + ny - 1) % ny, (y + 1) % ny)
    px = jnp.where(dx == 2, (x + nx - 1) % nx, x0)
    parent_y = jnp.where(at_y0, y, py)
    parent_x = jnp.where(jnp.logical_and(at_y0, dx != 0), px, x)
    parent_h = jnp.where(at_x0, h0, h)
    parent = (parent_y, parent_x, parent_h)
    kids = [
        (is_root, (y, x, 1 - h)),
        (at_x0, (y, (x + 1) % nx, h)),
        (at_x0, (y, (x + nx - 1) % nx, h)),
        (jnp.logical_and(at_y0, dx == 1), (y, (x + 1) % nx, h)),
        (dy < half, ((y + 1) % ny, x, h)),
        (jnp.logical_or(at_y0, dy > half + 1), ((y + ny - 1) % ny, x, h)),
    ]
    x_depth = jnp.where(dx == 0, 0, jnp.where(dx == 2, 2, 1))
    y_depth = jnp.where(dy <= half, dy, ny - dy)
    return is_root, parent, kids, dh + x_depth + y_depth


N_CHUNKS = 4
N_BLOCKS = 8
N_SLOTS = 7
MAX_DEPTH = 9
NARROW_LAG = 2
W_CHUNKS = 2


def bcast_kernel(src_ref, panel_ref, blocks_ref, nsend, nrecv, wsend, wrecv):
    y, x, h, q = positions()
    n = lax.axis_size("narrow")
    ny = lax.axis_size("wide_0")
    nx = lax.axis_size("wide_1")
    rows = panel_ref.shape[0] // N_CHUNKS
    even = q % 2 == 0
    n_has_parent, n_parent, n_kids = narrow_tree(q, n)

    trees = []
    for j in range(N_BLOCKS):
        if j < N_BLOCKS // 2:
            cw = jnp.where(q // 2 == 3, 3, ny // 2)
            is_root, parent, kids, depth = wide_tree(y, x, h, j, ny, nx, cw)
            active = q >= 0
            parent = tuple(jnp.where(even, p, o) for p, o in zip((*parent, q), (y, x, h, q - 1)))
            kids = [(jnp.logical_and(even, c), (*k, q)) for c, k in kids]
            kids.append((even, (y, x, h, q + 1)))
            is_root = jnp.logical_and(even, is_root)
            depth = depth + 1 - even.astype(jnp.int32)
        else:
            root = 4 * q + (j - N_BLOCKS // 2)
            is_root, parent, kids, depth = wide_tree(y, x, h, root, ny, nx)
            active = q > 0
            parent = (*parent, q)
            kids = [(c, (*k, q)) for c, k in kids]
            kids.append((q < 0, (y, x, h, q)))
        trees.append((active, is_root, parent, kids, depth))

    barrier = pltpu.get_barrier_semaphore()

    @pl.when(n_has_parent)
    def _():
        pl.semaphore_signal(barrier, 1, device_id=(y, x, h, n_parent), device_id_type=MESH_ID)

    peers = n_has_parent.astype(jnp.int32)
    for cond, kid in n_kids:
        peers = peers + cond.astype(jnp.int32)

        @pl.when(cond)
        def _():
            pl.semaphore_signal(barrier, 1, device_id=(y, x, h, kid), device_id_type=MESH_ID)

    for active, is_root, parent, kids, depth in trees:
        has_parent = jnp.logical_and(active, jnp.logical_not(is_root))
        peers = peers + has_parent.astype(jnp.int32)

        @pl.when(has_parent)
        def _():
            pl.semaphore_signal(barrier, 1, device_id=parent, device_id_type=MESH_ID)

        for cond, kid in kids:
            go = jnp.logical_and(active, cond)
            peers = peers + go.astype(jnp.int32)

            @pl.when(go)
            def _():
                pl.semaphore_signal(barrier, 1, device_id=kid, device_id_type=MESH_ID)

    pl.semaphore_wait(barrier, peers)

    def narrow_copy(src, c, k, kid):
        part = pl.ds(c * rows, rows)
        return pltpu.make_async_remote_copy(
            src_ref=src.at[part],
            dst_ref=panel_ref.at[part],
            send_sem=nsend.at[c, k],
            recv_sem=nrecv.at[c],
            device_id=(y, x, h, kid),
            device_id_type=MESH_ID,
        )

    def narrow_step(c):
        @pl.when(n_has_parent)
        def _():
            narrow_copy(panel_ref, c, 0, q).wait_recv()

        for k, (cond, kid) in enumerate(n_kids):
            @pl.when(jnp.logical_and(cond, q == 0))
            def _():
                narrow_copy(src_ref, c, k, kid).start()

            @pl.when(jnp.logical_and(cond, q != 0))
            def _():
                narrow_copy(panel_ref, c, k, kid).start()

    piece = rows // W_CHUNKS

    def wide_copy(src, j, c, k, kid):
        part = pl.ds(c * piece, piece)
        cols = pl.ds(0, (j + 1) * rows if j < N_BLOCKS // 2 else src.shape[1])
        return pltpu.make_async_remote_copy(
            src_ref=src.at[part, cols],
            dst_ref=blocks_ref.at[j, part, cols],
            send_sem=wsend.at[j, c, k],
            recv_sem=wrecv.at[j, c],
            device_id=kid,
            device_id_type=MESH_ID,
        )

    @pl.when(q == 0)
    def _():
        for c in range(N_CHUNKS):
            narrow_step(c)
        panel_ref[...] = src_ref[...]

    @pl.when(q != 0)
    def _():
        narrow_step(0)

    for j, (active, is_root, parent, kids, depth) in enumerate(trees):
        root_here = jnp.logical_and(active, is_root)
        for c in range(W_CHUNKS):
            for k, (cond, kid) in enumerate(kids):
                @pl.when(jnp.logical_and(jnp.logical_and(root_here, cond), q == 0))
                def _():
                    wide_copy(src_ref.at[pl.ds(0, rows)], j, c, k, kid).start()

                @pl.when(jnp.logical_and(jnp.logical_and(root_here, cond), q != 0))
                def _():
                    wide_copy(panel_ref.at[pl.ds(0, rows)], j, c, k, kid).start()

        @pl.when(jnp.logical_and(root_here, q == 0))
        def _():
            blocks_ref[j] = src_ref[pl.ds(0, rows)]

        @pl.when(jnp.logical_and(root_here, q != 0))
        def _():
            blocks_ref[j] = panel_ref[pl.ds(0, rows)]

    for level in range(1, MAX_DEPTH + W_CHUNKS - 1):
        for c in range(W_CHUNKS):
            for j, (active, is_root, parent, kids, depth) in enumerate(trees):
                here = jnp.logical_and(jnp.logical_and(active, jnp.logical_not(is_root)), depth + c == level)

                @pl.when(here)
                def _():
                    wide_copy(blocks_ref.at[j], j, c, 0, (y, x, h, q)).wait_recv()

                for k, (cond, kid) in enumerate(kids):
                    @pl.when(jnp.logical_and(here, cond))
                    def _():
                        wide_copy(blocks_ref.at[j], j, c, k, kid).start()

        c = level - NARROW_LAG
        if 1 <= c < N_CHUNKS:
            @pl.when(q != 0)
            def _():
                narrow_step(c)

    for c in range(N_CHUNKS):
        for k, (cond, kid) in enumerate(n_kids):
            @pl.when(cond)
            def _():
                narrow_copy(panel_ref, c, k, kid).wait_send()

    for j, (active, is_root, parent, kids, depth) in enumerate(trees):
        for c in range(W_CHUNKS):
            for k, (cond, kid) in enumerate(kids):
                @pl.when(jnp.logical_and(active, cond))
                def _():
                    wide_copy(blocks_ref.at[j], j, c, k, kid).wait_send()


def broadcast(panel):
    rows = panel.shape[0] // N_CHUNKS
    vmem = pl.BlockSpec(memory_space=pltpu.VMEM)
    return pl.pallas_call(
        bcast_kernel,
        out_shape=(
            jax.ShapeDtypeStruct(panel.shape, panel.dtype),
            jax.ShapeDtypeStruct((N_BLOCKS, rows, panel.shape[1]), panel.dtype),
        ),
        in_specs=[vmem],
        out_specs=(vmem, vmem),
        scratch_shapes=[
            pltpu.SemaphoreType.DMA((N_CHUNKS, 2)),
            pltpu.SemaphoreType.DMA((N_CHUNKS,)),
            pltpu.SemaphoreType.DMA((N_BLOCKS, W_CHUNKS, N_SLOTS)),
            pltpu.SemaphoreType.DMA((N_BLOCKS, W_CHUNKS)),
        ],
        compiler_params=pltpu.CompilerParams(collective_id=0, has_side_effects=True),
    )(panel)


def mm_t(a, b):
    return lax.dot_general(
        a, b, (((1,), (1,)), ((), ())),
        precision=HIGHEST_PRECISION, preferred_element_type=jnp.float32,
    )


def mm(a, b):
    return jnp.dot(a, b, precision=HIGHEST_PRECISION, preferred_element_type=jnp.float32)


def newton_inverse(lower, start, steps):
    inverse = start
    for _ in range(steps):
        inverse = 2 * inverse - mm(inverse, mm(lower, inverse))
    return inverse


def diagonal_inverse(lower):
    n = lower.shape[0]
    on_diag = lax.broadcasted_iota(jnp.int32, (n, n), 0) == lax.broadcasted_iota(jnp.int32, (n, n), 1)
    diag = jnp.sum(jnp.where(on_diag, lower, 0.0), axis=1, keepdims=True)
    return jnp.where(on_diag, 1.0 / diag, 0.0)


def cholesky_and_inverse(symmetric):
    n = symmetric.shape[0]
    nb = n // BS
    work = symmetric
    cols = []
    block_inverses = []
    for b in range(nb):
        head = work[:BS, :BS]
        diag = jnp.tril(jnp.linalg.cholesky(head, symmetrize_input=False))
        inv = newton_inverse(diag, diagonal_inverse(diag), (BS - 1).bit_length())
        block_inverses.append(inv)
        if b + 1 < nb:
            below = mm_t(work[BS:, :BS], inv)
            work = work[BS:, BS:] - mm_t(below, below)
            cols.append(jnp.concatenate([jnp.zeros((b * BS, BS), jnp.float32), diag, below], 0))
        else:
            cols.append(jnp.concatenate([jnp.zeros((b * BS, BS), jnp.float32), diag], 0))
    factor = jnp.concatenate(cols, 1)
    start = jnp.zeros((n, n), jnp.float32)
    for b in range(nb):
        start = lax.dynamic_update_slice(start, block_inverses[b], (b * BS, b * BS))
    inverse = newton_inverse(factor, start, max(1, (nb - 1).bit_length()))
    return factor, inverse


def shards(front, child_update, child_map):
    wide_count = lax.axis_size(WIDE)
    narrow_count = lax.axis_size("narrow")
    wide_index = lax.axis_index(WIDE)
    narrow_index = lax.axis_index("narrow")
    half_count = wide_count // 2
    local_rows, local_cols = front.shape
    front_slots = local_rows // BS
    block_total = front_slots * wide_count
    child_side = wide_index // half_count
    row_local = jnp.arange(local_rows, dtype=jnp.int32)
    global_row = (row_local // BS * wide_count + wide_index) * BS + row_local % BS
    col_local = jnp.arange(local_cols, dtype=jnp.int32)
    global_col = (col_local // PW * narrow_count + narrow_index) * PW + col_local % PW
    groups = child_update.reshape(2, front_slots, BS, local_cols)
    leaving = lax.dynamic_index_in_dim(groups, 1 - child_side, 0, keepdims=False)
    arrived = from_partner(leaving, WIDE, half_count.bit_length() - 1)

    def named_cols(side):
        names = lax.dynamic_slice_in_dim(child_map, side * block_total, block_total)
        return jnp.any(names[:, None] == (global_col // BS)[None, :], axis=0)

    kept_rows = lax.dynamic_index_in_dim(groups, child_side, 0, keepdims=False)
    kept_rows = jnp.where(named_cols(child_side)[None, None, :], kept_rows, 0.0)
    arrived = jnp.where(named_cols(1 - child_side)[None, None, :], arrived, 0.0)
    partner = (wide_index + half_count) % wide_count
    own_map = lax.dynamic_slice_in_dim(
        child_map, (wide_index * 2 + child_side) * front_slots, front_slots
    )
    got_map = lax.dynamic_slice_in_dim(
        child_map, (partner * 2 + child_side) * front_slots, front_slots
    )
    target = wide_index + wide_count * jnp.arange(front_slots, dtype=jnp.int32)
    own_select = (own_map[None, :] == target[:, None]).astype(jnp.float32)
    got_select = (got_map[None, :] == target[:, None]).astype(jnp.float32)
    own_part = jnp.dot(
        own_select,
        kept_rows.reshape(front_slots, BS * local_cols),
        precision=HIGHEST_PRECISION,
        preferred_element_type=jnp.float32,
    )
    got_part = jnp.dot(
        got_select,
        arrived.reshape(front_slots, BS * local_cols),
        precision=HIGHEST_PRECISION,
        preferred_element_type=jnp.float32,
    )
    matrix = front + (own_part + got_part).reshape(local_rows, local_cols)

    panel, blocks = broadcast(matrix)
    diag_block = blocks[: N_BLOCKS // 2].reshape(PW, PW)
    diag_block = jnp.where(
        lax.broadcasted_iota(jnp.int32, (PW, PW), 1) < (lax.broadcasted_iota(jnp.int32, (PW, PW), 0) // BS + 1) * BS,
        diag_block,
        0.0,
    )
    col_rows = blocks[N_BLOCKS // 2 :].reshape(PW, PW)

    factor_diag, inverse = cholesky_and_inverse(diag_block)
    own_factor = mm_t(panel, inverse)
    diag_rows = lax.dynamic_slice_in_dim(factor_diag, jnp.minimum(wide_index, 3) * BS, BS)
    top = jnp.where(wide_index * BS < PW, diag_rows, own_factor[:BS])
    own_factor = jnp.concatenate([top, own_factor[BS:]], 0)
    col_factor = mm_t(col_rows, inverse)
    update = mm_t(own_factor, col_factor)
    renewed = jnp.where(narrow_index == 0, own_factor, matrix - update)
    on_or_below = global_row[:, None] >= global_col[None, :]
    return jnp.where(on_or_below, renewed, jnp.zeros_like(renewed))


def solution(mesh):
    torus = Mesh(
        mesh.devices.reshape(8, 4, 2, mesh.shape["narrow"]),
        AXES,
    )
    placed = (P(WIDE, "narrow"), P(WIDE, "narrow"), P())
    return jax.shard_map(
        shards, mesh=torus, in_specs=placed, out_specs=P(WIDE, "narrow"), check_vma=False
    )
```

```python
import functools

import jax
import jax.numpy as jnp
from jax import lax
from jax.experimental import pallas as pl
from jax.experimental.pallas import tpu as pltpu
from jax.sharding import Mesh
from jax.sharding import PartitionSpec as P

BS = 128
PW = 512
WIDE = ("wide_0", "wide_1", "wide_2")
AXES = ("wide_0", "wide_1", "wide_2", "narrow")
MESH_ID = pl.DeviceIdType.MESH

HIGHEST_PRECISION = lax.Precision.HIGHEST


def from_partner(value, axis, distance):
    return lax.ppermute(value, axis, [(i, i ^ 1 << distance) for i in range(lax.axis_size(axis))])


def positions():
    return tuple(lax.axis_index(a) for a in AXES)


def narrow_tree(q, n):
    even = q % 2 == 0
    parent = jnp.where(even, q - 2, q - 1)
    kids = [(even, q + 1), (jnp.logical_and(even, q + 2 < n), q + 2)]
    return q > 0, parent, kids


def wide_tree(y, x, h, root, ny, nx):
    y0 = root // (2 * nx)
    x0 = (root // 2) % nx
    h0 = root % 2
    dy = (y - y0 + ny) % ny
    dx = (x - x0 + nx) % nx
    dh = (h - h0 + 2) % 2
    half = ny // 2
    at_y0 = dy == 0
    at_x0 = jnp.logical_and(at_y0, dx == 0)
    is_root = jnp.logical_and(at_x0, dh == 0)
    up = jnp.logical_and(dy >= 1, dy <= half)
    py = jnp.where(up, (y + ny - 1) % ny, (y + 1) % ny)
    px = jnp.where(dx == 2, (x + nx - 1) % nx, x0)
    parent_y = jnp.where(at_y0, y, py)
    parent_x = jnp.where(jnp.logical_and(at_y0, dx != 0), px, x)
    parent_h = jnp.where(at_x0, h0, h)
    parent = (parent_y, parent_x, parent_h)
    kids = [
        (is_root, (y, x, 1 - h)),
        (at_x0, (y, (x + 1) % nx, h)),
        (at_x0, (y, (x + nx - 1) % nx, h)),
        (jnp.logical_and(at_y0, dx == 1), (y, (x + 1) % nx, h)),
        (dy < half, ((y + 1) % ny, x, h)),
        (jnp.logical_or(at_y0, dy > half + 1), ((y + ny - 1) % ny, x, h)),
    ]
    x_depth = jnp.where(dx == 0, 0, jnp.where(dx == 2, 2, 1))
    y_depth = jnp.where(dy <= half, dy, ny - dy)
    return is_root, parent, kids, dh + x_depth + y_depth


N_CHUNKS = 4
N_BLOCKS = 8
N_SLOTS = 7
MAX_DEPTH = 9
NARROW_LAG = 1
W_CHUNKS = 2


def bcast_kernel(src_ref, panel_ref, blocks_ref, nsend, nrecv, wsend, wrecv):
    y, x, h, q = positions()
    n = lax.axis_size("narrow")
    ny = lax.axis_size("wide_0")
    nx = lax.axis_size("wide_1")
    rows = panel_ref.shape[0] // N_CHUNKS
    even = q % 2 == 0
    n_has_parent, n_parent, n_kids = narrow_tree(q, n)

    trees = []
    for j in range(N_BLOCKS):
        if j < N_BLOCKS // 2:
            is_root, parent, kids, depth = wide_tree(y, x, h, j, ny, nx)
            active = q >= 0
            parent = tuple(jnp.where(even, p, o) for p, o in zip((*parent, q), (y, x, h, q - 1)))
            kids = [(jnp.logical_and(even, c), (*k, q)) for c, k in kids]
            kids.append((even, (y, x, h, q + 1)))
            is_root = jnp.logical_and(even, is_root)
            depth = depth + 1 - even.astype(jnp.int32)
        else:
            root = 4 * q + (j - N_BLOCKS // 2)
            is_root, parent, kids, depth = wide_tree(y, x, h, root, ny, nx)
            active = q > 0
            parent = (*parent, q)
            kids = [(c, (*k, q)) for c, k in kids]
            kids.append((q < 0, (y, x, h, q)))
        trees.append((active, is_root, parent, kids, depth))

    barrier = pltpu.get_barrier_semaphore()

    @pl.when(n_has_parent)
    def _():
        pl.semaphore_signal(barrier, 1, device_id=(y, x, h, n_parent), device_id_type=MESH_ID)

    peers = n_has_parent.astype(jnp.int32)
    for cond, kid in n_kids:
        peers = peers + cond.astype(jnp.int32)

        @pl.when(cond)
        def _():
            pl.semaphore_signal(barrier, 1, device_id=(y, x, h, kid), device_id_type=MESH_ID)

    for active, is_root, parent, kids, depth in trees:
        has_parent = jnp.logical_and(active, jnp.logical_not(is_root))
        peers = peers + has_parent.astype(jnp.int32)

        @pl.when(has_parent)
        def _():
            pl.semaphore_signal(barrier, 1, device_id=parent, device_id_type=MESH_ID)

        for cond, kid in kids:
            go = jnp.logical_and(active, cond)
            peers = peers + go.astype(jnp.int32)

            @pl.when(go)
            def _():
                pl.semaphore_signal(barrier, 1, device_id=kid, device_id_type=MESH_ID)

    pl.semaphore_wait(barrier, peers)

    def narrow_copy(src, c, k, kid):
        part = pl.ds(c * rows, rows)
        return pltpu.make_async_remote_copy(
            src_ref=src.at[part],
            dst_ref=panel_ref.at[part],
            send_sem=nsend.at[c, k],
            recv_sem=nrecv.at[c],
            device_id=(y, x, h, kid),
            device_id_type=MESH_ID,
        )

    def narrow_step(c):
        @pl.when(n_has_parent)
        def _():
            narrow_copy(panel_ref, c, 0, q).wait_recv()

        for k, (cond, kid) in enumerate(n_kids):
            @pl.when(jnp.logical_and(cond, q == 0))
            def _():
                narrow_copy(src_ref, c, k, kid).start()

            @pl.when(jnp.logical_and(cond, q != 0))
            def _():
                narrow_copy(panel_ref, c, k, kid).start()

    piece = rows // W_CHUNKS

    def wide_copy(src, j, c, k, kid):
        part = pl.ds(c * piece, piece)
        cols = pl.ds(0, (j + 1) * rows if j < N_BLOCKS // 2 else src.shape[1])
        return pltpu.make_async_remote_copy(
            src_ref=src.at[part, cols],
            dst_ref=blocks_ref.at[j, part, cols],
            send_sem=wsend.at[j, c, k],
            recv_sem=wrecv.at[j, c],
            device_id=kid,
            device_id_type=MESH_ID,
        )

    @pl.when(q == 0)
    def _():
        for c in range(N_CHUNKS):
            narrow_step(c)
        panel_ref[...] = src_ref[...]

    @pl.when(q != 0)
    def _():
        narrow_step(0)

    for j, (active, is_root, parent, kids, depth) in enumerate(trees):
        root_here = jnp.logical_and(active, is_root)
        for c in range(W_CHUNKS):
            for k, (cond, kid) in enumerate(kids):
                @pl.when(jnp.logical_and(jnp.logical_and(root_here, cond), q == 0))
                def _():
                    wide_copy(src_ref.at[pl.ds(0, rows)], j, c, k, kid).start()

                @pl.when(jnp.logical_and(jnp.logical_and(root_here, cond), q != 0))
                def _():
                    wide_copy(panel_ref.at[pl.ds(0, rows)], j, c, k, kid).start()

        @pl.when(jnp.logical_and(root_here, q == 0))
        def _():
            blocks_ref[j] = src_ref[pl.ds(0, rows)]

        @pl.when(jnp.logical_and(root_here, q != 0))
        def _():
            blocks_ref[j] = panel_ref[pl.ds(0, rows)]

    for level in range(1, MAX_DEPTH + W_CHUNKS - 1):
        for c in range(W_CHUNKS):
            for j, (active, is_root, parent, kids, depth) in enumerate(trees):
                here = jnp.logical_and(jnp.logical_and(active, jnp.logical_not(is_root)), depth + c == level)

                @pl.when(here)
                def _():
                    wide_copy(blocks_ref.at[j], j, c, 0, (y, x, h, q)).wait_recv()

                for k, (cond, kid) in enumerate(kids):
                    @pl.when(jnp.logical_and(here, cond))
                    def _():
                        wide_copy(blocks_ref.at[j], j, c, k, kid).start()

        c = level - NARROW_LAG
        if 1 <= c < N_CHUNKS:
            @pl.when(q != 0)
            def _():
                narrow_step(c)

    for c in range(N_CHUNKS):
        for k, (cond, kid) in enumerate(n_kids):
            @pl.when(cond)
            def _():
                narrow_copy(panel_ref, c, k, kid).wait_send()

    for j, (active, is_root, parent, kids, depth) in enumerate(trees):
        for c in range(W_CHUNKS):
            for k, (cond, kid) in enumerate(kids):
                @pl.when(jnp.logical_and(active, cond))
                def _():
                    wide_copy(blocks_ref.at[j], j, c, k, kid).wait_send()


def broadcast(panel):
    rows = panel.shape[0] // N_CHUNKS
    vmem = pl.BlockSpec(memory_space=pltpu.VMEM)
    return pl.pallas_call(
        bcast_kernel,
        out_shape=(
            jax.ShapeDtypeStruct(panel.shape, panel.dtype),
            jax.ShapeDtypeStruct((N_BLOCKS, rows, panel.shape[1]), panel.dtype),
        ),
        in_specs=[vmem],
        out_specs=(vmem, vmem),
        scratch_shapes=[
            pltpu.SemaphoreType.DMA((N_CHUNKS, 2)),
            pltpu.SemaphoreType.DMA((N_CHUNKS,)),
            pltpu.SemaphoreType.DMA((N_BLOCKS, W_CHUNKS, N_SLOTS)),
            pltpu.SemaphoreType.DMA((N_BLOCKS, W_CHUNKS)),
        ],
        compiler_params=pltpu.CompilerParams(collective_id=0, has_side_effects=True),
    )(panel)


def mm_t(a, b):
    return lax.dot_general(
        a, b, (((1,), (1,)), ((), ())),
        precision=HIGHEST_PRECISION, preferred_element_type=jnp.float32,
    )


def mm(a, b):
    return jnp.dot(a, b, precision=HIGHEST_PRECISION, preferred_element_type=jnp.float32)


def newton_inverse(lower, start, steps):
    inverse = start
    for _ in range(steps):
        inverse = 2 * inverse - mm(inverse, mm(lower, inverse))
    return inverse


def diagonal_inverse(lower):
    n = lower.shape[0]
    on_diag = lax.broadcasted_iota(jnp.int32, (n, n), 0) == lax.broadcasted_iota(jnp.int32, (n, n), 1)
    diag = jnp.sum(jnp.where(on_diag, lower, 0.0), axis=1, keepdims=True)
    return jnp.where(on_diag, 1.0 / diag, 0.0)


def cholesky_and_inverse(symmetric):
    n = symmetric.shape[0]
    nb = n // BS
    work = symmetric
    cols = []
    block_inverses = []
    for b in range(nb):
        head = work[:BS, :BS]
        diag = jnp.tril(jnp.linalg.cholesky(head, symmetrize_input=False))
        inv = newton_inverse(diag, diagonal_inverse(diag), (BS - 1).bit_length())
        block_inverses.append(inv)
        if b + 1 < nb:
            below = mm_t(work[BS:, :BS], inv)
            work = work[BS:, BS:] - mm_t(below, below)
            cols.append(jnp.concatenate([jnp.zeros((b * BS, BS), jnp.float32), diag, below], 0))
        else:
            cols.append(jnp.concatenate([jnp.zeros((b * BS, BS), jnp.float32), diag], 0))
    factor = jnp.concatenate(cols, 1)
    start = jnp.zeros((n, n), jnp.float32)
    for b in range(nb):
        start = lax.dynamic_update_slice(start, block_inverses[b], (b * BS, b * BS))
    inverse = newton_inverse(factor, start, max(1, (nb - 1).bit_length()))
    return factor, inverse


def shards(front, child_update, child_map):
    wide_count = lax.axis_size(WIDE)
    narrow_count = lax.axis_size("narrow")
    wide_index = lax.axis_index(WIDE)
    narrow_index = lax.axis_index("narrow")
    half_count = wide_count // 2
    local_rows, local_cols = front.shape
    front_slots = local_rows // BS
    block_total = front_slots * wide_count
    child_side = wide_index // half_count
    row_local = jnp.arange(local_rows, dtype=jnp.int32)
    global_row = (row_local // BS * wide_count + wide_index) * BS + row_local % BS
    col_local = jnp.arange(local_cols, dtype=jnp.int32)
    global_col = (col_local // PW * narrow_count + narrow_index) * PW + col_local % PW
    groups = child_update.reshape(2, front_slots, BS, local_cols)
    leaving = lax.dynamic_index_in_dim(groups, 1 - child_side, 0, keepdims=False)
    arrived = from_partner(leaving, WIDE, half_count.bit_length() - 1)

    def named_cols(side):
        names = lax.dynamic_slice_in_dim(child_map, side * block_total, block_total)
        return jnp.any(names[:, None] == (global_col // BS)[None, :], axis=0)

    kept_rows = lax.dynamic_index_in_dim(groups, child_side, 0, keepdims=False)
    kept_rows = jnp.where(named_cols(child_side)[None, None, :], kept_rows, 0.0)
    arrived = jnp.where(named_cols(1 - child_side)[None, None, :], arrived, 0.0)
    partner = (wide_index + half_count) % wide_count
    own_map = lax.dynamic_slice_in_dim(
        child_map, (wide_index * 2 + child_side) * front_slots, front_slots
    )
    got_map = lax.dynamic_slice_in_dim(
        child_map, (partner * 2 + child_side) * front_slots, front_slots
    )
    target = wide_index + wide_count * jnp.arange(front_slots, dtype=jnp.int32)
    own_select = (own_map[None, :] == target[:, None]).astype(jnp.float32)
    got_select = (got_map[None, :] == target[:, None]).astype(jnp.float32)
    own_part = jnp.dot(
        own_select,
        kept_rows.reshape(front_slots, BS * local_cols),
        precision=HIGHEST_PRECISION,
        preferred_element_type=jnp.float32,
    )
    got_part = jnp.dot(
        got_select,
        arrived.reshape(front_slots, BS * local_cols),
        precision=HIGHEST_PRECISION,
        preferred_element_type=jnp.float32,
    )
    matrix = front + (own_part + got_part).reshape(local_rows, local_cols)

    panel, blocks = broadcast(matrix)
    diag_block = blocks[: N_BLOCKS // 2].reshape(PW, PW)
    diag_block = jnp.where(
        lax.broadcasted_iota(jnp.int32, (PW, PW), 1) < (lax.broadcasted_iota(jnp.int32, (PW, PW), 0) // BS + 1) * BS,
        diag_block,
        0.0,
    )
    col_rows = blocks[N_BLOCKS // 2 :].reshape(PW, PW)

    factor_diag, inverse = cholesky_and_inverse(diag_block)
    own_factor = mm_t(panel, inverse)
    diag_rows = lax.dynamic_slice_in_dim(factor_diag, jnp.minimum(wide_index, 3) * BS, BS)
    top = jnp.where(wide_index * BS < PW, diag_rows, own_factor[:BS])
    own_factor = jnp.concatenate([top, own_factor[BS:]], 0)
    col_factor = mm_t(col_rows, inverse)
    update = mm_t(own_factor, col_factor)
    renewed = jnp.where(narrow_index == 0, own_factor, matrix - update)
    on_or_below = global_row[:, None] >= global_col[None, :]
    return jnp.where(on_or_below, renewed, jnp.zeros_like(renewed))


def solution(mesh):
    torus = Mesh(
        mesh.devices.reshape(8, 4, 2, mesh.shape["narrow"]),
        AXES,
    )
    placed = (P(WIDE, "narrow"), P(WIDE, "narrow"), P())
    return jax.shard_map(
        shards, mesh=torus, in_specs=placed, out_specs=P(WIDE, "narrow"), check_vma=False
    )
```

```python
import functools

import jax
import jax.numpy as jnp
from jax import lax
from jax.experimental import pallas as pl
from jax.experimental.pallas import tpu as pltpu
from jax.sharding import Mesh
from jax.sharding import PartitionSpec as P

BS = 128
PW = 512
WIDE = ("wide_0", "wide_1", "wide_2")
AXES = ("wide_0", "wide_1", "wide_2", "narrow")
MESH_ID = pl.DeviceIdType.MESH

HIGHEST_PRECISION = lax.Precision.HIGHEST


def from_partner(value, axis, distance):
    return lax.ppermute(value, axis, [(i, i ^ 1 << distance) for i in range(lax.axis_size(axis))])


def positions():
    return tuple(lax.axis_index(a) for a in AXES)


def narrow_tree(q, n):
    even = q % 2 == 0
    parent = jnp.where(even, q - 2, q - 1)
    kids = [(even, q + 1), (jnp.logical_and(even, q + 2 < n), q + 2)]
    return q > 0, parent, kids


def wide_tree(y, x, h, root, ny, nx):
    y0 = root // (2 * nx)
    x0 = (root // 2) % nx
    h0 = root % 2
    dy = (y - y0 + ny) % ny
    dx = (x - x0 + nx) % nx
    dh = (h - h0 + 2) % 2
    half = ny // 2
    at_y0 = dy == 0
    at_x0 = jnp.logical_and(at_y0, dx == 0)
    is_root = jnp.logical_and(at_x0, dh == 0)
    up = jnp.logical_and(dy >= 1, dy <= half)
    py = jnp.where(up, (y + ny - 1) % ny, (y + 1) % ny)
    px = jnp.where(dx == 2, (x + nx - 1) % nx, x0)
    parent_y = jnp.where(at_y0, y, py)
    parent_x = jnp.where(jnp.logical_and(at_y0, dx != 0), px, x)
    parent_h = jnp.where(at_x0, h0, h)
    parent = (parent_y, parent_x, parent_h)
    kids = [
        (is_root, (y, x, 1 - h)),
        (at_x0, (y, (x + 1) % nx, h)),
        (at_x0, (y, (x + nx - 1) % nx, h)),
        (jnp.logical_and(at_y0, dx == 1), (y, (x + 1) % nx, h)),
        (dy < half, ((y + 1) % ny, x, h)),
        (jnp.logical_or(at_y0, dy > half + 1), ((y + ny - 1) % ny, x, h)),
    ]
    x_depth = jnp.where(dx == 0, 0, jnp.where(dx == 2, 2, 1))
    y_depth = jnp.where(dy <= half, dy, ny - dy)
    return is_root, parent, kids, dh + x_depth + y_depth


N_CHUNKS = 4
N_BLOCKS = 8
N_SLOTS = 7
MAX_DEPTH = 9
NARROW_LAG = 0
W_CHUNKS = 2


def bcast_kernel(src_ref, panel_ref, blocks_ref, nsend, nrecv, wsend, wrecv):
    y, x, h, q = positions()
    n = lax.axis_size("narrow")
    ny = lax.axis_size("wide_0")
    nx = lax.axis_size("wide_1")
    rows = panel_ref.shape[0] // N_CHUNKS
    even = q % 2 == 0
    n_has_parent, n_parent, n_kids = narrow_tree(q, n)

    trees = []
    for j in range(N_BLOCKS):
        if j < N_BLOCKS // 2:
            is_root, parent, kids, depth = wide_tree(y, x, h, j, ny, nx)
            active = q >= 0
            parent = tuple(jnp.where(even, p, o) for p, o in zip((*parent, q), (y, x, h, q - 1)))
            kids = [(jnp.logical_and(even, c), (*k, q)) for c, k in kids]
            kids.append((even, (y, x, h, q + 1)))
            is_root = jnp.logical_and(even, is_root)
            depth = depth + 1 - even.astype(jnp.int32)
        else:
            root = 4 * q + (j - N_BLOCKS // 2)
            is_root, parent, kids, depth = wide_tree(y, x, h, root, ny, nx)
            active = q > 0
            parent = (*parent, q)
            kids = [(c, (*k, q)) for c, k in kids]
            kids.append((q < 0, (y, x, h, q)))
        trees.append((active, is_root, parent, kids, depth))

    barrier = pltpu.get_barrier_semaphore()

    @pl.when(n_has_parent)
    def _():
        pl.semaphore_signal(barrier, 1, device_id=(y, x, h, n_parent), device_id_type=MESH_ID)

    peers = n_has_parent.astype(jnp.int32)
    for cond, kid in n_kids:
        peers = peers + cond.astype(jnp.int32)

        @pl.when(cond)
        def _():
            pl.semaphore_signal(barrier, 1, device_id=(y, x, h, kid), device_id_type=MESH_ID)

    for active, is_root, parent, kids, depth in trees:
        has_parent = jnp.logical_and(active, jnp.logical_not(is_root))
        peers = peers + has_parent.astype(jnp.int32)

        @pl.when(has_parent)
        def _():
            pl.semaphore_signal(barrier, 1, device_id=parent, device_id_type=MESH_ID)

        for cond, kid in kids:
            go = jnp.logical_and(active, cond)
            peers = peers + go.astype(jnp.int32)

            @pl.when(go)
            def _():
                pl.semaphore_signal(barrier, 1, device_id=kid, device_id_type=MESH_ID)

    pl.semaphore_wait(barrier, peers)

    def narrow_copy(src, c, k, kid):
        part = pl.ds(c * rows, rows)
        return pltpu.make_async_remote_copy(
            src_ref=src.at[part],
            dst_ref=panel_ref.at[part],
            send_sem=nsend.at[c, k],
            recv_sem=nrecv.at[c],
            device_id=(y, x, h, kid),
            device_id_type=MESH_ID,
        )

    def narrow_step(c):
        @pl.when(n_has_parent)
        def _():
            narrow_copy(panel_ref, c, 0, q).wait_recv()

        for k, (cond, kid) in enumerate(n_kids):
            @pl.when(jnp.logical_and(cond, q == 0))
            def _():
                narrow_copy(src_ref, c, k, kid).start()

            @pl.when(jnp.logical_and(cond, q != 0))
            def _():
                narrow_copy(panel_ref, c, k, kid).start()

    piece = rows // W_CHUNKS

    def wide_copy(src, j, c, k, kid):
        part = pl.ds(c * piece, piece)
        cols = pl.ds(0, (j + 1) * rows if j < N_BLOCKS // 2 else src.shape[1])
        return pltpu.make_async_remote_copy(
            src_ref=src.at[part, cols],
            dst_ref=blocks_ref.at[j, part, cols],
            send_sem=wsend.at[j, c, k],
            recv_sem=wrecv.at[j, c],
            device_id=kid,
            device_id_type=MESH_ID,
        )

    @pl.when(q == 0)
    def _():
        for c in range(N_CHUNKS):
            narrow_step(c)
        panel_ref[...] = src_ref[...]

    @pl.when(q != 0)
    def _():
        narrow_step(0)

    for j, (active, is_root, parent, kids, depth) in enumerate(trees):
        root_here = jnp.logical_and(active, is_root)
        for c in range(W_CHUNKS):
            for k, (cond, kid) in enumerate(kids):
                @pl.when(jnp.logical_and(jnp.logical_and(root_here, cond), q == 0))
                def _():
                    wide_copy(src_ref.at[pl.ds(0, rows)], j, c, k, kid).start()

                @pl.when(jnp.logical_and(jnp.logical_and(root_here, cond), q != 0))
                def _():
                    wide_copy(panel_ref.at[pl.ds(0, rows)], j, c, k, kid).start()

        @pl.when(jnp.logical_and(root_here, q == 0))
        def _():
            blocks_ref[j] = src_ref[pl.ds(0, rows)]

        @pl.when(jnp.logical_and(root_here, q != 0))
        def _():
            blocks_ref[j] = panel_ref[pl.ds(0, rows)]

    for level in range(1, MAX_DEPTH + W_CHUNKS - 1):
        for c in range(W_CHUNKS):
            for j, (active, is_root, parent, kids, depth) in enumerate(trees):
                here = jnp.logical_and(jnp.logical_and(active, jnp.logical_not(is_root)), depth + c == level)

                @pl.when(here)
                def _():
                    wide_copy(blocks_ref.at[j], j, c, 0, (y, x, h, q)).wait_recv()

                for k, (cond, kid) in enumerate(kids):
                    @pl.when(jnp.logical_and(here, cond))
                    def _():
                        wide_copy(blocks_ref.at[j], j, c, k, kid).start()

        c = level - NARROW_LAG
        if 1 <= c < N_CHUNKS:
            @pl.when(q != 0)
            def _():
                narrow_step(c)

    for c in range(N_CHUNKS):
        for k, (cond, kid) in enumerate(n_kids):
            @pl.when(cond)
            def _():
                narrow_copy(panel_ref, c, k, kid).wait_send()

    for j, (active, is_root, parent, kids, depth) in enumerate(trees):
        for c in range(W_CHUNKS):
            for k, (cond, kid) in enumerate(kids):
                @pl.when(jnp.logical_and(active, cond))
                def _():
                    wide_copy(blocks_ref.at[j], j, c, k, kid).wait_send()


def broadcast(panel):
    rows = panel.shape[0] // N_CHUNKS
    vmem = pl.BlockSpec(memory_space=pltpu.VMEM)
    return pl.pallas_call(
        bcast_kernel,
        out_shape=(
            jax.ShapeDtypeStruct(panel.shape, panel.dtype),
            jax.ShapeDtypeStruct((N_BLOCKS, rows, panel.shape[1]), panel.dtype),
        ),
        in_specs=[vmem],
        out_specs=(vmem, vmem),
        scratch_shapes=[
            pltpu.SemaphoreType.DMA((N_CHUNKS, 2)),
            pltpu.SemaphoreType.DMA((N_CHUNKS,)),
            pltpu.SemaphoreType.DMA((N_BLOCKS, W_CHUNKS, N_SLOTS)),
            pltpu.SemaphoreType.DMA((N_BLOCKS, W_CHUNKS)),
        ],
        compiler_params=pltpu.CompilerParams(collective_id=0, has_side_effects=True),
    )(panel)


def mm_t(a, b):
    return lax.dot_general(
        a, b, (((1,), (1,)), ((), ())),
        precision=HIGHEST_PRECISION, preferred_element_type=jnp.float32,
    )


def mm(a, b):
    return jnp.dot(a, b, precision=HIGHEST_PRECISION, preferred_element_type=jnp.float32)


def newton_inverse(lower, start, steps):
    inverse = start
    for _ in range(steps):
        inverse = 2 * inverse - mm(inverse, mm(lower, inverse))
    return inverse


def diagonal_inverse(lower):
    n = lower.shape[0]
    on_diag = lax.broadcasted_iota(jnp.int32, (n, n), 0) == lax.broadcasted_iota(jnp.int32, (n, n), 1)
    diag = jnp.sum(jnp.where(on_diag, lower, 0.0), axis=1, keepdims=True)
    return jnp.where(on_diag, 1.0 / diag, 0.0)


def cholesky_and_inverse(symmetric):
    n = symmetric.shape[0]
    nb = n // BS
    work = symmetric
    cols = []
    block_inverses = []
    for b in range(nb):
        head = work[:BS, :BS]
        diag = jnp.tril(jnp.linalg.cholesky(head, symmetrize_input=False))
        inv = newton_inverse(diag, diagonal_inverse(diag), (BS - 1).bit_length())
        block_inverses.append(inv)
        if b + 1 < nb:
            below = mm_t(work[BS:, :BS], inv)
            work = work[BS:, BS:] - mm_t(below, below)
            cols.append(jnp.concatenate([jnp.zeros((b * BS, BS), jnp.float32), diag, below], 0))
        else:
            cols.append(jnp.concatenate([jnp.zeros((b * BS, BS), jnp.float32), diag], 0))
    factor = jnp.concatenate(cols, 1)
    start = jnp.zeros((n, n), jnp.float32)
    for b in range(nb):
        start = lax.dynamic_update_slice(start, block_inverses[b], (b * BS, b * BS))
    inverse = newton_inverse(factor, start, max(1, (nb - 1).bit_length()))
    return factor, inverse


def shards(front, child_update, child_map):
    wide_count = lax.axis_size(WIDE)
    narrow_count = lax.axis_size("narrow")
    wide_index = lax.axis_index(WIDE)
    narrow_index = lax.axis_index("narrow")
    half_count = wide_count // 2
    local_rows, local_cols = front.shape
    front_slots = local_rows // BS
    block_total = front_slots * wide_count
    child_side = wide_index // half_count
    row_local = jnp.arange(local_rows, dtype=jnp.int32)
    global_row = (row_local // BS * wide_count + wide_index) * BS + row_local % BS
    col_local = jnp.arange(local_cols, dtype=jnp.int32)
    global_col = (col_local // PW * narrow_count + narrow_index) * PW + col_local % PW
    groups = child_update.reshape(2, front_slots, BS, local_cols)
    leaving = lax.dynamic_index_in_dim(groups, 1 - child_side, 0, keepdims=False)
    arrived = from_partner(leaving, WIDE, half_count.bit_length() - 1)

    def named_cols(side):
        names = lax.dynamic_slice_in_dim(child_map, side * block_total, block_total)
        return jnp.any(names[:, None] == (global_col // BS)[None, :], axis=0)

    kept_rows = lax.dynamic_index_in_dim(groups, child_side, 0, keepdims=False)
    kept_rows = jnp.where(named_cols(child_side)[None, None, :], kept_rows, 0.0)
    arrived = jnp.where(named_cols(1 - child_side)[None, None, :], arrived, 0.0)
    partner = (wide_index + half_count) % wide_count
    own_map = lax.dynamic_slice_in_dim(
        child_map, (wide_index * 2 + child_side) * front_slots, front_slots
    )
    got_map = lax.dynamic_slice_in_dim(
        child_map, (partner * 2 + child_side) * front_slots, front_slots
    )
    target = wide_index + wide_count * jnp.arange(front_slots, dtype=jnp.int32)
    own_select = (own_map[None, :] == target[:, None]).astype(jnp.float32)
    got_select = (got_map[None, :] == target[:, None]).astype(jnp.float32)
    own_part = jnp.dot(
        own_select,
        kept_rows.reshape(front_slots, BS * local_cols),
        precision=HIGHEST_PRECISION,
        preferred_element_type=jnp.float32,
    )
    got_part = jnp.dot(
        got_select,
        arrived.reshape(front_slots, BS * local_cols),
        precision=HIGHEST_PRECISION,
        preferred_element_type=jnp.float32,
    )
    matrix = front + (own_part + got_part).reshape(local_rows, local_cols)

    panel, blocks = broadcast(matrix)
    diag_block = blocks[: N_BLOCKS // 2].reshape(PW, PW)
    diag_block = jnp.where(
        lax.broadcasted_iota(jnp.int32, (PW, PW), 1) < (lax.broadcasted_iota(jnp.int32, (PW, PW), 0) // BS + 1) * BS,
        diag_block,
        0.0,
    )
    col_rows = blocks[N_BLOCKS // 2 :].reshape(PW, PW)

    factor_diag, inverse = cholesky_and_inverse(diag_block)
    own_factor = mm_t(panel, inverse)
    diag_rows = lax.dynamic_slice_in_dim(factor_diag, jnp.minimum(wide_index, 3) * BS, BS)
    top = jnp.where(wide_index * BS < PW, diag_rows, own_factor[:BS])
    own_factor = jnp.concatenate([top, own_factor[BS:]], 0)
    col_factor = mm_t(col_rows, inverse)
    update = mm_t(own_factor, col_factor)
    renewed = jnp.where(narrow_index == 0, own_factor, matrix - update)
    on_or_below = global_row[:, None] >= global_col[None, :]
    return jnp.where(on_or_below, renewed, jnp.zeros_like(renewed))


def solution(mesh):
    torus = Mesh(
        mesh.devices.reshape(8, 4, 2, mesh.shape["narrow"]),
        AXES,
    )
    placed = (P(WIDE, "narrow"), P(WIDE, "narrow"), P())
    return jax.shard_map(
        shards, mesh=torus, in_specs=placed, out_specs=P(WIDE, "narrow"), check_vma=False
    )
```

```python
import functools

import jax
import jax.numpy as jnp
from jax import lax
from jax.experimental import pallas as pl
from jax.experimental.pallas import tpu as pltpu
from jax.sharding import Mesh
from jax.sharding import PartitionSpec as P

BS = 128
PW = 512
WIDE = ("wide_0", "wide_1", "wide_2")
AXES = ("wide_0", "wide_1", "wide_2", "narrow")
MESH_ID = pl.DeviceIdType.MESH

HIGHEST_PRECISION = lax.Precision.HIGHEST


def from_partner(value, axis, distance):
    return lax.ppermute(value, axis, [(i, i ^ 1 << distance) for i in range(lax.axis_size(axis))])


def positions():
    return tuple(lax.axis_index(a) for a in AXES)


def narrow_tree(q, n):
    even = q % 2 == 0
    parent = jnp.where(even, q - 2, q - 1)
    kids = [(even, q + 1), (jnp.logical_and(even, q + 2 < n), q + 2)]
    return q > 0, parent, kids


def wide_tree(y, x, h, root, ny, nx):
    y0 = root // (2 * nx)
    x0 = (root // 2) % nx
    h0 = root % 2
    dy = (y - y0 + ny) % ny
    dx = (x - x0 + nx) % nx
    dh = (h - h0 + 2) % 2
    half = ny // 2
    at_y0 = dy == 0
    at_x0 = jnp.logical_and(at_y0, dx == 0)
    is_root = jnp.logical_and(at_x0, dh == 0)
    up = jnp.logical_and(dy >= 1, dy <= half)
    py = jnp.where(up, (y + ny - 1) % ny, (y + 1) % ny)
    px = jnp.where(dx == 2, (x + nx - 1) % nx, x0)
    parent_y = jnp.where(at_y0, y, py)
    parent_x = jnp.where(jnp.logical_and(at_y0, dx != 0), px, x)
    parent_h = jnp.where(at_x0, h0, h)
    parent = (parent_y, parent_x, parent_h)
    kids = [
        (is_root, (y, x, 1 - h)),
        (at_x0, (y, (x + 1) % nx, h)),
        (at_x0, (y, (x + nx - 1) % nx, h)),
        (jnp.logical_and(at_y0, dx == 1), (y, (x + 1) % nx, h)),
        (dy < half, ((y + 1) % ny, x, h)),
        (jnp.logical_or(at_y0, dy > half + 1), ((y + ny - 1) % ny, x, h)),
    ]
    x_depth = jnp.where(dx == 0, 0, jnp.where(dx == 2, 2, 1))
    y_depth = jnp.where(dy <= half, dy, ny - dy)
    return is_root, parent, kids, dh + x_depth + y_depth


N_CHUNKS = 4
N_BLOCKS = 8
N_SLOTS = 7
MAX_DEPTH = 9
NARROW_LAG = 1
W_CHUNKS = 4


def bcast_kernel(src_ref, panel_ref, blocks_ref, nsend, nrecv, wsend, wrecv):
    y, x, h, q = positions()
    n = lax.axis_size("narrow")
    ny = lax.axis_size("wide_0")
    nx = lax.axis_size("wide_1")
    rows = panel_ref.shape[0] // N_CHUNKS
    even = q % 2 == 0
    n_has_parent, n_parent, n_kids = narrow_tree(q, n)

    trees = []
    for j in range(N_BLOCKS):
        if j < N_BLOCKS // 2:
            is_root, parent, kids, depth = wide_tree(y, x, h, j, ny, nx)
            active = q >= 0
            parent = tuple(jnp.where(even, p, o) for p, o in zip((*parent, q), (y, x, h, q - 1)))
            kids = [(jnp.logical_and(even, c), (*k, q)) for c, k in kids]
            kids.append((even, (y, x, h, q + 1)))
            is_root = jnp.logical_and(even, is_root)
            depth = depth + 1 - even.astype(jnp.int32)
        else:
            root = 4 * q + (j - N_BLOCKS // 2)
            is_root, parent, kids, depth = wide_tree(y, x, h, root, ny, nx)
            active = q > 0
            parent = (*parent, q)
            kids = [(c, (*k, q)) for c, k in kids]
            kids.append((q < 0, (y, x, h, q)))
        trees.append((active, is_root, parent, kids, depth))

    barrier = pltpu.get_barrier_semaphore()

    @pl.when(n_has_parent)
    def _():
        pl.semaphore_signal(barrier, 1, device_id=(y, x, h, n_parent), device_id_type=MESH_ID)

    peers = n_has_parent.astype(jnp.int32)
    for cond, kid in n_kids:
        peers = peers + cond.astype(jnp.int32)

        @pl.when(cond)
        def _():
            pl.semaphore_signal(barrier, 1, device_id=(y, x, h, kid), device_id_type=MESH_ID)

    for active, is_root, parent, kids, depth in trees:
        has_parent = jnp.logical_and(active, jnp.logical_not(is_root))
        peers = peers + has_parent.astype(jnp.int32)

        @pl.when(has_parent)
        def _():
            pl.semaphore_signal(barrier, 1, device_id=parent, device_id_type=MESH_ID)

        for cond, kid in kids:
            go = jnp.logical_and(active, cond)
            peers = peers + go.astype(jnp.int32)

            @pl.when(go)
            def _():
                pl.semaphore_signal(barrier, 1, device_id=kid, device_id_type=MESH_ID)

    pl.semaphore_wait(barrier, peers)

    def narrow_copy(src, c, k, kid):
        part = pl.ds(c * rows, rows)
        return pltpu.make_async_remote_copy(
            src_ref=src.at[part],
            dst_ref=panel_ref.at[part],
            send_sem=nsend.at[c, k],
            recv_sem=nrecv.at[c],
            device_id=(y, x, h, kid),
            device_id_type=MESH_ID,
        )

    def narrow_step(c):
        @pl.when(n_has_parent)
        def _():
            narrow_copy(panel_ref, c, 0, q).wait_recv()

        for k, (cond, kid) in enumerate(n_kids):
            @pl.when(jnp.logical_and(cond, q == 0))
            def _():
                narrow_copy(src_ref, c, k, kid).start()

            @pl.when(jnp.logical_and(cond, q != 0))
            def _():
                narrow_copy(panel_ref, c, k, kid).start()

    piece = rows // W_CHUNKS

    def wide_copy(src, j, c, k, kid):
        part = pl.ds(c * piece, piece)
        cols = pl.ds(0, (j + 1) * rows if j < N_BLOCKS // 2 else src.shape[1])
        return pltpu.make_async_remote_copy(
            src_ref=src.at[part, cols],
            dst_ref=blocks_ref.at[j, part, cols],
            send_sem=wsend.at[j, c, k],
            recv_sem=wrecv.at[j, c],
            device_id=kid,
            device_id_type=MESH_ID,
        )

    @pl.when(q == 0)
    def _():
        for c in range(N_CHUNKS):
            narrow_step(c)
        panel_ref[...] = src_ref[...]

    @pl.when(q != 0)
    def _():
        narrow_step(0)

    for j, (active, is_root, parent, kids, depth) in enumerate(trees):
        root_here = jnp.logical_and(active, is_root)
        for c in range(W_CHUNKS):
            for k, (cond, kid) in enumerate(kids):
                @pl.when(jnp.logical_and(jnp.logical_and(root_here, cond), q == 0))
                def _():
                    wide_copy(src_ref.at[pl.ds(0, rows)], j, c, k, kid).start()

                @pl.when(jnp.logical_and(jnp.logical_and(root_here, cond), q != 0))
                def _():
                    wide_copy(panel_ref.at[pl.ds(0, rows)], j, c, k, kid).start()

        @pl.when(jnp.logical_and(root_here, q == 0))
        def _():
            blocks_ref[j] = src_ref[pl.ds(0, rows)]

        @pl.when(jnp.logical_and(root_here, q != 0))
        def _():
            blocks_ref[j] = panel_ref[pl.ds(0, rows)]

    for level in range(1, MAX_DEPTH + W_CHUNKS - 1):
        for c in range(W_CHUNKS):
            for j, (active, is_root, parent, kids, depth) in enumerate(trees):
                here = jnp.logical_and(jnp.logical_and(active, jnp.logical_not(is_root)), depth + c == level)

                @pl.when(here)
                def _():
                    wide_copy(blocks_ref.at[j], j, c, 0, (y, x, h, q)).wait_recv()

                for k, (cond, kid) in enumerate(kids):
                    @pl.when(jnp.logical_and(here, cond))
                    def _():
                        wide_copy(blocks_ref.at[j], j, c, k, kid).start()

        c = level - NARROW_LAG
        if 1 <= c < N_CHUNKS:
            @pl.when(q != 0)
            def _():
                narrow_step(c)

    for c in range(N_CHUNKS):
        for k, (cond, kid) in enumerate(n_kids):
            @pl.when(cond)
            def _():
                narrow_copy(panel_ref, c, k, kid).wait_send()

    for j, (active, is_root, parent, kids, depth) in enumerate(trees):
        for c in range(W_CHUNKS):
            for k, (cond, kid) in enumerate(kids):
                @pl.when(jnp.logical_and(active, cond))
                def _():
                    wide_copy(blocks_ref.at[j], j, c, k, kid).wait_send()


def broadcast(panel):
    rows = panel.shape[0] // N_CHUNKS
    vmem = pl.BlockSpec(memory_space=pltpu.VMEM)
    return pl.pallas_call(
        bcast_kernel,
        out_shape=(
            jax.ShapeDtypeStruct(panel.shape, panel.dtype),
            jax.ShapeDtypeStruct((N_BLOCKS, rows, panel.shape[1]), panel.dtype),
        ),
        in_specs=[vmem],
        out_specs=(vmem, vmem),
        scratch_shapes=[
            pltpu.SemaphoreType.DMA((N_CHUNKS, 2)),
            pltpu.SemaphoreType.DMA((N_CHUNKS,)),
            pltpu.SemaphoreType.DMA((N_BLOCKS, W_CHUNKS, N_SLOTS)),
            pltpu.SemaphoreType.DMA((N_BLOCKS, W_CHUNKS)),
        ],
        compiler_params=pltpu.CompilerParams(collective_id=0, has_side_effects=True),
    )(panel)


def mm_t(a, b):
    return lax.dot_general(
        a, b, (((1,), (1,)), ((), ())),
        precision=HIGHEST_PRECISION, preferred_element_type=jnp.float32,
    )


def mm(a, b):
    return jnp.dot(a, b, precision=HIGHEST_PRECISION, preferred_element_type=jnp.float32)


def newton_inverse(lower, start, steps):
    inverse = start
    for _ in range(steps):
        inverse = 2 * inverse - mm(inverse, mm(lower, inverse))
    return inverse


def diagonal_inverse(lower):
    n = lower.shape[0]
    on_diag = lax.broadcasted_iota(jnp.int32, (n, n), 0) == lax.broadcasted_iota(jnp.int32, (n, n), 1)
    diag = jnp.sum(jnp.where(on_diag, lower, 0.0), axis=1, keepdims=True)
    return jnp.where(on_diag, 1.0 / diag, 0.0)


def cholesky_and_inverse(symmetric):
    n = symmetric.shape[0]
    nb = n // BS
    work = symmetric
    cols = []
    block_inverses = []
    for b in range(nb):
        head = work[:BS, :BS]
        diag = jnp.tril(jnp.linalg.cholesky(head, symmetrize_input=False))
        inv = newton_inverse(diag, diagonal_inverse(diag), (BS - 1).bit_length())
        block_inverses.append(inv)
        if b + 1 < nb:
            below = mm_t(work[BS:, :BS], inv)
            work = work[BS:, BS:] - mm_t(below, below)
            cols.append(jnp.concatenate([jnp.zeros((b * BS, BS), jnp.float32), diag, below], 0))
        else:
            cols.append(jnp.concatenate([jnp.zeros((b * BS, BS), jnp.float32), diag], 0))
    factor = jnp.concatenate(cols, 1)
    start = jnp.zeros((n, n), jnp.float32)
    for b in range(nb):
        start = lax.dynamic_update_slice(start, block_inverses[b], (b * BS, b * BS))
    inverse = newton_inverse(factor, start, max(1, (nb - 1).bit_length()))
    return factor, inverse


def shards(front, child_update, child_map):
    wide_count = lax.axis_size(WIDE)
    narrow_count = lax.axis_size("narrow")
    wide_index = lax.axis_index(WIDE)
    narrow_index = lax.axis_index("narrow")
    half_count = wide_count // 2
    local_rows, local_cols = front.shape
    front_slots = local_rows // BS
    block_total = front_slots * wide_count
    child_side = wide_index // half_count
    row_local = jnp.arange(local_rows, dtype=jnp.int32)
    global_row = (row_local // BS * wide_count + wide_index) * BS + row_local % BS
    col_local = jnp.arange(local_cols, dtype=jnp.int32)
    global_col = (col_local // PW * narrow_count + narrow_index) * PW + col_local % PW
    groups = child_update.reshape(2, front_slots, BS, local_cols)
    leaving = lax.dynamic_index_in_dim(groups, 1 - child_side, 0, keepdims=False)
    arrived = from_partner(leaving, WIDE, half_count.bit_length() - 1)

    def named_cols(side):
        names = lax.dynamic_slice_in_dim(child_map, side * block_total, block_total)
        return jnp.any(names[:, None] == (global_col // BS)[None, :], axis=0)

    kept_rows = lax.dynamic_index_in_dim(groups, child_side, 0, keepdims=False)
    kept_rows = jnp.where(named_cols(child_side)[None, None, :], kept_rows, 0.0)
    arrived = jnp.where(named_cols(1 - child_side)[None, None, :], arrived, 0.0)
    partner = (wide_index + half_count) % wide_count
    own_map = lax.dynamic_slice_in_dim(
        child_map, (wide_index * 2 + child_side) * front_slots, front_slots
    )
    got_map = lax.dynamic_slice_in_dim(
        child_map, (partner * 2 + child_side) * front_slots, front_slots
    )
    target = wide_index + wide_count * jnp.arange(front_slots, dtype=jnp.int32)
    own_select = (own_map[None, :] == target[:, None]).astype(jnp.float32)
    got_select = (got_map[None, :] == target[:, None]).astype(jnp.float32)
    own_part = jnp.dot(
        own_select,
        kept_rows.reshape(front_slots, BS * local_cols),
        precision=HIGHEST_PRECISION,
        preferred_element_type=jnp.float32,
    )
    got_part = jnp.dot(
        got_select,
        arrived.reshape(front_slots, BS * local_cols),
        precision=HIGHEST_PRECISION,
        preferred_element_type=jnp.float32,
    )
    matrix = front + (own_part + got_part).reshape(local_rows, local_cols)

    panel, blocks = broadcast(matrix)
    diag_block = blocks[: N_BLOCKS // 2].reshape(PW, PW)
    diag_block = jnp.where(
        lax.broadcasted_iota(jnp.int32, (PW, PW), 1) < (lax.broadcasted_iota(jnp.int32, (PW, PW), 0) // BS + 1) * BS,
        diag_block,
        0.0,
    )
    col_rows = blocks[N_BLOCKS // 2 :].reshape(PW, PW)

    factor_diag, inverse = cholesky_and_inverse(diag_block)
    own_factor = mm_t(panel, inverse)
    diag_rows = lax.dynamic_slice_in_dim(factor_diag, jnp.minimum(wide_index, 3) * BS, BS)
    top = jnp.where(wide_index * BS < PW, diag_rows, own_factor[:BS])
    own_factor = jnp.concatenate([top, own_factor[BS:]], 0)
    col_factor = mm_t(col_rows, inverse)
    update = mm_t(own_factor, col_factor)
    renewed = jnp.where(narrow_index == 0, own_factor, matrix - update)
    on_or_below = global_row[:, None] >= global_col[None, :]
    return jnp.where(on_or_below, renewed, jnp.zeros_like(renewed))


def solution(mesh):
    torus = Mesh(
        mesh.devices.reshape(8, 4, 2, mesh.shape["narrow"]),
        AXES,
    )
    placed = (P(WIDE, "narrow"), P(WIDE, "narrow"), P())
    return jax.shard_map(
        shards, mesh=torus, in_specs=placed, out_specs=P(WIDE, "narrow"), check_vma=False
    )
```

```python
import functools

import jax
import jax.numpy as jnp
from jax import lax
from jax.experimental import pallas as pl
from jax.experimental.pallas import tpu as pltpu
from jax.sharding import Mesh
from jax.sharding import PartitionSpec as P

BS = 128
PW = 512
WIDE = ("wide_0", "wide_1", "wide_2")
AXES = ("wide_0", "wide_1", "wide_2", "narrow")
MESH_ID = pl.DeviceIdType.MESH

HIGHEST_PRECISION = lax.Precision.HIGHEST


def from_partner(value, axis, distance):
    return lax.ppermute(value, axis, [(i, i ^ 1 << distance) for i in range(lax.axis_size(axis))])


def positions():
    return tuple(lax.axis_index(a) for a in AXES)


def narrow_tree(q, n):
    even = q % 2 == 0
    parent = jnp.where(even, q - 2, q - 1)
    kids = [(even, q + 1), (jnp.logical_and(even, q + 2 < n), q + 2)]
    return q > 0, parent, kids


def wide_tree(y, x, h, root, ny, nx):
    y0 = root // (2 * nx)
    x0 = (root // 2) % nx
    h0 = root % 2
    dy = (y - y0 + ny) % ny
    dx = (x - x0 + nx) % nx
    dh = (h - h0 + 2) % 2
    half = ny // 2
    at_y0 = dy == 0
    at_x0 = jnp.logical_and(at_y0, dx == 0)
    is_root = jnp.logical_and(at_x0, dh == 0)
    up = jnp.logical_and(dy >= 1, dy <= half)
    py = jnp.where(up, (y + ny - 1) % ny, (y + 1) % ny)
    px = jnp.where(dx == 2, (x + nx - 1) % nx, x0)
    parent_y = jnp.where(at_y0, y, py)
    parent_x = jnp.where(jnp.logical_and(at_y0, dx != 0), px, x)
    parent_h = jnp.where(at_x0, h0, h)
    parent = (parent_y, parent_x, parent_h)
    kids = [
        (is_root, (y, x, 1 - h)),
        (at_x0, (y, (x + 1) % nx, h)),
        (at_x0, (y, (x + nx - 1) % nx, h)),
        (jnp.logical_and(at_y0, dx == 1), (y, (x + 1) % nx, h)),
        (dy < half, ((y + 1) % ny, x, h)),
        (jnp.logical_or(at_y0, dy > half + 1), ((y + ny - 1) % ny, x, h)),
    ]
    x_depth = jnp.where(dx == 0, 0, jnp.where(dx == 2, 2, 1))
    y_depth = jnp.where(dy <= half, dy, ny - dy)
    return is_root, parent, kids, dh + x_depth + y_depth


N_CHUNKS = 4
N_BLOCKS = 8
N_SLOTS = 7
MAX_DEPTH = 9
NARROW_LAG = 1
W_CHUNKS = 2


def bcast_kernel(src_ref, panel_ref, blocks_ref, nsend, nrecv, wsend, wrecv):
    y, x, h, q = positions()
    n = lax.axis_size("narrow")
    ny = lax.axis_size("wide_0")
    nx = lax.axis_size("wide_1")
    rows = panel_ref.shape[0] // N_CHUNKS
    even = q % 2 == 0
    n_has_parent, n_parent, n_kids = narrow_tree(q, n)

    trees = []
    for j in range(N_BLOCKS):
        if j < N_BLOCKS // 2:
            is_root, parent, kids, depth = wide_tree(y, x, h, j, ny, nx)
            active = q >= 0
            parent = tuple(jnp.where(even, p, o) for p, o in zip((*parent, q), (y, x, h, q - 1)))
            kids = [(jnp.logical_and(even, c), (*k, q)) for c, k in kids]
            kids.append((even, (y, x, h, q + 1)))
            is_root = jnp.logical_and(even, is_root)
            depth = depth + 1 - even.astype(jnp.int32)
        else:
            root = 4 * q + (j - N_BLOCKS // 2)
            is_root, parent, kids, depth = wide_tree(y, x, h, root, ny, nx)
            active = q > 0
            parent = (*parent, q)
            kids = [(c, (*k, q)) for c, k in kids]
            kids.append((q < 0, (y, x, h, q)))
        trees.append((active, is_root, parent, kids, depth))

    barrier = pltpu.get_barrier_semaphore()

    @pl.when(n_has_parent)
    def _():
        pl.semaphore_signal(barrier, 1, device_id=(y, x, h, n_parent), device_id_type=MESH_ID)

    peers = n_has_parent.astype(jnp.int32)
    for cond, kid in n_kids:
        peers = peers + cond.astype(jnp.int32)

        @pl.when(cond)
        def _():
            pl.semaphore_signal(barrier, 1, device_id=(y, x, h, kid), device_id_type=MESH_ID)

    for active, is_root, parent, kids, depth in trees:
        has_parent = jnp.logical_and(active, jnp.logical_not(is_root))
        peers = peers + has_parent.astype(jnp.int32)

        @pl.when(has_parent)
        def _():
            pl.semaphore_signal(barrier, 1, device_id=parent, device_id_type=MESH_ID)

        for cond, kid in kids:
            go = jnp.logical_and(active, cond)
            peers = peers + go.astype(jnp.int32)

            @pl.when(go)
            def _():
                pl.semaphore_signal(barrier, 1, device_id=kid, device_id_type=MESH_ID)

    pl.semaphore_wait(barrier, peers)

    def narrow_copy(src, c, k, kid):
        part = pl.ds(c * rows, rows)
        return pltpu.make_async_remote_copy(
            src_ref=src.at[part],
            dst_ref=panel_ref.at[part],
            send_sem=nsend.at[c, k],
            recv_sem=nrecv.at[c],
            device_id=(y, x, h, kid),
            device_id_type=MESH_ID,
        )

    def narrow_step(c):
        @pl.when(n_has_parent)
        def _():
            narrow_copy(panel_ref, c, 0, q).wait_recv()

        for k, (cond, kid) in enumerate(n_kids):
            @pl.when(jnp.logical_and(cond, q == 0))
            def _():
                narrow_copy(src_ref, c, k, kid).start()

            @pl.when(jnp.logical_and(cond, q != 0))
            def _():
                narrow_copy(panel_ref, c, k, kid).start()

    piece = rows // W_CHUNKS

    def wide_copy(src, j, c, k, kid):
        part = pl.ds(c * piece, piece)
        cols = pl.ds(0, (j + 1) * rows if j < N_BLOCKS // 2 else src.shape[1])
        return pltpu.make_async_remote_copy(
            src_ref=src.at[part, cols],
            dst_ref=blocks_ref.at[j, part, cols],
            send_sem=wsend.at[j, c, k],
            recv_sem=wrecv.at[j, c],
            device_id=kid,
            device_id_type=MESH_ID,
        )

    narrow_step(0)

    @pl.when(q == 0)
    def _():
        panel_ref[...] = src_ref[...]

    for j, (active, is_root, parent, kids, depth) in enumerate(trees):
        root_here = jnp.logical_and(active, is_root)
        for c in range(W_CHUNKS):
            for k, (cond, kid) in enumerate(kids):
                @pl.when(jnp.logical_and(jnp.logical_and(root_here, cond), q == 0))
                def _():
                    wide_copy(src_ref.at[pl.ds(0, rows)], j, c, k, kid).start()

                @pl.when(jnp.logical_and(jnp.logical_and(root_here, cond), q != 0))
                def _():
                    wide_copy(panel_ref.at[pl.ds(0, rows)], j, c, k, kid).start()

        @pl.when(jnp.logical_and(root_here, q == 0))
        def _():
            blocks_ref[j] = src_ref[pl.ds(0, rows)]

        @pl.when(jnp.logical_and(root_here, q != 0))
        def _():
            blocks_ref[j] = panel_ref[pl.ds(0, rows)]

    for level in range(1, MAX_DEPTH + W_CHUNKS - 1):
        for c in range(W_CHUNKS):
            for j, (active, is_root, parent, kids, depth) in enumerate(trees):
                here = jnp.logical_and(jnp.logical_and(active, jnp.logical_not(is_root)), depth + c == level)

                @pl.when(here)
                def _():
                    wide_copy(blocks_ref.at[j], j, c, 0, (y, x, h, q)).wait_recv()

                for k, (cond, kid) in enumerate(kids):
                    @pl.when(jnp.logical_and(here, cond))
                    def _():
                        wide_copy(blocks_ref.at[j], j, c, k, kid).start()

        c = level - NARROW_LAG
        if 1 <= c < N_CHUNKS:
            narrow_step(c)

    for c in range(N_CHUNKS):
        for k, (cond, kid) in enumerate(n_kids):
            @pl.when(cond)
            def _():
                narrow_copy(panel_ref, c, k, kid).wait_send()

    for j, (active, is_root, parent, kids, depth) in enumerate(trees):
        for c in range(W_CHUNKS):
            for k, (cond, kid) in enumerate(kids):
                @pl.when(jnp.logical_and(active, cond))
                def _():
                    wide_copy(blocks_ref.at[j], j, c, k, kid).wait_send()


def broadcast(panel):
    rows = panel.shape[0] // N_CHUNKS
    vmem = pl.BlockSpec(memory_space=pltpu.VMEM)
    return pl.pallas_call(
        bcast_kernel,
        out_shape=(
            jax.ShapeDtypeStruct(panel.shape, panel.dtype),
            jax.ShapeDtypeStruct((N_BLOCKS, rows, panel.shape[1]), panel.dtype),
        ),
        in_specs=[vmem],
        out_specs=(vmem, vmem),
        scratch_shapes=[
            pltpu.SemaphoreType.DMA((N_CHUNKS, 2)),
            pltpu.SemaphoreType.DMA((N_CHUNKS,)),
            pltpu.SemaphoreType.DMA((N_BLOCKS, W_CHUNKS, N_SLOTS)),
            pltpu.SemaphoreType.DMA((N_BLOCKS, W_CHUNKS)),
        ],
        compiler_params=pltpu.CompilerParams(collective_id=0, has_side_effects=True),
    )(panel)


def mm_t(a, b):
    return lax.dot_general(
        a, b, (((1,), (1,)), ((), ())),
        precision=HIGHEST_PRECISION, preferred_element_type=jnp.float32,
    )


def mm(a, b):
    return jnp.dot(a, b, precision=HIGHEST_PRECISION, preferred_element_type=jnp.float32)


def newton_inverse(lower, start, steps):
    inverse = start
    for _ in range(steps):
        inverse = 2 * inverse - mm(inverse, mm(lower, inverse))
    return inverse


def diagonal_inverse(lower):
    n = lower.shape[0]
    on_diag = lax.broadcasted_iota(jnp.int32, (n, n), 0) == lax.broadcasted_iota(jnp.int32, (n, n), 1)
    diag = jnp.sum(jnp.where(on_diag, lower, 0.0), axis=1, keepdims=True)
    return jnp.where(on_diag, 1.0 / diag, 0.0)


def cholesky_and_inverse(symmetric):
    n = symmetric.shape[0]
    nb = n // BS
    work = symmetric
    cols = []
    block_inverses = []
    for b in range(nb):
        head = work[:BS, :BS]
        diag = jnp.tril(jnp.linalg.cholesky(head, symmetrize_input=False))
        inv = newton_inverse(diag, diagonal_inverse(diag), (BS - 1).bit_length())
        block_inverses.append(inv)
        if b + 1 < nb:
            below = mm_t(work[BS:, :BS], inv)
            work = work[BS:, BS:] - mm_t(below, below)
            cols.append(jnp.concatenate([jnp.zeros((b * BS, BS), jnp.float32), diag, below], 0))
        else:
            cols.append(jnp.concatenate([jnp.zeros((b * BS, BS), jnp.float32), diag], 0))
    factor = jnp.concatenate(cols, 1)
    start = jnp.zeros((n, n), jnp.float32)
    for b in range(nb):
        start = lax.dynamic_update_slice(start, block_inverses[b], (b * BS, b * BS))
    inverse = newton_inverse(factor, start, max(1, (nb - 1).bit_length()))
    return factor, inverse


def shards(front, child_update, child_map):
    wide_count = lax.axis_size(WIDE)
    narrow_count = lax.axis_size("narrow")
    wide_index = lax.axis_index(WIDE)
    narrow_index = lax.axis_index("narrow")
    half_count = wide_count // 2
    local_rows, local_cols = front.shape
    front_slots = local_rows // BS
    block_total = front_slots * wide_count
    child_side = wide_index // half_count
    row_local = jnp.arange(local_rows, dtype=jnp.int32)
    global_row = (row_local // BS * wide_count + wide_index) * BS + row_local % BS
    col_local = jnp.arange(local_cols, dtype=jnp.int32)
    global_col = (col_local // PW * narrow_count + narrow_index) * PW + col_local % PW
    groups = child_update.reshape(2, front_slots, BS, local_cols)
    leaving = lax.dynamic_index_in_dim(groups, 1 - child_side, 0, keepdims=False)
    arrived = from_partner(leaving, WIDE, half_count.bit_length() - 1)

    def named_cols(side):
        names = lax.dynamic_slice_in_dim(child_map, side * block_total, block_total)
        return jnp.any(names[:, None] == (global_col // BS)[None, :], axis=0)

    kept_rows = lax.dynamic_index_in_dim(groups, child_side, 0, keepdims=False)
    kept_rows = jnp.where(named_cols(child_side)[None, None, :], kept_rows, 0.0)
    arrived = jnp.where(named_cols(1 - child_side)[None, None, :], arrived, 0.0)
    partner = (wide_index + half_count) % wide_count
    own_map = lax.dynamic_slice_in_dim(
        child_map, (wide_index * 2 + child_side) * front_slots, front_slots
    )
    got_map = lax.dynamic_slice_in_dim(
        child_map, (partner * 2 + child_side) * front_slots, front_slots
    )
    target = wide_index + wide_count * jnp.arange(front_slots, dtype=jnp.int32)
    own_select = (own_map[None, :] == target[:, None]).astype(jnp.float32)
    got_select = (got_map[None, :] == target[:, None]).astype(jnp.float32)
    own_part = jnp.dot(
        own_select,
        kept_rows.reshape(front_slots, BS * local_cols),
        precision=HIGHEST_PRECISION,
        preferred_element_type=jnp.float32,
    )
    got_part = jnp.dot(
        got_select,
        arrived.reshape(front_slots, BS * local_cols),
        precision=HIGHEST_PRECISION,
        preferred_element_type=jnp.float32,
    )
    matrix = front + (own_part + got_part).reshape(local_rows, local_cols)

    panel, blocks = broadcast(matrix)
    diag_block = blocks[: N_BLOCKS // 2].reshape(PW, PW)
    diag_block = jnp.where(
        lax.broadcasted_iota(jnp.int32, (PW, PW), 1) < (lax.broadcasted_iota(jnp.int32, (PW, PW), 0) // BS + 1) * BS,
        diag_block,
        0.0,
    )
    col_rows = blocks[N_BLOCKS // 2 :].reshape(PW, PW)

    factor_diag, inverse = cholesky_and_inverse(diag_block)
    own_factor = mm_t(panel, inverse)
    diag_rows = lax.dynamic_slice_in_dim(factor_diag, jnp.minimum(wide_index, 3) * BS, BS)
    top = jnp.where(wide_index * BS < PW, diag_rows, own_factor[:BS])
    own_factor = jnp.concatenate([top, own_factor[BS:]], 0)
    col_factor = mm_t(col_rows, inverse)
    update = mm_t(own_factor, col_factor)
    renewed = jnp.where(narrow_index == 0, own_factor, matrix - update)
    on_or_below = global_row[:, None] >= global_col[None, :]
    return jnp.where(on_or_below, renewed, jnp.zeros_like(renewed))


def solution(mesh):
    torus = Mesh(
        mesh.devices.reshape(8, 4, 2, mesh.shape["narrow"]),
        AXES,
    )
    placed = (P(WIDE, "narrow"), P(WIDE, "narrow"), P())
    return jax.shard_map(
        shards, mesh=torus, in_specs=placed, out_specs=P(WIDE, "narrow"), check_vma=False
    )
```
